32 devices in a mesh: seq: 8 (over z, core), ctx: 4 (over y, x).
Axes of the slice: x: 2, y: 2, z: 4, core: 2. Of those that a mesh axis runs over, the one named last changes fastest.
Arguments:
- tokens: bfloat16 [8, 2048, 896], P('seq', 'ctx'), may hold values from -6 to 6
- attention_gain: bfloat16 [896], P('ctx'), may hold values from 0.5 to 1.5
- project_weight: bfloat16 [896, 1152], P('seq', 'ctx'), may hold values from -0.1875 to 0.1875
- project_bias: bfloat16 [1152], P('ctx'), may hold values from -1.1953125 to 1.1953125
- output_weight: bfloat16 [896, 896], P('seq', 'ctx'), may hold values from -0.75 to 0.75
- feedforward_gain: bfloat16 [896], P('ctx'), may hold values from 0.5 to 1.5
- gate_weight: bfloat16 [896, 4864], P('seq', 'ctx'), may hold values from -0.1875 to 0.1875
- up_weight: bfloat16 [896, 4864], P('seq', 'ctx'), may hold values from -0.1875 to 0.1875
- down_weight: bfloat16 [4864, 896], P('seq', 'ctx'), may hold values from -0.078125 to 0.078125
- cotangent: bfloat16 [8, 2048, 896], P('seq', 'ctx'), may hold values from -6 to 6
Outputs:
- layer_output: bfloat16 [8, 2048, 896], P('seq', 'ctx')
- tokens_gradient: float32 [8, 2048, 896], P('seq', 'ctx')
- attention_gain_gradient: float32 [896], P('ctx')
- project_weight_gradient: float32 [896, 1152], P('seq', 'ctx')
- project_bias_gradient: float32 [1152], P('ctx')
- output_weight_gradient: float32 [896, 896], P('seq', 'ctx')
- feedforward_gain_gradient: float32 [896], P('ctx')
- gate_weight_gradient: float32 [896, 4864], P('seq', 'ctx')
- up_weight_gradient: float32 [896, 4864], P('seq', 'ctx')
- down_weight_gradient: float32 [4864, 896], P('seq', 'ctx')
The draws below stay inside these ranges and needn't reach their ends.
All inputs are finite; a program needn't handle non-finite values.
Results may differ from the reference program's by a relative error of at most 0.02.
Values may be sent and summed in bfloat16 or wider, within the bound.
No kernel may reach another device: no remote copies, remote signals or barrier semaphores. Data moves between devices by JAX's collectives and lax.ppermute only.
A program may use at most 192 MiB of HBM per device.

```python
import math
import jax
import jax.numpy as jnp
from jax import lax

D = 896
HEADS = 14
KV_HEADS = 2
HEAD_DIM = 64
FF = 4864
QKV = 1152
SEQ_LEN = 2048
SEQUENCES = 8


def block_levels(key, extent, split, smallest, largest):
    gain, own = 1.0, jax.random.fold_in(key, 6)
    for position, parts in split:
        steps = jnp.exp(jax.random.uniform(jax.random.fold_in(own, position), (parts,), jnp.float32, smallest / len(split), largest / len(split)))
        gain = gain * jnp.repeat(steps, extent[position] // parts).reshape([-1 if axis == position else 1 for axis in range(len(extent))])
    return gain


def gaussian(own_key, dims, scale, most, shards=(), kind=jnp.bfloat16):
    array = jax.random.normal(own_key, dims, jnp.float32) * scale
    if len(shards) > 0:
        array = block_levels(own_key, dims, shards, -0.22, 0.18) * array
    return jnp.clip(array, min=-most, max=most).astype(kind)


def setup_inputs(seed: int = 0) -> dict:
    keys = jax.random.split(jax.random.key(seed), 11)
    return {
        "tokens": gaussian(keys[0], (SEQUENCES, SEQ_LEN, D), 1.0, 6.0, ((0, 8), (1, 4))),
        "attention_gain": jnp.clip(1.0 + 0.1 * jax.random.normal(keys[1], (D,), jnp.float32), 0.5, 1.5).astype(jnp.bfloat16),
        "project_weight": gaussian(keys[2], (D, QKV), D ** -0.5, 0.1875, ((0, 8), (1, 4))),
        "project_bias": gaussian(keys[3], (QKV,), 0.2, 1.1953125, ((0, 4),)),
        "output_weight": gaussian(keys[4], (HEADS * HEAD_DIM, D), 64 ** -0.5, 0.75, ((0, 8), (1, 4))),
        "feedforward_gain": jnp.clip(1.0 + 0.1 * jax.random.normal(keys[5], (D,), jnp.float32), 0.5, 1.5).astype(jnp.bfloat16),
        "gate_weight": gaussian(keys[6], (D, FF), D ** -0.5, 0.1875, ((0, 8), (1, 4))),
        "up_weight": gaussian(keys[7], (D, FF), D ** -0.5, 0.1875, ((0, 8), (1, 4))),
        "down_weight": gaussian(keys[8], (FF, D), FF ** -0.5, 0.078125, ((0, 8), (1, 4))),
        "cotangent": gaussian(keys[9], (SEQUENCES, SEQ_LEN, D), 1.0, 6.0, ((0, 8), (1, 4))),
    }


@jax.custom_vjp
def low(v):
    return lax.optimization_barrier(v.astype(jnp.bfloat16)).astype(jnp.float32)

@jax.custom_vjp
def low_back(v):
    return v

def low_keep(v):
    return (low(v), None)

def low_pass(kept, grad):
    return (grad,)

def back_keep(v):
    return (v, None)

def back_low(kept, grad):
    return (low(grad),)
low.defvjp(low_keep, low_pass)
low_back.defvjp(back_keep, back_low)
norm_eps = 1e-06
rope_base = 1000000.0
masked_value = -1e+30
highest = lax.Precision.HIGHEST

def inverse_rms(tensor):
    return lax.rsqrt(lax.optimization_barrier(jnp.mean(tensor * tensor, axis=-1, keepdims=True)) + norm_eps)

def rotary(tensor, positions):
    half_width = tensor.shape[-1] // 2
    steps_up = jnp.arange(half_width).astype(tensor.dtype)
    frequency = jnp.power(jnp.asarray(rope_base, tensor.dtype), -2.0 * steps_up / tensor.shape[-1])
    angles = positions.astype(tensor.dtype)[:, None] * frequency[None, :]
    cosine = jnp.cos(angles)[:, None, :]
    sine_part = jnp.sin(angles)[:, None, :]
    first_half = tensor[..., :half_width]
    second = tensor[..., half_width:]
    return jnp.concatenate([first_half * cosine - second * sine_part, second * cosine + first_half * sine_part], axis=-1)

def attention(queries, key_heads, values):
    group_size, length = (queries.shape[0], queries.shape[1])
    block_rows = min(512, length)
    block_count = length // block_rows
    grouped = queries.reshape(group_size, block_count, block_rows, KV_HEADS, HEADS // KV_HEADS, HEAD_DIM)
    grouped = jnp.moveaxis(grouped, 1, 0)
    starts = jnp.arange(block_count) * block_rows
    key_pos = jnp.arange(length)

    @jax.checkpoint
    def one_block(pair_inputs):
        query_rows, start_row = pair_inputs
        raw_scores = jnp.einsum('gqhrd,gkhd->ghrqk', query_rows, key_heads, precision=highest) * HEAD_DIM ** (-0.5)
        scores = low_back(raw_scores)
        query_pos = start_row + jnp.arange(block_rows)
        allowed = key_pos[None, :] <= query_pos[:, None]
        scores = jnp.where(allowed, scores, masked_value)
        running_max = lax.optimization_barrier(jnp.max(scores, axis=-1, keepdims=True))
        weights = jnp.exp(scores - running_max)
        soft_weights = low(weights / lax.optimization_barrier(jnp.sum(weights, axis=-1, keepdims=True)))
        return jnp.einsum('ghrqk,gkhd->gqhrd', soft_weights, values, precision=highest)
    outputs = lax.map(one_block, (grouped, starts))
    return jnp.moveaxis(outputs, 0, 1).reshape(group_size, length, HEADS * HEAD_DIM)

def layer(inputs, attention_gain, project_weight, project_bias, output_weight, feedforward_gain, gate_weight, up_weight, down_weight):
    group_size, length = (inputs.shape[0], inputs.shape[1])
    query_width = HEADS * HEAD_DIM
    key_width = KV_HEADS * HEAD_DIM
    normed = low(inputs * inverse_rms(inputs) * attention_gain)
    project = low_back(jnp.einsum('gld,de->gle', normed, project_weight, precision=highest) + project_bias)
    positions = jnp.arange(length)
    queries = project[..., :query_width].reshape(group_size, length, HEADS, HEAD_DIM)
    key_heads = project[..., query_width:query_width + key_width].reshape(group_size, length, KV_HEADS, HEAD_DIM)
    values = project[..., query_width + key_width:].reshape(group_size, length, KV_HEADS, HEAD_DIM)
    queries = low(rotary(queries, positions)).reshape(group_size, length, KV_HEADS, HEADS // KV_HEADS, HEAD_DIM)
    key_heads = low(rotary(key_heads, positions))
    values = low(values)
    mixed_heads = low(low_back(attention(queries, key_heads, values)))
    hidden = inputs + low_back(jnp.einsum('gle,ed->gld', mixed_heads, output_weight, precision=highest))
    normed_ffn = low(hidden * inverse_rms(hidden) * feedforward_gain)
    gate_value = low_back(jnp.einsum('gld,df->glf', normed_ffn, gate_weight, precision=highest))
    up_value = low_back(jnp.einsum('gld,df->glf', normed_ffn, up_weight, precision=highest))
    active = low(jax.nn.silu(gate_value) * up_value)
    return hidden + low_back(jnp.einsum('glf,fd->gld', active, down_weight, precision=highest))

def reference(tokens, attention_gain, project_weight, project_bias, output_weight, feedforward_gain, gate_weight, up_weight, down_weight, cotangent):
    params = tuple((weight.astype(jnp.float32) for weight in (attention_gain, project_weight, project_bias, output_weight, feedforward_gain, gate_weight, up_weight, down_weight)))
    sequence_total, length, model_width = tokens.shape
    group_size = math.gcd(sequence_total, max(1, 4096 // length))
    group_count = sequence_total // group_size
    inputs = tokens.astype(jnp.float32).reshape(group_count, group_size, length, model_width)
    grads_in = cotangent.astype(jnp.float32).reshape(group_count, group_size, length, model_width)

    def step(grad_sums, pair_inputs):
        group_block, group_grad = pair_inputs
        output, pullback = jax.vjp(layer, group_block, *params)
        pulled = pullback(group_grad)
        grad_sums = tuple((earlier + latest for earlier, latest in zip(grad_sums, pulled[1:])))
        return (grad_sums, (output.astype(jnp.bfloat16), pulled[0]))
    start_sums = tuple((jnp.zeros_like(weight) for weight in params))
    grad_sums, (outputs, input_grads) = lax.scan(step, start_sums, (inputs, grads_in))
    return (outputs.reshape(sequence_total, length, model_width), input_grads.reshape(sequence_total, length, model_width), grad_sums[0], grad_sums[1], grad_sums[2], grad_sums[3], grad_sums[4], grad_sums[5], grad_sums[6], grad_sums[7])
```

```python
import math
import jax
import jax.numpy as jnp
from jax import lax
from jax.experimental import pallas as pl
from jax.experimental.pallas import tpu as pltpu
from jax.sharding import PartitionSpec as P

HEADS = 14
KV_HEADS = 2
HEAD_DIM = 64
GROUP = HEADS // KV_HEADS
PAIRS = HEADS // 2
PAIR = 2 * HEAD_DIM
Q_WIDTH = HEADS * HEAD_DIM
K_WIDTH = KV_HEADS * HEAD_DIM

norm_eps = 1e-06
rope_base = 1000000.0
masked_value = -1e30
score_scale = HEAD_DIM ** (-0.5)
log2_e = math.log2(math.e)
bf16 = jnp.bfloat16
f32 = jnp.float32


def inverse_rms(tensor):
    return lax.rsqrt(jnp.mean(tensor * tensor, axis=-1, keepdims=True) + norm_eps)


def rotate(tensor, positions, forward):
    half_width = tensor.shape[-1] // 2
    steps_up = jnp.arange(half_width).astype(f32)
    frequency = jnp.power(jnp.asarray(rope_base, f32), -2.0 * steps_up / tensor.shape[-1])
    angles = positions.astype(f32)[:, None] * frequency[None, :]
    cosine = jnp.cos(angles)[:, None, :]
    sine_part = jnp.sin(angles)[:, None, :]
    if not forward:
        sine_part = -sine_part
    first_half = tensor[..., :half_width]
    second = tensor[..., half_width:]
    return jnp.concatenate(
        [first_half * cosine - second * sine_part, second * cosine + first_half * sine_part],
        axis=-1,
    )


def dot(a, b, dims):
    return lax.dot_general(a, b, (dims, ((), ())), preferred_element_type=f32)


NN = ((1,), (0,))
NT = ((1,), (1,))
TN = ((0,), (0,))


def pair_sides(x, x_swapped):
    low = lax.broadcasted_iota(jnp.int32, x.shape, 1) < HEAD_DIM
    zero = jnp.zeros_like(x)
    left = (jnp.where(low, x, zero), jnp.where(low, x_swapped, zero))
    right = (jnp.where(low, zero, x_swapped), jnp.where(low, zero, x))
    sides = {}
    for pair in range(PAIRS):
        key = (2 * pair // GROUP, (2 * pair + 1) // GROUP)
        if key not in sides:
            sides[key] = jnp.concatenate([left[key[0]], right[key[1]]], axis=0)
    return sides


def forward_kernel(place_ref, q_ref, k_ref, vt_ref, o_ref, lse_ref, top_ref, total_ref, acc_ref):
    block = q_ref.shape[1]
    last = place_ref[pl.program_id(0) % 2]
    top_ref[...] = jnp.full_like(top_ref, masked_value)
    total_ref[...] = jnp.zeros_like(total_ref)
    acc_ref[...] = jnp.zeros_like(acc_ref)
    scale = score_scale * log2_e

    def step(index, diagonal):
        start = pl.multiple_of(index * block, block)
        sides = pair_sides(
            k_ref[0, pl.ds(start, block), :PAIR], k_ref[0, pl.ds(start, block), PAIR:]
        )
        values = vt_ref[0, index]
        if diagonal:
            key_at = lax.broadcasted_iota(jnp.int32, (block, block), 0)
            query_at = lax.broadcasted_iota(jnp.int32, (block, block), 1)
            allowed = key_at <= query_at
        for pair in range(PAIRS):
            both = dot(
                sides[(2 * pair // GROUP, (2 * pair + 1) // GROUP)],
                q_ref[0, :, pair * PAIR : (pair + 1) * PAIR],
                NT,
            )
            for odd in range(2):
                head = 2 * pair + odd
                kv = head // GROUP
                scores = both[odd * block : (odd + 1) * block] * scale
                if diagonal:
                    scores = jnp.where(allowed, scores, masked_value)
                old = top_ref[head : head + 1, :]
                new = jnp.maximum(old, jnp.max(scores, axis=0, keepdims=True))
                shrink = jnp.exp2(old - new)
                weights = jnp.exp2(scores - new)
                top_ref[head : head + 1, :] = new
                total_ref[head : head + 1, :] = total_ref[
                    head : head + 1, :
                ] * shrink + jnp.sum(weights, axis=0, keepdims=True)
                rows = slice(head * HEAD_DIM, (head + 1) * HEAD_DIM)
                acc_ref[rows, :] = acc_ref[rows, :] * shrink + dot(
                    values[kv * HEAD_DIM : (kv + 1) * HEAD_DIM], weights.astype(bf16), NN
                )

    def body(index, carry):
        step(index, False)
        return carry

    lax.fori_loop(0, last, body, 0)
    step(last, True)
    for pair in range(PAIRS):
        parts = []
        for odd in range(2):
            head = 2 * pair + odd
            parts.append(
                acc_ref[head * HEAD_DIM : (head + 1) * HEAD_DIM, :]
                / total_ref[head : head + 1, :]
            )
        o_ref[0, :, pair * PAIR : (pair + 1) * PAIR] = jnp.transpose(
            jnp.concatenate(parts, axis=0)
        ).astype(bf16)
    lse_ref[0] = top_ref[...] + jnp.log2(total_ref[...])


def backward_kernel(
    place_ref, q_ref, k_ref, v_ref, kt_ref, o_ref, g_ref, lse_ref, dq_ref, dk_ref, dv_ref, acc_ref
):
    block = q_ref.shape[1]
    last = place_ref[pl.program_id(0) % 2]
    scale = score_scale * log2_e

    @pl.when(pl.program_id(0) % 2 == 0)
    def _():
        dk_ref[...] = jnp.zeros_like(dk_ref)
        dv_ref[...] = jnp.zeros_like(dv_ref)

    acc_ref[...] = jnp.zeros_like(acc_ref)
    product = g_ref[0].astype(f32) * o_ref[0].astype(f32)
    coarse = product.astype(bf16)
    fine = (product - coarse.astype(f32)).astype(bf16)
    head_of = lax.broadcasted_iota(jnp.int32, (16, Q_WIDTH), 1) // HEAD_DIM
    picks = (head_of == lax.broadcasted_iota(jnp.int32, (16, Q_WIDTH), 0)).astype(bf16)
    delta = dot(picks, coarse, NT) + dot(picks, fine, NT)

    def step(index, diagonal):
        start = pl.multiple_of(index * block, block)
        key_sides = pair_sides(
            k_ref[0, pl.ds(start, block), :PAIR], k_ref[0, pl.ds(start, block), PAIR:]
        )
        value_sides = pair_sides(
            v_ref[0, pl.ds(start, block), :PAIR], v_ref[0, pl.ds(start, block), PAIR:]
        )
        keys_turned = kt_ref[0, index]
        if diagonal:
            key_at = lax.broadcasted_iota(jnp.int32, (block, block), 0)
            query_at = lax.broadcasted_iota(jnp.int32, (block, block), 1)
            allowed = key_at <= query_at
        key_sum = [[None, None], [None, None]]
        value_sum = [[None, None], [None, None]]

        def add(sums, odd, kv, part):
            sums[odd][kv] = part if sums[odd][kv] is None else sums[odd][kv] + part

        for pair in range(PAIRS):
            which = (2 * pair // GROUP, (2 * pair + 1) // GROUP)
            lanes = slice(pair * PAIR, (pair + 1) * PAIR)
            queries = q_ref[0, :, lanes]
            grads = g_ref[0, :, lanes]
            both = dot(key_sides[which], queries, NT)
            both_grads = dot(value_sides[which], grads, NT)
            low_weights = []
            low_scores = []
            for odd in range(2):
                head = 2 * pair + odd
                part = slice(odd * block, (odd + 1) * block)
                weights = jnp.exp2(both[part] * scale - lse_ref[0, head : head + 1, :])
                if diagonal:
                    weights = jnp.where(allowed, weights, 0.0)
                change = weights * (both_grads[part] - delta[head : head + 1, :])
                low_weights.append(weights.astype(bf16))
                low_scores.append(change.astype(bf16))
                rows = slice(head * HEAD_DIM, (head + 1) * HEAD_DIM)
                acc_ref[rows, :] += dot(
                    keys_turned[which[odd] * HEAD_DIM : (which[odd] + 1) * HEAD_DIM],
                    low_scores[odd],
                    NN,
                )
            value_part = dot(jnp.concatenate(low_weights, axis=0), grads, NN)
            key_part = dot(jnp.concatenate(low_scores, axis=0), queries, NN)
            for odd in range(2):
                part = slice(odd * block, (odd + 1) * block)
                add(value_sum, odd, which[odd], value_part[part])
                add(key_sum, odd, which[odd], key_part[part])
        low = lax.broadcasted_iota(jnp.int32, (block, PAIR), 1) < HEAD_DIM
        rows = pl.ds(start, block)
        for sums, out_ref, factor in ((key_sum, dk_ref, score_scale), (value_sum, dv_ref, 1.0)):
            straight = jnp.where(low, sums[0][0], sums[1][1])
            crossed = jnp.where(low, sums[0][1], sums[1][0])
            out_ref[0, rows, :PAIR] += straight * factor
            out_ref[0, rows, PAIR:] += crossed * factor

    def body(index, carry):
        step(index, False)
        return carry

    lax.fori_loop(0, last, body, 0)
    step(last, True)
    for pair in range(PAIRS):
        dq_ref[0, :, pair * PAIR : (pair + 1) * PAIR] = (
            jnp.transpose(acc_ref[pair * PAIR : (pair + 1) * PAIR, :]) * score_scale
        )


def swap_heads(x):
    return jnp.concatenate([x[..., HEAD_DIM:], x[..., :HEAD_DIM]], axis=-1)


def attention_specs(count, block, length):
    def rows(width):
        return pl.BlockSpec((1, block, width), lambda i, place: (i, 0, 0))

    def whole(height, width):
        return pl.BlockSpec((1, height, width), lambda i, place: (i // 2, 0, 0))

    turned = pl.BlockSpec((1, length // block, PAIR, block), lambda i, place: (i // 2, 0, 0, 0))
    stats = pl.BlockSpec((1, 16, block), lambda i, place: (i, 0, 0))
    return rows, whole, turned, stats


def attend_forward(places, queries, keys_both, values_turned):
    count, block, _ = queries.shape
    length = keys_both.shape[1]
    rows, whole, turned, stats = attention_specs(count, block, length)
    pairs_done = count * block * (length // 2 + block) * HEADS
    return pl.pallas_call(
        forward_kernel,
        grid_spec=pltpu.PrefetchScalarGridSpec(
            num_scalar_prefetch=1,
            grid=(count,),
            in_specs=[rows(Q_WIDTH), whole(length, 2 * PAIR), turned],
            out_specs=[rows(Q_WIDTH), stats],
            scratch_shapes=[
                pltpu.VMEM((16, block), f32),
                pltpu.VMEM((16, block), f32),
                pltpu.VMEM((Q_WIDTH, block), f32),
            ],
        ),
        out_shape=[
            jax.ShapeDtypeStruct((count, block, Q_WIDTH), bf16),
            jax.ShapeDtypeStruct((count, 16, block), f32),
        ],
        cost_estimate=pl.CostEstimate(
            flops=pairs_done * 4 * 256, bytes_accessed=4 << 20, transcendentals=pairs_done
        ),
        name="attend_forward",
    )(places, queries, keys_both, values_turned)


def attend_backward(places, queries, keys_both, values_both, keys_turned, mixed, grads, stats_in):
    count, block, _ = queries.shape
    length = keys_both.shape[1]
    rows, whole, turned, stats = attention_specs(count, block, length)
    pairs_done = count * block * (length // 2 + block) * HEADS
    return pl.pallas_call(
        backward_kernel,
        grid_spec=pltpu.PrefetchScalarGridSpec(
            num_scalar_prefetch=1,
            grid=(count,),
            in_specs=[
                rows(Q_WIDTH),
                whole(length, 2 * PAIR),
                whole(length, 2 * PAIR),
                turned,
                rows(Q_WIDTH),
                rows(Q_WIDTH),
                stats,
            ],
            out_specs=[rows(Q_WIDTH), whole(length, 2 * PAIR), whole(length, 2 * PAIR)],
            scratch_shapes=[pltpu.VMEM((Q_WIDTH, block), f32)],
        ),
        out_shape=[
            jax.ShapeDtypeStruct((count, block, Q_WIDTH), f32),
            jax.ShapeDtypeStruct((count // 2, length, 2 * PAIR), f32),
            jax.ShapeDtypeStruct((count // 2, length, 2 * PAIR), f32),
        ],
        cost_estimate=pl.CostEstimate(
            flops=pairs_done * 10 * 256, bytes_accessed=8 << 20, transcendentals=pairs_done
        ),
        name="attend_backward",
    )(places, queries, keys_both, values_both, keys_turned, mixed, grads, stats_in)


def hop(x, ctx_size, mask):
    return lax.ppermute(x, "ctx", [(i, i ^ mask) for i in range(ctx_size)])


def gather_pieces(x, ctx_size):
    if ctx_size != 4:
        return [x] + [hop(x, ctx_size, k) for k in range(1, ctx_size)]
    half = x.shape[0] // 2
    front, back = x[:half], x[half:]
    front_1 = hop(front, 4, 1)
    back_2 = hop(back, 4, 2)
    front_far = hop(jnp.concatenate([front, front_1], axis=0), 4, 2)
    back_far = hop(jnp.concatenate([back, back_2], axis=0), 4, 1)
    return [
        x,
        jnp.concatenate([front_1, back_far[:half]], axis=0),
        jnp.concatenate([front_far[:half], back_2], axis=0),
        jnp.concatenate([front_far[half:], back_far[half:]], axis=0),
    ]


def sum_pieces(pieces, ctx_size):
    if ctx_size != 4:
        total = pieces[0]
        for k in range(1, ctx_size):
            total = total + hop(pieces[k].astype(bf16), ctx_size, k).astype(f32)
        return total
    half = pieces[0].shape[0] // 2
    front = [piece[:half] for piece in pieces]
    back = [piece[half:] for piece in pieces]
    front_got = hop(jnp.concatenate([front[1], front[3]], axis=0).astype(bf16), 4, 1)
    back_got = hop(jnp.concatenate([back[2], back[3]], axis=0).astype(bf16), 4, 2)
    front_next = front[2] + front_got[half:].astype(f32)
    back_next = back[1] + back_got[half:].astype(f32)
    front_last = hop(front_next.astype(bf16), 4, 2).astype(f32)
    back_last = hop(back_next.astype(bf16), 4, 1).astype(f32)
    return jnp.concatenate(
        [
            front[0] + front_got[:half].astype(f32) + front_last,
            back[0] + back_got[:half].astype(f32) + back_last,
        ],
        axis=0,
    )


def in_order(pieces, place, ctx_size):
    result = jnp.zeros((ctx_size,) + pieces[0].shape, pieces[0].dtype)
    for k, piece in enumerate(pieces):
        result = lax.dynamic_update_index_in_dim(result, piece, place ^ k, 0)
    return result


def on_device(
    seq_size,
    ctx_size,
    tokens,
    attention_gain,
    project_weight,
    project_bias,
    output_weight,
    feedforward_gain,
    gate_weight,
    up_weight,
    down_weight,
    cotangent,
):
    sequences, block_rows, width = tokens.shape
    place = lax.axis_index("ctx")
    half = block_rows // 2
    length = block_rows * ctx_size
    rows = sequences * block_rows
    fold = seq_size // ctx_size
    mirror = [(i, ctx_size - 1 - i) for i in range(ctx_size)]
    turn = [
        ((c * fold + r) * ctx_size + q, (q * fold + r) * ctx_size + c)
        for c in range(ctx_size)
        for r in range(fold)
        for q in range(ctx_size)
    ]

    def zigzag(x):
        return jnp.concatenate([x[:, :half], lax.ppermute(x[:, half:], "ctx", mirror)], axis=1)

    places = jnp.stack([2 * place, 2 * (ctx_size - 1 - place) + 1]).astype(jnp.int32)
    positions = (places[:, None] * half + jnp.arange(half, dtype=jnp.int32)[None, :]).reshape(-1)

    def columns_whole(shard):
        pieces = [shard] + [hop(shard, ctx_size, k) for k in range(1, ctx_size)]
        ordered = in_order(pieces, place, ctx_size)
        return jnp.moveaxis(ordered, 0, 1).reshape(shard.shape[0], -1)

    def rows_whole(shard):
        return lax.all_gather(shard, "seq", axis=0, tiled=True)

    gain_width = attention_gain.shape[0]
    bias_width = project_bias.shape[0]
    vectors = jnp.concatenate([attention_gain, project_bias, feedforward_gain])[None, :]
    vector_pieces = [vectors] + [hop(vectors, ctx_size, k) for k in range(1, ctx_size)]
    vectors_all = in_order(vector_pieces, place, ctx_size)[:, 0, :].astype(f32)
    attention_full = vectors_all[:, :gain_width].reshape(-1)
    bias_full = vectors_all[:, gain_width : gain_width + bias_width].reshape(-1)
    feedforward_full = vectors_all[:, gain_width + bias_width :].reshape(-1)

    project_full = rows_whole(columns_whole(project_weight))
    output_full = rows_whole(columns_whole(output_weight))
    gate_mine = rows_whole(gate_weight)
    up_mine = rows_whole(up_weight)
    down_rows, down_columns = down_weight.shape
    down_turned = lax.ppermute(down_weight, ("seq", "ctx"), turn)
    down_mine = (
        lax.all_gather(down_turned, "seq", axis=0)
        .reshape(ctx_size, fold, down_rows, down_columns)
        .transpose(1, 2, 0, 3)
        .reshape(fold * down_rows, width)
    )

    inputs = zigzag(tokens).reshape(rows, width).astype(f32)
    grad_low = zigzag(cotangent).reshape(rows, width)
    grad_pieces = gather_pieces(grad_low, ctx_size)

    inverse_attention = inverse_rms(inputs)
    normed = (inputs * inverse_attention * attention_full).astype(bf16)
    projected = dot(normed, project_full, NN) + bias_full
    queries = rotate(
        projected[:, :Q_WIDTH].reshape(rows, HEADS, HEAD_DIM), jnp.tile(positions, sequences), True
    ).astype(bf16)
    queries = queries.reshape(sequences * 2, half, Q_WIDTH)
    keys_mine = (
        rotate(
            projected[:, Q_WIDTH : Q_WIDTH + K_WIDTH].reshape(rows, KV_HEADS, HEAD_DIM),
            jnp.tile(positions, sequences),
            True,
        )
        .astype(bf16)
        .reshape(rows, K_WIDTH)
    )
    values_mine = projected[:, Q_WIDTH + K_WIDTH :].astype(bf16)
    pairs_mine = jnp.concatenate([keys_mine, values_mine], axis=-1).reshape(
        sequences, 2, half, 2 * K_WIDTH
    )
    pair_pieces = [pairs_mine] + [hop(pairs_mine, ctx_size, k) for k in range(1, ctx_size)]
    pairs_all = jnp.zeros((sequences, 2 * ctx_size, half, 2 * K_WIDTH), bf16)
    for k, piece in enumerate(pair_pieces):
        owner = place ^ k
        pairs_all = lax.dynamic_update_slice_in_dim(pairs_all, piece[:, :1], 2 * owner, 1)
        pairs_all = lax.dynamic_update_slice_in_dim(
            pairs_all, piece[:, 1:], 2 * (ctx_size - 1 - owner) + 1, 1
        )
    pairs_all = pairs_all.reshape(sequences, length, 2 * K_WIDTH)
    keys_all = pairs_all[..., :K_WIDTH]
    values_all = pairs_all[..., K_WIDTH:]
    keys_both = jnp.concatenate([keys_all, swap_heads(keys_all)], axis=-1)
    values_both = jnp.concatenate([values_all, swap_heads(values_all)], axis=-1)


    def turned(x):
        return jnp.swapaxes(x.reshape(sequences, 2 * ctx_size, half, K_WIDTH), 2, 3)

    keys_turned = turned(keys_all)
    values_turned = turned(values_all)
    mixed, row_stats = attend_forward(places, queries, keys_both, values_turned)
    mixed_rows = mixed.reshape(rows, Q_WIDTH)
    hidden = inputs + dot(mixed_rows, output_full, NN)
    inverse_ffn = inverse_rms(hidden)
    normed_ffn = (hidden * inverse_ffn * feedforward_full).astype(bf16)

    normed_pieces = gather_pieces(normed_ffn, ctx_size)
    active_pieces = []
    grad_gate_pieces = []
    grad_up_pieces = []
    output_pieces = []
    grad_normed_pieces = []
    for piece, grad_piece in zip(normed_pieces, grad_pieces):
        gate_value = dot(piece, gate_mine, NN)
        up_value = dot(piece, up_mine, NN)
        grad_active = dot(grad_piece, down_mine, NT)
        sigmoid_gate = jax.nn.sigmoid(gate_value)
        active = (gate_value * sigmoid_gate * up_value).astype(bf16)
        grad_gate = (
            grad_active * up_value * sigmoid_gate * (1.0 + gate_value * (1.0 - sigmoid_gate))
        ).astype(bf16)
        grad_up = (grad_active * gate_value * sigmoid_gate).astype(bf16)
        grad_normed_pieces.append(dot(grad_gate, gate_mine, NT) + dot(grad_up, up_mine, NT))
        output_pieces.append(dot(active, down_mine, NN))
        active_pieces.append(active)
        grad_gate_pieces.append(grad_gate)
        grad_up_pieces.append(grad_up)
    grad_normed_ffn = sum_pieces(grad_normed_pieces, ctx_size)
    output_zigzag = hidden + sum_pieces(output_pieces, ctx_size)
    layer_output = zigzag(output_zigzag.astype(bf16).reshape(tokens.shape))

    normed_tokens = jnp.concatenate(normed_pieces, axis=0)
    grad_tokens = jnp.concatenate(grad_pieces, axis=0)
    active_tokens = jnp.concatenate(active_pieces, axis=0)
    grad_gate_weight = dot(normed_tokens, jnp.concatenate(grad_gate_pieces, axis=0), TN)
    grad_up_weight = dot(normed_tokens, jnp.concatenate(grad_up_pieces, axis=0), TN)
    grad_down_weight = dot(active_tokens, grad_tokens, TN)

    def rows_summed(whole):
        return lax.psum_scatter(whole.astype(bf16), "seq", scatter_dimension=0, tiled=True)

    gate_out = rows_summed(grad_gate_weight).astype(f32)
    up_out = rows_summed(grad_up_weight).astype(f32)
    down_parts = (
        grad_down_weight.astype(bf16)
        .reshape(fold, down_rows, ctx_size, down_columns)
        .transpose(2, 0, 1, 3)
        .reshape(seq_size * down_rows, down_columns)
    )
    down_out = lax.ppermute(
        rows_summed(down_parts), ("seq", "ctx"), [(b, a) for a, b in turn]
    ).astype(f32)

    grad_ffn_gain = jnp.sum(grad_normed_ffn * hidden * inverse_ffn, axis=0)
    weighted_ffn = grad_normed_ffn * feedforward_full
    grad_hidden = (
        grad_low.astype(f32)
        + inverse_ffn * weighted_ffn
        - hidden
        * inverse_ffn
        * inverse_ffn
        * inverse_ffn
        * jnp.mean(weighted_ffn * hidden, axis=-1, keepdims=True)
    )
    hidden_low = grad_hidden.astype(bf16)
    grad_output_weight = dot(mixed_rows, hidden_low, TN)
    grad_mixed = dot(hidden_low, output_full, NT).astype(bf16)

    grad_queries, key_grads, value_grads = attend_backward(
        places,
        queries,
        keys_both,
        values_both,
        keys_turned,
        mixed,
        grad_mixed.reshape(sequences * 2, half, Q_WIDTH),
        row_stats,
    )
    key_total = key_grads[..., :K_WIDTH] + swap_heads(key_grads[..., K_WIDTH:])
    value_total = value_grads[..., :K_WIDTH] + swap_heads(value_grads[..., K_WIDTH:])
    both_total = jnp.concatenate([key_total, value_total], axis=-1).reshape(
        sequences, 2 * ctx_size, half, 2 * K_WIDTH
    )
    both_pieces = []
    for k in range(ctx_size):
        owner = place ^ k
        both_pieces.append(
            jnp.concatenate(
                [
                    lax.dynamic_slice_in_dim(both_total, 2 * owner, 1, 1),
                    lax.dynamic_slice_in_dim(both_total, 2 * (ctx_size - 1 - owner) + 1, 1, 1),
                ],
                axis=1,
            )
        )
    both_sum = both_pieces[0]
    for k in range(1, ctx_size):
        both_sum = both_sum + hop(both_pieces[k].astype(bf16), ctx_size, k).astype(f32)
    both_sum = both_sum.reshape(rows, 2 * K_WIDTH)

    def unrotate(x, heads):
        return (
            rotate(x.reshape(rows, heads, HEAD_DIM), jnp.tile(positions, sequences), False)
            .astype(bf16)
            .reshape(rows, heads * HEAD_DIM)
        )

    grad_projected = jnp.concatenate(
        [
            unrotate(grad_queries, HEADS),
            unrotate(both_sum[:, :K_WIDTH], KV_HEADS),
            both_sum[:, K_WIDTH:].astype(bf16),
        ],
        axis=-1,
    )
    grad_project_weight = dot(normed, grad_projected, TN)
    grad_project_bias = jnp.sum(grad_projected.astype(f32), axis=0)
    grad_normed = dot(grad_projected, project_full, NT)
    grad_attention_gain = jnp.sum(grad_normed * inputs * inverse_attention, axis=0)
    weighted_attention = grad_normed * attention_full
    tokens_grad = (
        grad_hidden
        + inverse_attention * weighted_attention
        - inputs
        * inverse_attention
        * inverse_attention
        * inverse_attention
        * jnp.mean(weighted_attention * inputs, axis=-1, keepdims=True)
    ).reshape(tokens.shape)
    tokens_gradient = jnp.concatenate(
        [
            tokens_grad[:, :half],
            lax.ppermute(tokens_grad[:, half:].astype(bf16), "ctx", mirror).astype(f32),
        ],
        axis=1,
    )

    def columns_summed(partial):
        own = partial.shape[1] // ctx_size

        def part(k):
            return lax.dynamic_slice_in_dim(partial, (place ^ k) * own, own, 1)

        total = part(0).astype(f32)
        for k in range(1, ctx_size):
            total = total + hop(part(k), ctx_size, k).astype(f32)
        return total

    output_out = columns_summed(rows_summed(grad_output_weight))
    project_out = columns_summed(rows_summed(grad_project_weight))
    sums = lax.psum(
        jnp.concatenate([grad_attention_gain, grad_project_bias, grad_ffn_gain]), ("seq", "ctx")
    )

    def my_part(start, whole):
        own = whole // ctx_size
        return lax.dynamic_slice_in_dim(sums, start + place * own, own, 0)

    project_width = bias_width * ctx_size
    return (
        layer_output,
        tokens_gradient,
        my_part(0, width),
        project_out,
        my_part(width, project_width),
        output_out,
        my_part(width + project_width, width),
        gate_out,
        up_out,
        down_out,
    )


def solution(mesh):
    matrix = P("seq", "ctx")
    vector = P("ctx")
    activation = P("seq", "ctx", None)

    def step(*arrays):
        return on_device(mesh.shape["seq"], mesh.shape["ctx"], *arrays)

    return jax.shard_map(
        step,
        mesh=mesh,
        in_specs=(
            activation,
            vector,
            matrix,
            vector,
            matrix,
            vector,
            matrix,
            matrix,
            matrix,
            activation,
        ),
        out_specs=(
            activation,
            activation,
            vector,
            matrix,
            vector,
            matrix,
            vector,
            matrix,
            matrix,
            matrix,
        ),
        check_vma=False,
    )
```

```python
import math
import jax
import jax.numpy as jnp
from jax import lax
from jax.experimental import pallas as pl
from jax.experimental.pallas import tpu as pltpu
from jax.sharding import PartitionSpec as P

HEADS = 14
KV_HEADS = 2
HEAD_DIM = 64
GROUP = HEADS // KV_HEADS
PAIRS = HEADS // 2
PAIR = 2 * HEAD_DIM
Q_WIDTH = HEADS * HEAD_DIM
K_WIDTH = KV_HEADS * HEAD_DIM

norm_eps = 1e-06
rope_base = 1000000.0
masked_value = -1e30
score_scale = HEAD_DIM ** (-0.5)
log2_e = math.log2(math.e)
bf16 = jnp.bfloat16
f32 = jnp.float32


def inverse_rms(tensor):
    return lax.rsqrt(jnp.mean(tensor * tensor, axis=-1, keepdims=True) + norm_eps)


def dot(a, b, dims):
    return lax.dot_general(a, b, (dims, ((), ())), preferred_element_type=f32)


NN = ((1,), (0,))
NT = ((1,), (1,))
TN = ((0,), (0,))


def rotation_tables(positions):
    half_width = HEAD_DIM // 2
    steps_up = jnp.arange(half_width).astype(f32)
    frequency = jnp.power(jnp.asarray(rope_base, f32), -2.0 * steps_up / HEAD_DIM)
    angles = positions.astype(f32)[:, None] * frequency[None, :]
    cosine = jnp.cos(angles)
    sine = jnp.sin(angles)
    return (
        jnp.concatenate([cosine, cosine, cosine, cosine], axis=-1),
        jnp.concatenate([-sine, sine, -sine, sine], axis=-1),
    )


def turn_pair(x, cosine, sine):
    lane = lax.broadcasted_iota(jnp.int32, x.shape, 1)
    quarter = HEAD_DIM // 2
    other = jnp.where(
        (lane // quarter) % 2 == 0,
        pltpu.roll(x, PAIR - quarter, 1),
        pltpu.roll(x, quarter, 1),
    )
    return x * cosine + other * sine


def swap_pair(x):
    return pltpu.roll(x.astype(f32), HEAD_DIM, 1)


def params():
    return pltpu.CompilerParams(vmem_limit_bytes=60 << 20)


def project_kernel(x_ref, gain_ref, w_ref, bias_ref, cos_ref, sin_ref, normed_ref, q_ref, kv_ref):
    x = x_ref[...].astype(f32)
    normed = (x * inverse_rms(x) * gain_ref[...]).astype(bf16)
    normed_ref[...] = normed
    projected = dot(normed, w_ref[...], NN) + bias_ref[...]
    cosine = cos_ref[...]
    sine = sin_ref[...]
    for pair in range(PAIRS + 1):
        lanes = slice(pair * PAIR, (pair + 1) * PAIR)
        turned = turn_pair(projected[:, lanes], cosine, sine).astype(bf16)
        if pair < PAIRS:
            q_ref[:, lanes] = turned
        else:
            kv_ref[:, :K_WIDTH] = turned
    kv_ref[:, K_WIDTH:] = projected[:, Q_WIDTH + K_WIDTH :].astype(bf16)


def row_spec(tile, width):
    return pl.BlockSpec((tile, width), lambda i: (i, 0))


def full_spec(*shape):
    return pl.BlockSpec(shape, lambda i: (0,) * len(shape))


def project_forward(tokens, gain, weight, bias, cosine, sine):
    rows, width = tokens.shape
    tile = rows // 2
    columns = weight.shape[1]
    return pl.pallas_call(
        project_kernel,
        grid=(2,),
        in_specs=[
            row_spec(tile, width),
            full_spec(1, width),
            full_spec(width, columns),
            full_spec(1, columns),
            row_spec(tile, PAIR),
            row_spec(tile, PAIR),
        ],
        out_specs=[row_spec(tile, width), row_spec(tile, Q_WIDTH), row_spec(tile, 2 * K_WIDTH)],
        out_shape=[
            jax.ShapeDtypeStruct((rows, width), bf16),
            jax.ShapeDtypeStruct((rows, Q_WIDTH), bf16),
            jax.ShapeDtypeStruct((rows, 2 * K_WIDTH), bf16),
        ],
        cost_estimate=pl.CostEstimate(
            flops=4 * rows * width * columns, bytes_accessed=5 << 20, transcendentals=0
        ),
        compiler_params=params(),
        name="project_forward",
    )(tokens, gain, weight, bias, cosine, sine)


def project_back_kernel(
    gq_ref, w_ref, x_ref, gain_ref, hidden_ref, cos_ref, sin_ref, *rest
):
    parts = rest[:-4]
    gkv_ref, tokens_ref, gain_sum_ref, bias_sum_ref = rest[-4:]
    total = parts[0][...].astype(f32)
    for part in parts[1:]:
        total = total + part[...].astype(f32)
    turned = turn_pair(total[:, :K_WIDTH], cos_ref[...], -sin_ref[...]).astype(bf16)
    gkv_ref[:, :K_WIDTH] = turned
    gkv_ref[:, K_WIDTH:] = total[:, K_WIDTH:].astype(bf16)
    grads = jnp.concatenate([gq_ref[...], gkv_ref[...]], axis=1)
    grad_normed = dot(grads, w_ref[...], NT)
    x = x_ref[...].astype(f32)
    inverse = inverse_rms(x)
    weighted = grad_normed * gain_ref[...]
    tokens_ref[...] = (
        hidden_ref[...]
        + inverse * weighted
        - x * (inverse * inverse * inverse * jnp.mean(weighted * x, axis=-1, keepdims=True))
    )

    @pl.when(pl.program_id(0) == 0)
    def _():
        gain_sum_ref[...] = jnp.zeros_like(gain_sum_ref)
        bias_sum_ref[...] = jnp.zeros_like(bias_sum_ref)

    gain_sum_ref[...] += jnp.sum(grad_normed * x * inverse, axis=0, keepdims=True)
    bias_sum_ref[...] += jnp.sum(grads.astype(f32), axis=0, keepdims=True)


def project_backward(grad_queries, weight, tokens, gain, grad_hidden, cosine, sine, parts):
    rows, width = tokens.shape
    tile = rows // 2
    columns = weight.shape[1]
    return pl.pallas_call(
        project_back_kernel,
        grid=(2,),
        in_specs=[
            row_spec(tile, Q_WIDTH),
            full_spec(width, columns),
            row_spec(tile, width),
            full_spec(1, width),
            row_spec(tile, width),
            row_spec(tile, PAIR),
            row_spec(tile, PAIR),
        ]
        + [row_spec(tile, 2 * K_WIDTH)] * len(parts),
        out_specs=[
            row_spec(tile, 2 * K_WIDTH),
            row_spec(tile, width),
            full_spec(1, width),
            full_spec(1, columns),
        ],
        out_shape=[
            jax.ShapeDtypeStruct((rows, 2 * K_WIDTH), bf16),
            jax.ShapeDtypeStruct((rows, width), f32),
            jax.ShapeDtypeStruct((1, width), f32),
            jax.ShapeDtypeStruct((1, columns), f32),
        ],
        cost_estimate=pl.CostEstimate(
            flops=4 * rows * width * columns, bytes_accessed=8 << 20, transcendentals=0
        ),
        compiler_params=params(),
        name="project_backward",
    )(grad_queries, weight, tokens, gain, grad_hidden, cosine, sine, *parts)


def pair_sides(both):
    x, x_swapped = both[:, :PAIR], both[:, PAIR:]
    low = lax.broadcasted_iota(jnp.int32, x.shape, 1) < HEAD_DIM
    zero = jnp.zeros_like(x)
    left = (jnp.where(low, x, zero), jnp.where(low, x_swapped, zero))
    right = (jnp.where(low, zero, x_swapped), jnp.where(low, zero, x))
    sides = {}
    for pair in range(PAIRS):
        key = (2 * pair // GROUP, (2 * pair + 1) // GROUP)
        if key not in sides:
            sides[key] = jnp.concatenate([left[key[0]], right[key[1]]], axis=0)
    return sides


def causal(block):
    key_at = lax.broadcasted_iota(jnp.int32, (block, block), 0)
    query_at = lax.broadcasted_iota(jnp.int32, (block, block), 1)
    return key_at <= query_at


def forward_kernel(order_ref, q_ref, *rest):
    parts = rest[:-7]
    o_ref, lse_ref, keys_ref, turned_ref, top_ref, total_ref, acc_ref = rest[-7:]
    block = q_ref.shape[1]
    turn = pl.program_id(0) % 2
    last = order_ref[turn]

    @pl.when(turn == 0)
    def _():
        for number, part in enumerate(parts):
            for half in range(2):
                at = order_ref[2 * number + half]
                keys = part[0, half, :, :K_WIDTH]
                keys_ref[at, :, :PAIR] = keys
                keys_ref[at, :, PAIR:] = swap_pair(keys).astype(bf16)
                turned_ref[at] = jnp.transpose(part[0, half, :, K_WIDTH:].astype(f32)).astype(
                    bf16
                )

    top_ref[...] = jnp.full_like(top_ref, masked_value)
    total_ref[...] = jnp.zeros_like(total_ref)
    acc_ref[...] = jnp.zeros_like(acc_ref)
    scale = score_scale * log2_e

    def step(index, diagonal):
        sides = pair_sides(keys_ref[index])
        values = turned_ref[index]
        if diagonal:
            allowed = causal(block)
        for pair in range(PAIRS):
            both = dot(
                sides[(2 * pair // GROUP, (2 * pair + 1) // GROUP)],
                q_ref[0, :, pair * PAIR : (pair + 1) * PAIR],
                NT,
            )
            for odd in range(2):
                head = 2 * pair + odd
                kv = head // GROUP
                scores = both[odd * block : (odd + 1) * block] * scale
                if diagonal:
                    scores = jnp.where(allowed, scores, masked_value)
                old = top_ref[head : head + 1, :]
                new = jnp.maximum(old, jnp.max(scores, axis=0, keepdims=True))
                shrink = jnp.exp2(old - new)
                weights = jnp.exp2(scores - new)
                top_ref[head : head + 1, :] = new
                total_ref[head : head + 1, :] = total_ref[
                    head : head + 1, :
                ] * shrink + jnp.sum(weights, axis=0, keepdims=True)
                rows = slice(head * HEAD_DIM, (head + 1) * HEAD_DIM)
                acc_ref[rows, :] = acc_ref[rows, :] * shrink + dot(
                    values[kv * HEAD_DIM : (kv + 1) * HEAD_DIM], weights.astype(bf16), NN
                )

    def body(index, carry):
        step(index, False)
        return carry

    lax.fori_loop(0, last, body, 0)
    step(last, True)
    for pair in range(PAIRS):
        halves = []
        for odd in range(2):
            head = 2 * pair + odd
            halves.append(
                acc_ref[head * HEAD_DIM : (head + 1) * HEAD_DIM, :]
                / total_ref[head : head + 1, :]
            )
        o_ref[0, :, pair * PAIR : (pair + 1) * PAIR] = jnp.transpose(
            jnp.concatenate(halves, axis=0)
        ).astype(bf16)
    lse_ref[0] = top_ref[...] + jnp.log2(total_ref[...])


def backward_kernel(order_ref, q_ref, o_ref, g_ref, lse_ref, cos_ref, sin_ref, *rest):
    parts = rest[:-8]
    dq_ref, dkv_ref, keys_ref, values_ref, turned_ref, dk_ref, dv_ref, acc_ref = rest[-8:]
    block = q_ref.shape[1]
    turn = pl.program_id(0) % 2
    last = order_ref[turn]
    scale = score_scale * log2_e

    @pl.when(turn == 0)
    def _():
        dk_ref[...] = jnp.zeros_like(dk_ref)
        dv_ref[...] = jnp.zeros_like(dv_ref)
        for number, part in enumerate(parts):
            for half in range(2):
                at = order_ref[2 * number + half]
                keys = part[0, half, :, :K_WIDTH]
                values = part[0, half, :, K_WIDTH:]
                keys_ref[at, :, :PAIR] = keys
                keys_ref[at, :, PAIR:] = swap_pair(keys).astype(bf16)
                values_ref[at, :, :PAIR] = values
                values_ref[at, :, PAIR:] = swap_pair(values).astype(bf16)
                turned_ref[at] = jnp.transpose(keys.astype(f32)).astype(bf16)

    acc_ref[...] = jnp.zeros_like(acc_ref)
    product = g_ref[0].astype(f32) * o_ref[0].astype(f32)
    coarse = product.astype(bf16)
    fine = (product - coarse.astype(f32)).astype(bf16)
    head_of = lax.broadcasted_iota(jnp.int32, (16, Q_WIDTH), 1) // HEAD_DIM
    picks = (head_of == lax.broadcasted_iota(jnp.int32, (16, Q_WIDTH), 0)).astype(bf16)
    delta = dot(picks, coarse, NT) + dot(picks, fine, NT)

    def step(index, diagonal):
        key_sides = pair_sides(keys_ref[index])
        value_sides = pair_sides(values_ref[index])
        keys_turned = turned_ref[index]
        if diagonal:
            allowed = causal(block)
        key_sum = [[None, None], [None, None]]
        value_sum = [[None, None], [None, None]]

        def add(sums, odd, kv, part):
            sums[odd][kv] = part if sums[odd][kv] is None else sums[odd][kv] + part

        for pair in range(PAIRS):
            which = (2 * pair // GROUP, (2 * pair + 1) // GROUP)
            lanes = slice(pair * PAIR, (pair + 1) * PAIR)
            queries = q_ref[0, :, lanes]
            grads = g_ref[0, :, lanes]
            both = dot(key_sides[which], queries, NT)
            both_grads = dot(value_sides[which], grads, NT)
            low_weights = []
            low_scores = []
            for odd in range(2):
                head = 2 * pair + odd
                part = slice(odd * block, (odd + 1) * block)
                weights = jnp.exp2(both[part] * scale - lse_ref[0, head : head + 1, :])
                if diagonal:
                    weights = jnp.where(allowed, weights, 0.0)
                change = weights * (both_grads[part] - delta[head : head + 1, :])
                low_weights.append(weights.astype(bf16))
                low_scores.append(change.astype(bf16))
                rows = slice(head * HEAD_DIM, (head + 1) * HEAD_DIM)
                acc_ref[rows, :] += dot(
                    keys_turned[which[odd] * HEAD_DIM : (which[odd] + 1) * HEAD_DIM],
                    low_scores[odd],
                    NN,
                )
            value_part = dot(jnp.concatenate(low_weights, axis=0), grads, NN)
            key_part = dot(jnp.concatenate(low_scores, axis=0), queries, NN)
            for odd in range(2):
                part = slice(odd * block, (odd + 1) * block)
                add(value_sum, odd, which[odd], value_part[part])
                add(key_sum, odd, which[odd], key_part[part])
        low = lax.broadcasted_iota(jnp.int32, (block, PAIR), 1) < HEAD_DIM
        for sums, out_ref in ((key_sum, dk_ref), (value_sum, dv_ref)):
            out_ref[index, :, :PAIR] += jnp.where(low, sums[0][0], sums[1][1])
            out_ref[index, :, PAIR:] += jnp.where(low, sums[0][1], sums[1][0])

    def body(index, carry):
        step(index, False)
        return carry

    lax.fori_loop(0, last, body, 0)
    step(last, True)
    for pair in range(PAIRS):
        straight = jnp.transpose(acc_ref[pair * PAIR : (pair + 1) * PAIR, :]) * score_scale
        dq_ref[0, :, pair * PAIR : (pair + 1) * PAIR] = turn_pair(
            straight, cos_ref[0], -sin_ref[0]
        ).astype(bf16)

    @pl.when(turn == 1)
    def _():
        for slot in range(2 * len(parts)):
            at = order_ref[slot]
            keys = dk_ref[at, :, :PAIR] + swap_pair(dk_ref[at, :, PAIR:])
            dkv_ref[0, slot, :, :K_WIDTH] = (keys * score_scale).astype(bf16)
            values = dv_ref[at, :, :PAIR] + swap_pair(dv_ref[at, :, PAIR:])
            dkv_ref[0, slot, :, K_WIDTH:] = values.astype(bf16)


def attention_specs(block, parts):
    def rows(width):
        return pl.BlockSpec((1, block, width), lambda i, order: (i, 0, 0))

    def halves(number):
        return pl.BlockSpec((1, number, block, 2 * K_WIDTH), lambda i, order: (i // 2, 0, 0, 0))

    stats = pl.BlockSpec((1, 16, block), lambda i, order: (i, 0, 0))
    return rows, halves, stats


def attend_forward(order, queries, parts):
    count, block, _ = queries.shape
    slots = 2 * len(parts)
    rows, halves, stats = attention_specs(block, parts)
    pairs_done = count * block * (slots // 2 + 1) * block * HEADS
    return pl.pallas_call(
        forward_kernel,
        grid_spec=pltpu.PrefetchScalarGridSpec(
            num_scalar_prefetch=1,
            grid=(count,),
            in_specs=[rows(Q_WIDTH)] + [halves(2)] * len(parts),
            out_specs=[rows(Q_WIDTH), stats],
            scratch_shapes=[
                pltpu.VMEM((slots, block, 2 * PAIR), bf16),
                pltpu.VMEM((slots, PAIR, block), bf16),
                pltpu.VMEM((16, block), f32),
                pltpu.VMEM((16, block), f32),
                pltpu.VMEM((Q_WIDTH, block), f32),
            ],
        ),
        out_shape=[
            jax.ShapeDtypeStruct((count, block, Q_WIDTH), bf16),
            jax.ShapeDtypeStruct((count, 16, block), f32),
        ],
        cost_estimate=pl.CostEstimate(
            flops=pairs_done * 4 * 256, bytes_accessed=4 << 20, transcendentals=pairs_done
        ),
        compiler_params=params(),
        name="attend_forward",
    )(order, queries, *parts)


def attend_backward(order, queries, parts, mixed, grads, stats_in, cosine, sine):
    count, block, _ = queries.shape
    slots = 2 * len(parts)
    rows, halves, stats = attention_specs(block, parts)
    pairs_done = count * block * (slots // 2 + 1) * block * HEADS
    return pl.pallas_call(
        backward_kernel,
        grid_spec=pltpu.PrefetchScalarGridSpec(
            num_scalar_prefetch=1,
            grid=(count,),
            in_specs=[
                rows(Q_WIDTH),
                rows(Q_WIDTH),
                rows(Q_WIDTH),
                stats,
                rows(PAIR),
                rows(PAIR),
            ]
            + [halves(2)] * len(parts),
            out_specs=[rows(Q_WIDTH), halves(slots)],
            scratch_shapes=[
                pltpu.VMEM((slots, block, 2 * PAIR), bf16),
                pltpu.VMEM((slots, block, 2 * PAIR), bf16),
                pltpu.VMEM((slots, PAIR, block), bf16),
                pltpu.VMEM((slots, block, 2 * PAIR), f32),
                pltpu.VMEM((slots, block, 2 * PAIR), f32),
                pltpu.VMEM((Q_WIDTH, block), f32),
            ],
        ),
        out_shape=[
            jax.ShapeDtypeStruct((count, block, Q_WIDTH), bf16),
            jax.ShapeDtypeStruct((count // 2, slots, block, 2 * K_WIDTH), bf16),
        ],
        cost_estimate=pl.CostEstimate(
            flops=pairs_done * 10 * 256, bytes_accessed=8 << 20, transcendentals=pairs_done
        ),
        compiler_params=params(),
        name="attend_backward",
    )(order, queries, mixed, grads, stats_in, cosine, sine, *parts)


def ffn_kernel(x_ref, c_ref, w_ref, *rest):
    out_ref, grad_ref, x_all, c_all, active_all, gate_all, up_all = rest[-7:]
    seq_size, _, depth, columns = w_ref.shape
    width = seq_size * depth
    x = x_ref[...]
    c = c_ref[...]
    x_all[0] = x
    c_all[0] = c
    gate_w = w_ref[:, 0].reshape(width, columns)
    up_w = w_ref[:, 1].reshape(width, columns)
    down_w = w_ref[:, 2].reshape(width, columns)
    gate = dot(x, gate_w, NN)
    up = dot(x, up_w, NN)
    grad_active = dot(c, down_w, NN)
    sigmoid = jax.nn.sigmoid(gate)
    silu = gate * sigmoid
    active = (silu * up).astype(bf16)
    grad_gate = (grad_active * up * sigmoid * (1.0 + gate * (1.0 - sigmoid))).astype(bf16)
    grad_up = (grad_active * silu).astype(bf16)
    active_all[0] = active
    gate_all[0] = grad_gate
    up_all[0] = grad_up
    grad_ref[...] = (dot(grad_gate, gate_w, NT) + dot(grad_up, up_w, NT)).astype(bf16)
    out_ref[...] = dot(active, down_w, NT).astype(bf16)


def ffn(number, count, x, c, weights, buffers):
    rows, width = x.shape
    columns = weights.shape[3]
    tile = rows // 2

    def slot(columns):
        return pl.BlockSpec((1, tile, columns), lambda i: (number, i, 0))

    wide = jax.ShapeDtypeStruct((count, rows, width), bf16)
    inner = jax.ShapeDtypeStruct((count, rows, columns), bf16)
    return pl.pallas_call(
        ffn_kernel,
        grid=(2,),
        in_specs=[row_spec(tile, width), row_spec(tile, width), full_spec(*weights.shape)]
        + [pl.BlockSpec(memory_space=pl.ANY)] * len(buffers),
        out_specs=[row_spec(tile, width), row_spec(tile, width)]
        + [slot(width)] * 2
        + [slot(columns)] * 3,
        out_shape=[jax.ShapeDtypeStruct((rows, width), bf16)] * 2 + [wide] * 2 + [inner] * 3,
        input_output_aliases={3 + i: 2 + i for i in range(len(buffers))},
        cost_estimate=pl.CostEstimate(
            flops=14 * rows * width * columns, bytes_accessed=16 << 20, transcendentals=0
        ),
        compiler_params=params(),
        name="ffn",
    )(x, c, weights, *buffers)


def ffn_weights_kernel(x_ref, c_ref, active_ref, gate_ref, up_ref, out_ref, acc_ref):
    step = pl.program_id(0)
    seq_size, _, depth, columns = out_ref.shape

    @pl.when(step == 0)
    def _():
        acc_ref[...] = jnp.zeros_like(acc_ref)

    x = x_ref[0]
    acc_ref[0] += dot(x, gate_ref[0], TN)
    acc_ref[1] += dot(x, up_ref[0], TN)
    acc_ref[2] += dot(c_ref[0], active_ref[0], TN)

    @pl.when(step == pl.num_programs(0) - 1)
    def _():
        for which in range(3):
            out_ref[:, which] = acc_ref[which].reshape(seq_size, depth, columns).astype(bf16)


def ffn_weights(seq_size, x, c, active, grad_gate, grad_up):
    count, rows, width = x.shape
    columns = active.shape[2]

    def slot(columns):
        return pl.BlockSpec((1, rows, columns), lambda i: (i, 0, 0))

    shape = (seq_size, 3, width // seq_size, columns)
    return pl.pallas_call(
        ffn_weights_kernel,
        grid=(count,),
        in_specs=[slot(width)] * 2 + [slot(columns)] * 3,
        out_specs=pl.BlockSpec(shape, lambda i: (0, 0, 0, 0)),
        out_shape=jax.ShapeDtypeStruct(shape, bf16),
        scratch_shapes=[pltpu.VMEM((3, width, columns), f32)],
        cost_estimate=pl.CostEstimate(
            flops=6 * count * rows * width * columns, bytes_accessed=30 << 20, transcendentals=0
        ),
        compiler_params=params(),
        name="ffn_weights",
    )(x, c, active, grad_gate, grad_up)


def hop(x, ctx_size, mask):
    return lax.ppermute(x, "ctx", [(i, i ^ mask) for i in range(ctx_size)])


def spread(x, ctx_size):
    if ctx_size != 4:
        return [x] + [hop(x, ctx_size, k) for k in range(1, ctx_size)]
    half = x.shape[0] // 2
    front, back = x[:half], x[half:]
    front_1 = hop(front, 4, 1)
    back_2 = hop(back, 4, 2)
    front_far = hop(jnp.concatenate([front, front_1], axis=0), 4, 2)
    back_far = hop(jnp.concatenate([back, back_2], axis=0), 4, 1)
    return [x, jnp.concatenate([front_1, back_2], axis=0), front_far, back_far]


def gathered_sum(parts, ctx_size):
    if ctx_size != 4:
        total = parts[0].astype(f32)
        for k in range(1, ctx_size):
            total = total + hop(parts[k], ctx_size, k).astype(f32)
        return total
    own, near, front_far, back_far = parts
    half = own.shape[0] // 2
    front_got = hop(front_far, 4, 2)
    back_got = hop(back_far, 4, 1)
    front_next = (near[:half].astype(f32) + front_got[half:].astype(f32)).astype(bf16)
    back_next = (near[half:].astype(f32) + back_got[half:].astype(f32)).astype(bf16)
    front_last = hop(front_next, 4, 1)
    back_last = hop(back_next, 4, 2)
    return jnp.concatenate(
        [
            own[:half].astype(f32) + front_got[:half].astype(f32) + front_last.astype(f32),
            own[half:].astype(f32) + back_got[:half].astype(f32) + back_last.astype(f32),
        ],
        axis=0,
    )


def in_order(pieces, place, ctx_size):
    result = jnp.zeros((ctx_size,) + pieces[0].shape, pieces[0].dtype)
    for k, piece in enumerate(pieces):
        result = lax.dynamic_update_index_in_dim(result, piece, place ^ k, 0)
    return result


def on_device(
    seq_size,
    ctx_size,
    tokens,
    attention_gain,
    project_weight,
    project_bias,
    output_weight,
    feedforward_gain,
    gate_weight,
    up_weight,
    down_weight,
    cotangent,
):
    sequences, block_rows, width = tokens.shape
    place = lax.axis_index("ctx")
    half = block_rows // 2
    rows = sequences * block_rows
    fold = seq_size // ctx_size
    fold_place = lax.axis_index("seq") % fold
    mirror = [(i, ctx_size - 1 - i) for i in range(ctx_size)]

    def crossed(x, j):
        return lax.ppermute(
            x,
            ("seq", "ctx"),
            [
                ((c * fold + r) * ctx_size + q, (q * fold + (r + j) % fold) * ctx_size + c)
                for c in range(ctx_size)
                for r in range(fold)
                for q in range(ctx_size)
            ],
        )

    def crossed_parts(parts):
        came = jnp.zeros_like(parts)
        for j in range(fold):
            part = lax.dynamic_index_in_dim(parts, (fold_place + j) % fold, 0, keepdims=False)
            came = lax.dynamic_update_index_in_dim(
                came, crossed(part, j), (fold_place - j) % fold, 0
            )
        return came

    def zigzag(x):
        return jnp.concatenate([x[:, :half], lax.ppermute(x[:, half:], "ctx", mirror)], axis=1)

    owners = [place ^ k for k in range(ctx_size)]
    order = jnp.stack(
        [spot for owner in owners for spot in (2 * owner, 2 * (ctx_size - 1 - owner) + 1)]
    ).astype(jnp.int32)
    positions = (order[:2, None] * half + jnp.arange(half, dtype=jnp.int32)[None, :]).reshape(-1)
    cosine, sine = rotation_tables(jnp.tile(positions, sequences))

    def columns_whole(shard):
        pieces = [shard] + [hop(shard, ctx_size, k) for k in range(1, ctx_size)]
        ordered = in_order(pieces, place, ctx_size)
        return jnp.moveaxis(ordered, 0, 1).reshape(shard.shape[0], -1)

    gain_width = attention_gain.shape[0]
    bias_width = project_bias.shape[0]
    project_full = lax.all_gather(columns_whole(project_weight), "seq", axis=0, tiled=True)
    vectors = jnp.concatenate([attention_gain, project_bias, feedforward_gain])[None, :]
    vector_pieces = [vectors] + [hop(vectors, ctx_size, k) for k in range(1, ctx_size)]
    vectors_all = in_order(vector_pieces, place, ctx_size)[:, 0, :].astype(f32)
    attention_full = vectors_all[:, :gain_width].reshape(1, -1)
    bias_full = vectors_all[:, gain_width : gain_width + bias_width].reshape(1, -1)
    feedforward_full = vectors_all[:, gain_width + bias_width :].reshape(1, -1)

    output_columns = columns_whole(output_weight)
    down_rows, down_columns = down_weight.shape
    depth = down_columns // fold
    down_turned = crossed_parts(down_weight.T.reshape(fold, depth, down_rows))
    down_turned = jnp.moveaxis(down_turned, 0, 1).reshape(depth, fold * down_rows)
    output_full = lax.all_gather(output_columns, "seq", axis=0, tiled=True)
    weights_mine = lax.all_gather(
        jnp.stack([gate_weight, up_weight, down_turned]), "seq", axis=0
    )

    tokens_mine = zigzag(tokens).reshape(rows, width)
    normed, queries, pairs_mine = project_forward(
        tokens_mine, attention_full, project_full, bias_full, cosine, sine
    )
    queries = queries.reshape(sequences * 2, half, Q_WIDTH)
    pairs_mine = pairs_mine.reshape(sequences, 2, half, 2 * K_WIDTH)
    pair_parts = [pairs_mine] + [hop(pairs_mine, ctx_size, k) for k in range(1, ctx_size)]
    cotangent_late = lax.optimization_barrier((cotangent, pair_parts[-1]))[0]
    grad_low = zigzag(cotangent_late).reshape(rows, width)
    grad_parts = spread(grad_low, ctx_size)
    mixed, row_stats = attend_forward(order, queries, pair_parts)
    mixed_rows = mixed.reshape(rows, Q_WIDTH)
    hidden = tokens_mine.astype(f32) + dot(mixed_rows, output_full, NN)
    inverse_ffn = inverse_rms(hidden)
    normed_ffn = (hidden * inverse_ffn * feedforward_full).astype(bf16)

    normed_parts = spread(normed_ffn, ctx_size)
    output_parts = []
    grad_normed_parts = []
    buffers = []
    for number, (part, grad_part) in enumerate(zip(normed_parts, grad_parts)):
        output_part, grad_normed_part, *buffers = ffn(
            number, ctx_size, part, grad_part, weights_mine, buffers
        )
        output_parts.append(output_part)
        grad_normed_parts.append(grad_normed_part)
    grad_normed_ffn = gathered_sum(grad_normed_parts, ctx_size)
    weight_grads = lax.psum_scatter(ffn_weights(seq_size, *buffers), "seq", scatter_dimension=0)

    grad_ffn_gain = jnp.sum(grad_normed_ffn * hidden * inverse_ffn, axis=0)
    weighted_ffn = grad_normed_ffn * feedforward_full
    grad_hidden = (
        grad_low.astype(f32)
        + inverse_ffn * weighted_ffn
        - hidden
        * inverse_ffn
        * inverse_ffn
        * inverse_ffn
        * jnp.mean(weighted_ffn * hidden, axis=-1, keepdims=True)
    )
    hidden_low = grad_hidden.astype(bf16)
    grad_mixed = dot(hidden_low, output_full, NT).astype(bf16)

    grad_queries, pair_grads = attend_backward(
        order,
        queries,
        pair_parts,
        mixed,
        grad_mixed.reshape(sequences * 2, half, Q_WIDTH),
        row_stats,
        cosine.reshape(sequences * 2, half, PAIR),
        sine.reshape(sequences * 2, half, PAIR),
    )
    pair_sums = [pair_grads[:, :2].reshape(rows, 2 * K_WIDTH)]
    for k in range(1, ctx_size):
        pair_sums.append(
            hop(pair_grads[:, 2 * k : 2 * k + 2], ctx_size, k).reshape(rows, 2 * K_WIDTH)
        )
    grad_queries = grad_queries.reshape(rows, Q_WIDTH)
    grad_pairs, tokens_grad, gain_sum, bias_sum = project_backward(
        grad_queries,
        project_full,
        tokens_mine,
        attention_full,
        grad_hidden,
        cosine,
        sine,
        pair_sums,
    )

    def columns_then_rows_summed(turned):
        parts = turned.astype(bf16).reshape(ctx_size, turned.shape[0] // ctx_size, turned.shape[1])

        def part(k):
            return lax.dynamic_index_in_dim(parts, place ^ k, 0, keepdims=False)

        total = part(0).astype(f32)
        for k in range(1, ctx_size):
            total = total + hop(part(k), ctx_size, k).astype(f32)
        return lax.psum_scatter(
            total.astype(bf16).T, "seq", scatter_dimension=0, tiled=True
        ).astype(f32)

    output_out = columns_then_rows_summed(dot(hidden_low, mixed_rows, TN))
    project_out = columns_then_rows_summed(
        dot(jnp.concatenate([grad_queries, grad_pairs], axis=1), normed, TN)
    )

    tokens_grad = tokens_grad.reshape(tokens.shape)
    tokens_gradient = jnp.concatenate(
        [
            tokens_grad[:, :half],
            lax.ppermute(tokens_grad[:, half:].astype(bf16), "ctx", mirror).astype(f32),
        ],
        axis=1,
    )
    output_late = lax.optimization_barrier((tuple(output_parts), grad_mixed))[0]
    output_zigzag = hidden + gathered_sum(list(output_late), ctx_size)
    layer_output = zigzag(output_zigzag.astype(bf16).reshape(tokens.shape))

    down_grads = weight_grads[2].reshape(depth, fold, down_rows)
    down_out = crossed_parts(jnp.moveaxis(down_grads, 1, 0)).reshape(down_columns, down_rows).T

    sums = lax.psum(
        jnp.concatenate([gain_sum[0], bias_sum[0], grad_ffn_gain]), ("seq", "ctx")
    )

    def my_part(start, whole):
        own = whole // ctx_size
        return lax.dynamic_slice_in_dim(sums, start + place * own, own, 0)

    project_width = bias_width * ctx_size
    return (
        layer_output,
        tokens_gradient,
        my_part(0, width),
        project_out,
        my_part(width, project_width),
        output_out,
        my_part(width + project_width, width),
        weight_grads[0].astype(f32),
        weight_grads[1].astype(f32),
        down_out.astype(f32),
    )


def solution(mesh):
    matrix = P("seq", "ctx")
    vector = P("ctx")
    activation = P("seq", "ctx", None)

    def step(*arrays):
        return on_device(mesh.shape["seq"], mesh.shape["ctx"], *arrays)

    return jax.shard_map(
        step,
        mesh=mesh,
        in_specs=(
            activation,
            vector,
            matrix,
            vector,
            matrix,
            vector,
            matrix,
            matrix,
            matrix,
            activation,
        ),
        out_specs=(
            activation,
            activation,
            vector,
            matrix,
            vector,
            matrix,
            vector,
            matrix,
            matrix,
            matrix,
        ),
        check_vma=False,
    )
```

```python
import math
import jax
import jax.numpy as jnp
from jax import lax
from jax.experimental import pallas as pl
from jax.experimental.pallas import tpu as pltpu
from jax.sharding import PartitionSpec as P

HEADS = 14
KV_HEADS = 2
HEAD_DIM = 64
GROUP = HEADS // KV_HEADS
PAIRS = HEADS // 2
PAIR = 2 * HEAD_DIM
Q_WIDTH = HEADS * HEAD_DIM
K_WIDTH = KV_HEADS * HEAD_DIM

norm_eps = 1e-06
rope_base = 1000000.0
masked_value = -1e30
score_scale = HEAD_DIM ** (-0.5)
log2_e = math.log2(math.e)
bf16 = jnp.bfloat16
f32 = jnp.float32


def inverse_rms(tensor):
    return lax.rsqrt(jnp.mean(tensor * tensor, axis=-1, keepdims=True) + norm_eps)


def dot(a, b, dims):
    return lax.dot_general(a, b, (dims, ((), ())), preferred_element_type=f32)


NN = ((1,), (0,))
NT = ((1,), (1,))
TN = ((0,), (0,))


def rotation_tables(positions):
    half_width = HEAD_DIM // 2
    steps_up = jnp.arange(half_width).astype(f32)
    frequency = jnp.power(jnp.asarray(rope_base, f32), -2.0 * steps_up / HEAD_DIM)
    angles = positions.astype(f32)[:, None] * frequency[None, :]
    cosine = jnp.cos(angles)
    sine = jnp.sin(angles)
    return (
        jnp.concatenate([cosine, cosine, cosine, cosine], axis=-1),
        jnp.concatenate([-sine, sine, -sine, sine], axis=-1),
    )


def turn_pair(x, cosine, sine):
    lane = lax.broadcasted_iota(jnp.int32, x.shape, 1)
    quarter = HEAD_DIM // 2
    other = jnp.where(
        (lane // quarter) % 2 == 0,
        pltpu.roll(x, PAIR - quarter, 1),
        pltpu.roll(x, quarter, 1),
    )
    return x * cosine + other * sine


def swap_pair(x):
    return pltpu.roll(x.astype(f32), HEAD_DIM, 1)


def params():
    return pltpu.CompilerParams(vmem_limit_bytes=60 << 20)


def project_kernel(x_ref, gain_ref, w_ref, bias_ref, cos_ref, sin_ref, normed_ref, q_ref, kv_ref):
    x = x_ref[...].astype(f32)
    normed = (x * inverse_rms(x) * gain_ref[...]).astype(bf16)
    normed_ref[...] = normed
    projected = dot(normed, w_ref[...], NN) + bias_ref[...]
    cosine = cos_ref[...]
    sine = sin_ref[...]
    for pair in range(PAIRS + 1):
        lanes = slice(pair * PAIR, (pair + 1) * PAIR)
        turned = turn_pair(projected[:, lanes], cosine, sine).astype(bf16)
        if pair < PAIRS:
            q_ref[:, lanes] = turned
        else:
            kv_ref[:, :K_WIDTH] = turned
    kv_ref[:, K_WIDTH:] = projected[:, Q_WIDTH + K_WIDTH :].astype(bf16)


def row_spec(tile, width):
    return pl.BlockSpec((tile, width), lambda i: (i, 0))


def full_spec(*shape):
    return pl.BlockSpec(shape, lambda i: (0,) * len(shape))


def project_forward(tokens, gain, weight, bias, cosine, sine):
    rows, width = tokens.shape
    tile = rows // 2
    columns = Q_WIDTH + 2 * K_WIDTH
    return pl.pallas_call(
        project_kernel,
        grid=(2,),
        in_specs=[
            row_spec(tile, width),
            full_spec(1, width),
            full_spec(width, columns),
            full_spec(1, columns),
            row_spec(tile, PAIR),
            row_spec(tile, PAIR),
        ],
        out_specs=[row_spec(tile, width), row_spec(tile, Q_WIDTH), row_spec(tile, 2 * K_WIDTH)],
        out_shape=[
            jax.ShapeDtypeStruct((rows, width), bf16),
            jax.ShapeDtypeStruct((rows, Q_WIDTH), bf16),
            jax.ShapeDtypeStruct((rows, 2 * K_WIDTH), bf16),
        ],
        cost_estimate=pl.CostEstimate(
            flops=4 * rows * width * columns, bytes_accessed=5 << 20, transcendentals=0
        ),
        compiler_params=params(),
        name="project_forward",
    )(tokens, gain, weight, bias, cosine, sine)


def project_back_kernel(
    gq_ref, w_ref, x_ref, gain_ref, hidden_ref, cos_ref, sin_ref, *rest
):
    parts = rest[:-4]
    gkv_ref, tokens_ref, gain_sum_ref, bias_sum_ref = rest[-4:]
    total = parts[0][...].astype(f32)
    for part in parts[1:]:
        total = total + part[...].astype(f32)
    turned = turn_pair(total[:, :K_WIDTH], cos_ref[...], -sin_ref[...]).astype(bf16)
    gkv_ref[:, :K_WIDTH] = turned
    gkv_ref[:, K_WIDTH:] = total[:, K_WIDTH:].astype(bf16)
    grads = jnp.concatenate([gq_ref[...], gkv_ref[...]], axis=1)
    grad_normed = dot(grads, w_ref[...], NT)
    x = x_ref[...].astype(f32)
    inverse = inverse_rms(x)
    weighted = grad_normed * gain_ref[...]
    tokens_ref[...] = (
        hidden_ref[...]
        + inverse * weighted
        - x * (inverse * inverse * inverse * jnp.mean(weighted * x, axis=-1, keepdims=True))
    )

    @pl.when(pl.program_id(0) == 0)
    def _():
        gain_sum_ref[...] = jnp.zeros_like(gain_sum_ref)
        bias_sum_ref[...] = jnp.zeros_like(bias_sum_ref)

    gain_sum_ref[...] += jnp.sum(grad_normed * x * inverse, axis=0, keepdims=True)
    bias_sum_ref[...] += jnp.sum(grads.astype(f32), axis=0, keepdims=True)


def project_backward(grad_queries, weight, tokens, gain, grad_hidden, cosine, sine, parts):
    rows, width = tokens.shape
    tile = rows // 2
    columns = Q_WIDTH + 2 * K_WIDTH
    return pl.pallas_call(
        project_back_kernel,
        grid=(2,),
        in_specs=[
            row_spec(tile, Q_WIDTH),
            full_spec(width, columns),
            row_spec(tile, width),
            full_spec(1, width),
            row_spec(tile, width),
            row_spec(tile, PAIR),
            row_spec(tile, PAIR),
        ]
        + [row_spec(tile, 2 * K_WIDTH)] * len(parts),
        out_specs=[
            row_spec(tile, 2 * K_WIDTH),
            row_spec(tile, width),
            full_spec(1, width),
            full_spec(1, columns),
        ],
        out_shape=[
            jax.ShapeDtypeStruct((rows, 2 * K_WIDTH), bf16),
            jax.ShapeDtypeStruct((rows, width), f32),
            jax.ShapeDtypeStruct((1, width), f32),
            jax.ShapeDtypeStruct((1, columns), f32),
        ],
        cost_estimate=pl.CostEstimate(
            flops=4 * rows * width * columns, bytes_accessed=8 << 20, transcendentals=0
        ),
        compiler_params=params(),
        name="project_backward",
    )(grad_queries, weight, tokens, gain, grad_hidden, cosine, sine, *parts)


def pieces_kernel(lhs_ref, *rest):
    rhs_refs = rest[:-1]
    out_ref = rest[-1]
    ranks, owners, depth, own = out_ref.shape
    rhs = jnp.concatenate([ref[...] for ref in rhs_refs], axis=1)
    whole = dot(lhs_ref[...], rhs, TN)
    for rank in range(ranks):
        part = whole[:, rank * own : (rank + 1) * own]
        out_ref[rank] = part.reshape(owners, depth, own).astype(bf16)


def weight_pieces(ctx_size, seq_size, lhs, *rhs):
    rows, width = lhs.shape
    columns = sum(x.shape[1] for x in rhs)
    shape = (ctx_size, seq_size, width // seq_size, columns // ctx_size)
    return pl.pallas_call(
        pieces_kernel,
        grid=(1,),
        in_specs=[full_spec(*x.shape) for x in (lhs, *rhs)],
        out_specs=full_spec(*shape),
        out_shape=jax.ShapeDtypeStruct(shape, bf16),
        cost_estimate=pl.CostEstimate(
            flops=4 * rows * width * columns, bytes_accessed=5 << 20, transcendentals=0
        ),
        compiler_params=params(),
        name="weight_pieces",
    )(lhs, *rhs)


def pair_sides(both):
    x, x_swapped = both[:, :PAIR], both[:, PAIR:]
    low = lax.broadcasted_iota(jnp.int32, x.shape, 1) < HEAD_DIM
    zero = jnp.zeros_like(x)
    left = (jnp.where(low, x, zero), jnp.where(low, x_swapped, zero))
    right = (jnp.where(low, zero, x_swapped), jnp.where(low, zero, x))
    sides = {}
    for pair in range(PAIRS):
        key = (2 * pair // GROUP, (2 * pair + 1) // GROUP)
        if key not in sides:
            sides[key] = jnp.concatenate([left[key[0]], right[key[1]]], axis=0)
    return sides


def causal(block):
    key_at = lax.broadcasted_iota(jnp.int32, (block, block), 0)
    query_at = lax.broadcasted_iota(jnp.int32, (block, block), 1)
    return key_at <= query_at


def forward_kernel(order_ref, q_ref, *rest):
    parts = rest[:-7]
    o_ref, lse_ref, keys_ref, turned_ref, top_ref, total_ref, acc_ref = rest[-7:]
    block = q_ref.shape[1]
    turn = pl.program_id(0) % 2
    last = order_ref[turn]

    @pl.when(turn == 0)
    def _():
        for number, part in enumerate(parts):
            for half in range(2):
                at = order_ref[2 * number + half]
                keys = part[0, half, :, :K_WIDTH]
                keys_ref[at, :, :PAIR] = keys
                keys_ref[at, :, PAIR:] = swap_pair(keys).astype(bf16)
                turned_ref[at] = jnp.transpose(part[0, half, :, K_WIDTH:].astype(f32)).astype(
                    bf16
                )

    top_ref[...] = jnp.full_like(top_ref, masked_value)
    total_ref[...] = jnp.zeros_like(total_ref)
    acc_ref[...] = jnp.zeros_like(acc_ref)
    scale = score_scale * log2_e

    def step(index, diagonal):
        sides = pair_sides(keys_ref[index])
        values = turned_ref[index]
        if diagonal:
            allowed = causal(block)
        for pair in range(PAIRS):
            both = dot(
                sides[(2 * pair // GROUP, (2 * pair + 1) // GROUP)],
                q_ref[0, :, pair * PAIR : (pair + 1) * PAIR],
                NT,
            )
            for odd in range(2):
                head = 2 * pair + odd
                kv = head // GROUP
                scores = both[odd * block : (odd + 1) * block] * scale
                if diagonal:
                    scores = jnp.where(allowed, scores, masked_value)
                old = top_ref[head : head + 1, :]
                new = jnp.maximum(old, jnp.max(scores, axis=0, keepdims=True))
                shrink = jnp.exp2(old - new)
                weights = jnp.exp2(scores - new)
                top_ref[head : head + 1, :] = new
                total_ref[head : head + 1, :] = total_ref[
                    head : head + 1, :
                ] * shrink + jnp.sum(weights, axis=0, keepdims=True)
                rows = slice(head * HEAD_DIM, (head + 1) * HEAD_DIM)
                acc_ref[rows, :] = acc_ref[rows, :] * shrink + dot(
                    values[kv * HEAD_DIM : (kv + 1) * HEAD_DIM], weights.astype(bf16), NN
                )

    def body(index, carry):
        step(index, False)
        return carry

    lax.fori_loop(0, last, body, 0)
    step(last, True)
    for pair in range(PAIRS):
        halves = []
        for odd in range(2):
            head = 2 * pair + odd
            halves.append(
                acc_ref[head * HEAD_DIM : (head + 1) * HEAD_DIM, :]
                / total_ref[head : head + 1, :]
            )
        o_ref[0, :, pair * PAIR : (pair + 1) * PAIR] = jnp.transpose(
            jnp.concatenate(halves, axis=0)
        ).astype(bf16)
    lse_ref[0] = top_ref[...] + jnp.log2(total_ref[...])


def backward_kernel(order_ref, q_ref, o_ref, g_ref, lse_ref, cos_ref, sin_ref, *rest):
    parts = rest[:-8]
    dq_ref, dkv_ref, keys_ref, values_ref, turned_ref, dk_ref, dv_ref, acc_ref = rest[-8:]
    block = q_ref.shape[1]
    turn = pl.program_id(0) % 2
    last = order_ref[turn]
    scale = score_scale * log2_e

    @pl.when(turn == 0)
    def _():
        dk_ref[...] = jnp.zeros_like(dk_ref)
        dv_ref[...] = jnp.zeros_like(dv_ref)
        for number, part in enumerate(parts):
            for half in range(2):
                at = order_ref[2 * number + half]
                keys = part[0, half, :, :K_WIDTH]
                values = part[0, half, :, K_WIDTH:]
                keys_ref[at, :, :PAIR] = keys
                keys_ref[at, :, PAIR:] = swap_pair(keys).astype(bf16)
                values_ref[at, :, :PAIR] = values
                values_ref[at, :, PAIR:] = swap_pair(values).astype(bf16)
                turned_ref[at] = jnp.transpose(keys.astype(f32)).astype(bf16)

    acc_ref[...] = jnp.zeros_like(acc_ref)
    product = g_ref[0].astype(f32) * o_ref[0].astype(f32)
    coarse = product.astype(bf16)
    fine = (product - coarse.astype(f32)).astype(bf16)
    head_of = lax.broadcasted_iota(jnp.int32, (16, Q_WIDTH), 1) // HEAD_DIM
    picks = (head_of == lax.broadcasted_iota(jnp.int32, (16, Q_WIDTH), 0)).astype(bf16)
    delta = dot(picks, coarse, NT) + dot(picks, fine, NT)

    def step(index, diagonal):
        key_sides = pair_sides(keys_ref[index])
        value_sides = pair_sides(values_ref[index])
        keys_turned = turned_ref[index]
        if diagonal:
            allowed = causal(block)
        key_sum = [[None, None], [None, None]]
        value_sum = [[None, None], [None, None]]

        def add(sums, odd, kv, part):
            sums[odd][kv] = part if sums[odd][kv] is None else sums[odd][kv] + part

        for pair in range(PAIRS):
            which = (2 * pair // GROUP, (2 * pair + 1) // GROUP)
            lanes = slice(pair * PAIR, (pair + 1) * PAIR)
            queries = q_ref[0, :, lanes]
            grads = g_ref[0, :, lanes]
            both = dot(key_sides[which], queries, NT)
            both_grads = dot(value_sides[which], grads, NT)
            low_weights = []
            low_scores = []
            for odd in range(2):
                head = 2 * pair + odd
                part = slice(odd * block, (odd + 1) * block)
                weights = jnp.exp2(both[part] * scale - lse_ref[0, head : head + 1, :])
                if diagonal:
                    weights = jnp.where(allowed, weights, 0.0)
                change = weights * (both_grads[part] - delta[head : head + 1, :])
                low_weights.append(weights.astype(bf16))
                low_scores.append(change.astype(bf16))
                rows = slice(head * HEAD_DIM, (head + 1) * HEAD_DIM)
                acc_ref[rows, :] += dot(
                    keys_turned[which[odd] * HEAD_DIM : (which[odd] + 1) * HEAD_DIM],
                    low_scores[odd],
                    NN,
                )
            value_part = dot(jnp.concatenate(low_weights, axis=0), grads, NN)
            key_part = dot(jnp.concatenate(low_scores, axis=0), queries, NN)
            for odd in range(2):
                part = slice(odd * block, (odd + 1) * block)
                add(value_sum, odd, which[odd], value_part[part])
                add(key_sum, odd, which[odd], key_part[part])
        low = lax.broadcasted_iota(jnp.int32, (block, PAIR), 1) < HEAD_DIM
        for sums, out_ref in ((key_sum, dk_ref), (value_sum, dv_ref)):
            out_ref[index, :, :PAIR] += jnp.where(low, sums[0][0], sums[1][1])
            out_ref[index, :, PAIR:] += jnp.where(low, sums[0][1], sums[1][0])

    def body(index, carry):
        step(index, False)
        return carry

    lax.fori_loop(0, last, body, 0)
    step(last, True)
    for pair in range(PAIRS):
        straight = jnp.transpose(acc_ref[pair * PAIR : (pair + 1) * PAIR, :]) * score_scale
        dq_ref[0, :, pair * PAIR : (pair + 1) * PAIR] = turn_pair(
            straight, cos_ref[0], -sin_ref[0]
        ).astype(bf16)

    @pl.when(turn == 1)
    def _():
        for slot in range(2 * len(parts)):
            at = order_ref[slot]
            keys = dk_ref[at, :, :PAIR] + swap_pair(dk_ref[at, :, PAIR:])
            dkv_ref[0, slot, :, :K_WIDTH] = (keys * score_scale).astype(bf16)
            values = dv_ref[at, :, :PAIR] + swap_pair(dv_ref[at, :, PAIR:])
            dkv_ref[0, slot, :, K_WIDTH:] = values.astype(bf16)


def attention_specs(block, parts):
    def rows(width):
        return pl.BlockSpec((1, block, width), lambda i, order: (i, 0, 0))

    def halves(number):
        return pl.BlockSpec((1, number, block, 2 * K_WIDTH), lambda i, order: (i // 2, 0, 0, 0))

    stats = pl.BlockSpec((1, 16, block), lambda i, order: (i, 0, 0))
    return rows, halves, stats


def attend_forward(order, queries, parts):
    count, block, _ = queries.shape
    slots = 2 * len(parts)
    rows, halves, stats = attention_specs(block, parts)
    pairs_done = count * block * (slots // 2 + 1) * block * HEADS
    return pl.pallas_call(
        forward_kernel,
        grid_spec=pltpu.PrefetchScalarGridSpec(
            num_scalar_prefetch=1,
            grid=(count,),
            in_specs=[rows(Q_WIDTH)] + [halves(2)] * len(parts),
            out_specs=[rows(Q_WIDTH), stats],
            scratch_shapes=[
                pltpu.VMEM((slots, block, 2 * PAIR), bf16),
                pltpu.VMEM((slots, PAIR, block), bf16),
                pltpu.VMEM((16, block), f32),
                pltpu.VMEM((16, block), f32),
                pltpu.VMEM((Q_WIDTH, block), f32),
            ],
        ),
        out_shape=[
            jax.ShapeDtypeStruct((count, block, Q_WIDTH), bf16),
            jax.ShapeDtypeStruct((count, 16, block), f32),
        ],
        cost_estimate=pl.CostEstimate(
            flops=pairs_done * 4 * 256, bytes_accessed=4 << 20, transcendentals=pairs_done
        ),
        compiler_params=params(),
        name="attend_forward",
    )(order, queries, *parts)


def attend_backward(order, queries, parts, mixed, grads, stats_in, cosine, sine):
    count, block, _ = queries.shape
    slots = 2 * len(parts)
    rows, halves, stats = attention_specs(block, parts)
    pairs_done = count * block * (slots // 2 + 1) * block * HEADS
    return pl.pallas_call(
        backward_kernel,
        grid_spec=pltpu.PrefetchScalarGridSpec(
            num_scalar_prefetch=1,
            grid=(count,),
            in_specs=[
                rows(Q_WIDTH),
                rows(Q_WIDTH),
                rows(Q_WIDTH),
                stats,
                rows(PAIR),
                rows(PAIR),
            ]
            + [halves(2)] * len(parts),
            out_specs=[rows(Q_WIDTH), halves(slots)],
            scratch_shapes=[
                pltpu.VMEM((slots, block, 2 * PAIR), bf16),
                pltpu.VMEM((slots, block, 2 * PAIR), bf16),
                pltpu.VMEM((slots, PAIR, block), bf16),
                pltpu.VMEM((slots, block, 2 * PAIR), f32),
                pltpu.VMEM((slots, block, 2 * PAIR), f32),
                pltpu.VMEM((Q_WIDTH, block), f32),
            ],
        ),
        out_shape=[
            jax.ShapeDtypeStruct((count, block, Q_WIDTH), bf16),
            jax.ShapeDtypeStruct((count // 2, slots, block, 2 * K_WIDTH), bf16),
        ],
        cost_estimate=pl.CostEstimate(
            flops=pairs_done * 10 * 256, bytes_accessed=8 << 20, transcendentals=pairs_done
        ),
        compiler_params=params(),
        name="attend_backward",
    )(order, queries, mixed, grads, stats_in, cosine, sine, *parts)


def ffn_kernel(x_ref, c_ref, w_ref, *rest):
    out_ref, grad_ref, x_all, c_all, active_all, gate_all, up_all = rest[-7:]
    seq_size, _, depth, columns = w_ref.shape
    width = seq_size * depth
    x = x_ref[...]
    c = c_ref[...]
    x_all[0] = x
    c_all[0] = c
    gate_w = w_ref[:, 0].reshape(width, columns)
    up_w = w_ref[:, 1].reshape(width, columns)
    down_w = w_ref[:, 2].reshape(width, columns)
    gate = dot(x, gate_w, NN)
    up = dot(x, up_w, NN)
    grad_active = dot(c, down_w, NN)
    sigmoid = jax.nn.sigmoid(gate)
    silu = gate * sigmoid
    active = (silu * up).astype(bf16)
    grad_gate = (grad_active * up * sigmoid * (1.0 + gate * (1.0 - sigmoid))).astype(bf16)
    grad_up = (grad_active * silu).astype(bf16)
    active_all[0] = active
    gate_all[0] = grad_gate
    up_all[0] = grad_up
    grad_ref[...] = (dot(grad_gate, gate_w, NT) + dot(grad_up, up_w, NT)).astype(bf16)
    out_ref[...] = dot(active, down_w, NT).astype(bf16)


def ffn(number, count, x, c, weights, buffers):
    rows, width = x.shape
    columns = weights.shape[3]
    tile = rows // 2

    def slot(columns):
        return pl.BlockSpec((1, tile, columns), lambda i: (number, i, 0))

    wide = jax.ShapeDtypeStruct((count, rows, width), bf16)
    inner = jax.ShapeDtypeStruct((count, rows, columns), bf16)
    return pl.pallas_call(
        ffn_kernel,
        grid=(2,),
        in_specs=[row_spec(tile, width), row_spec(tile, width), full_spec(*weights.shape)]
        + [pl.BlockSpec(memory_space=pl.ANY)] * len(buffers),
        out_specs=[row_spec(tile, width), row_spec(tile, width)]
        + [slot(width)] * 2
        + [slot(columns)] * 3,
        out_shape=[jax.ShapeDtypeStruct((rows, width), bf16)] * 2 + [wide] * 2 + [inner] * 3,
        input_output_aliases={3 + i: 2 + i for i in range(len(buffers))},
        cost_estimate=pl.CostEstimate(
            flops=14 * rows * width * columns, bytes_accessed=16 << 20, transcendentals=0
        ),
        compiler_params=params(),
        name="ffn",
    )(x, c, weights, *buffers)


def ffn_weights_kernel(x_ref, c_ref, active_ref, gate_ref, up_ref, out_ref, acc_ref):
    step = pl.program_id(0)
    seq_size, _, depth, columns = out_ref.shape

    @pl.when(step == 0)
    def _():
        acc_ref[...] = jnp.zeros_like(acc_ref)

    x = x_ref[0]
    acc_ref[0] += dot(x, gate_ref[0], TN)
    acc_ref[1] += dot(x, up_ref[0], TN)
    acc_ref[2] += dot(c_ref[0], active_ref[0], TN)

    @pl.when(step == pl.num_programs(0) - 1)
    def _():
        for which in range(3):
            out_ref[:, which] = acc_ref[which].reshape(seq_size, depth, columns).astype(bf16)


def ffn_weights(seq_size, x, c, active, grad_gate, grad_up):
    count, rows, width = x.shape
    columns = active.shape[2]

    def slot(columns):
        return pl.BlockSpec((1, rows, columns), lambda i: (i, 0, 0))

    shape = (seq_size, 3, width // seq_size, columns)
    return pl.pallas_call(
        ffn_weights_kernel,
        grid=(count,),
        in_specs=[slot(width)] * 2 + [slot(columns)] * 3,
        out_specs=pl.BlockSpec(shape, lambda i: (0, 0, 0, 0)),
        out_shape=jax.ShapeDtypeStruct(shape, bf16),
        scratch_shapes=[pltpu.VMEM((3, width, columns), f32)],
        cost_estimate=pl.CostEstimate(
            flops=6 * count * rows * width * columns, bytes_accessed=30 << 20, transcendentals=0
        ),
        compiler_params=params(),
        name="ffn_weights",
    )(x, c, active, grad_gate, grad_up)


def hop(x, ctx_size, mask):
    return lax.ppermute(x, "ctx", [(i, i ^ mask) for i in range(ctx_size)])


def spread(x, ctx_size):
    if ctx_size != 4:
        return [x] + [hop(x, ctx_size, k) for k in range(1, ctx_size)]
    half = x.shape[0] // 2
    front, back = x[:half], x[half:]
    front_1 = hop(front, 4, 1)
    back_2 = hop(back, 4, 2)
    front_far = hop(jnp.concatenate([front, front_1], axis=0), 4, 2)
    back_far = hop(jnp.concatenate([back, back_2], axis=0), 4, 1)
    return [x, jnp.concatenate([front_1, back_2], axis=0), front_far, back_far]


def first_hops(parts, ctx_size):
    if ctx_size != 4:
        return [hop(parts[k], ctx_size, k) for k in range(1, ctx_size)]
    return [hop(parts[2], 4, 2), hop(parts[3], 4, 1)]


def gathered_sum(parts, got, ctx_size):
    if ctx_size != 4:
        total = parts[0].astype(f32)
        for part in got:
            total = total + part.astype(f32)
        return total
    own, near = parts[:2]
    front_got, back_got = got
    half = own.shape[0] // 2
    front_next = (near[:half].astype(f32) + front_got[half:].astype(f32)).astype(bf16)
    back_next = (near[half:].astype(f32) + back_got[half:].astype(f32)).astype(bf16)
    front_last = hop(front_next, 4, 1)
    back_last = hop(back_next, 4, 2)
    return jnp.concatenate(
        [
            own[:half].astype(f32) + front_got[:half].astype(f32) + front_last.astype(f32),
            own[half:].astype(f32) + back_got[:half].astype(f32) + back_last.astype(f32),
        ],
        axis=0,
    )


def pick(index, cases):
    return cases[0] if len(cases) == 1 else lax.select_n(index, *cases)


def on_device(
    seq_size,
    ctx_size,
    tokens,
    attention_gain,
    project_weight,
    project_bias,
    output_weight,
    feedforward_gain,
    gate_weight,
    up_weight,
    down_weight,
    cotangent,
):
    sequences, block_rows, width = tokens.shape
    place = lax.axis_index("ctx")
    half = block_rows // 2
    rows = sequences * block_rows
    fold = seq_size // ctx_size
    seq_place = lax.axis_index("seq")
    fold_place = seq_place % fold
    mirror = [(i, ctx_size - 1 - i) for i in range(ctx_size)]

    def crossed(x, j):
        return lax.ppermute(
            x,
            ("seq", "ctx"),
            [
                ((c * fold + r) * ctx_size + q, (q * fold + (r + j) % fold) * ctx_size + c)
                for c in range(ctx_size)
                for r in range(fold)
                for q in range(ctx_size)
            ],
        )

    def crossed_parts(parts):
        came = [
            crossed(pick(fold_place, [parts[(f + j) % fold] for f in range(fold)]), j)
            for j in range(fold)
        ]
        return [
            pick(fold_place, [came[(f - t) % fold] for f in range(fold)]) for t in range(fold)
        ]

    def zigzag(x):
        return jnp.concatenate([x[:, :half], lax.ppermute(x[:, half:], "ctx", mirror)], axis=1)

    owners = [place ^ k for k in range(ctx_size)]
    order = jnp.stack(
        [spot for owner in owners for spot in (2 * owner, 2 * (ctx_size - 1 - owner) + 1)]
    ).astype(jnp.int32)
    positions = (order[:2, None] * half + jnp.arange(half, dtype=jnp.int32)[None, :]).reshape(-1)
    cosine, sine = rotation_tables(jnp.tile(positions, sequences))

    gain_width = attention_gain.shape[0]
    bias_width = project_bias.shape[0]
    depth_mine, own_width = project_weight.shape
    vectors = jnp.concatenate([attention_gain, project_bias, feedforward_gain])
    both = jnp.concatenate([project_weight, output_weight], axis=1)
    spare = -vectors.shape[0] % both.shape[1]
    payload = jnp.concatenate(
        [both, jnp.pad(vectors, (0, spare)).reshape(-1, both.shape[1])], axis=0
    )
    pieces = [payload] + [hop(payload, ctx_size, k) for k in range(1, ctx_size)]
    ordered = [
        pick(place, [pieces[rank ^ p] for p in range(ctx_size)]) for rank in range(ctx_size)
    ]
    both_columns = jnp.concatenate(
        [piece[:depth_mine, :own_width] for piece in ordered]
        + [piece[:depth_mine, own_width:] for piece in ordered],
        axis=1,
    )
    vectors_all = [piece[depth_mine:].reshape(-1).astype(f32) for piece in ordered]

    def vector_whole(start, size):
        return jnp.concatenate([v[start : start + size] for v in vectors_all])[None, :]

    attention_full = vector_whole(0, gain_width)
    bias_full = vector_whole(gain_width, bias_width)
    feedforward_full = vector_whole(gain_width + bias_width, gain_width)
    both_full = lax.all_gather(both_columns, "seq", axis=0, tiled=True)
    output_full = both_full[:, Q_WIDTH + 2 * K_WIDTH :]

    tokens_late, down_late = lax.optimization_barrier((tokens, down_weight, both_columns))[:2]
    down_rows, down_columns = down_weight.shape
    depth = down_columns // fold
    down_turned = jnp.concatenate(
        crossed_parts(list(down_late.T.reshape(fold, depth, down_rows))), axis=1
    )
    weights_mine = lax.all_gather(
        jnp.stack([gate_weight, up_weight, down_turned]), "seq", axis=0
    )

    tokens_mine = zigzag(tokens_late).reshape(rows, width)
    normed, queries, pairs_mine = project_forward(
        tokens_mine, attention_full, both_full, bias_full, cosine, sine
    )
    queries = queries.reshape(sequences * 2, half, Q_WIDTH)
    pairs_mine = pairs_mine.reshape(sequences, 2, half, 2 * K_WIDTH)
    pair_parts = [pairs_mine] + [hop(pairs_mine, ctx_size, k) for k in range(1, ctx_size)]
    cotangent_late = lax.optimization_barrier((cotangent, pair_parts[-1]))[0]
    grad_low = zigzag(cotangent_late).reshape(rows, width)
    grad_parts = spread(grad_low, ctx_size)
    mixed, row_stats = attend_forward(order, queries, pair_parts)
    mixed_rows = mixed.reshape(rows, Q_WIDTH)
    hidden = tokens_mine.astype(f32) + dot(mixed_rows, output_full, NN)
    inverse_ffn = inverse_rms(hidden)
    normed_ffn = (hidden * inverse_ffn * feedforward_full).astype(bf16)

    normed_parts = spread(normed_ffn, ctx_size)
    output_parts = []
    grad_normed_parts = []
    buffers = []
    for number, (part, grad_part) in enumerate(zip(normed_parts, grad_parts)):
        output_part, grad_normed_part, *buffers = ffn(
            number, ctx_size, part, grad_part, weights_mine, buffers
        )
        output_parts.append(output_part)
        grad_normed_parts.append(grad_normed_part)
    ffn_grads, normed_got = lax.optimization_barrier(
        (ffn_weights(seq_size, *buffers), first_hops(grad_normed_parts, ctx_size))
    )
    grad_normed_ffn = gathered_sum(grad_normed_parts, normed_got, ctx_size)
    weight_grads = lax.psum_scatter(ffn_grads, "seq", scatter_dimension=0)

    grad_ffn_gain = jnp.sum(grad_normed_ffn * hidden * inverse_ffn, axis=0)
    weighted_ffn = grad_normed_ffn * feedforward_full
    grad_hidden = (
        grad_low.astype(f32)
        + inverse_ffn * weighted_ffn
        - hidden
        * inverse_ffn
        * inverse_ffn
        * inverse_ffn
        * jnp.mean(weighted_ffn * hidden, axis=-1, keepdims=True)
    )
    hidden_low = grad_hidden.astype(bf16)
    grad_mixed = dot(hidden_low, output_full, NT).astype(bf16)

    output_late = lax.optimization_barrier((output_parts, grad_mixed))[0]
    output_got = first_hops(output_late, ctx_size)

    grad_queries, pair_grads = attend_backward(
        order,
        queries,
        pair_parts,
        mixed,
        grad_mixed.reshape(sequences * 2, half, Q_WIDTH),
        row_stats,
        cosine.reshape(sequences * 2, half, PAIR),
        sine.reshape(sequences * 2, half, PAIR),
    )
    pair_grads, output_got = lax.optimization_barrier((pair_grads, output_got))
    pair_sums = [pair_grads[:, :2].reshape(rows, 2 * K_WIDTH)]
    for k in range(1, ctx_size):
        pair_sums.append(
            hop(pair_grads[:, 2 * k : 2 * k + 2], ctx_size, k).reshape(rows, 2 * K_WIDTH)
        )
    grad_queries = grad_queries.reshape(rows, Q_WIDTH)
    grad_pairs, tokens_grad, gain_sum, bias_sum = project_backward(
        grad_queries,
        both_full,
        tokens_mine,
        attention_full,
        grad_hidden,
        cosine,
        sine,
        pair_sums,
    )

    def owners_sum(parts):
        _, owners, deep, own = parts.shape
        parts = parts.reshape(ctx_size, owners // 2, 2, deep, own)
        core = seq_place % 2
        mine = pick(core, [parts[:, :, 0], parts[:, :, 1]])
        other = pick(core, [parts[:, :, 1], parts[:, :, 0]])
        swapped = lax.ppermute(other, "seq", [(i, i ^ 1) for i in range(seq_size)])
        chip = (mine.astype(f32) + swapped.astype(f32)).astype(bf16)

        def part(k):
            return lax.dynamic_index_in_dim(chip, place ^ k, 0, keepdims=False)

        total = part(0).astype(f32)
        for k in range(1, ctx_size):
            total = total + hop(part(k), ctx_size, k).astype(f32)
        column = total.astype(bf16)
        floor = seq_place // 2
        floors = seq_size // 2
        total = lax.dynamic_index_in_dim(column, floor, 0, keepdims=False).astype(f32)
        for step in range(1, floors):
            sent = lax.dynamic_index_in_dim(column, (floor + step) % floors, 0, keepdims=False)
            total = total + lax.ppermute(
                sent, "seq", [(i, (i + 2 * step) % seq_size) for i in range(seq_size)]
            ).astype(f32)
        return total

    output_out = owners_sum(weight_pieces(ctx_size, seq_size, mixed_rows, hidden_low))
    project_out = owners_sum(
        weight_pieces(ctx_size, seq_size, normed, grad_queries, grad_pairs)
    )

    tokens_grad = tokens_grad.reshape(tokens.shape)
    tokens_gradient = jnp.concatenate(
        [
            tokens_grad[:, :half],
            lax.ppermute(tokens_grad[:, half:].astype(bf16), "ctx", mirror).astype(f32),
        ],
        axis=1,
    )
    output_zigzag = hidden + gathered_sum(output_late, output_got, ctx_size)
    layer_output = zigzag(output_zigzag.astype(bf16).reshape(tokens.shape))

    down_grads = weight_grads[2].reshape(depth, fold, down_rows)
    down_out = jnp.concatenate(
        crossed_parts([down_grads[:, t] for t in range(fold)]), axis=0
    ).T

    sums = jnp.concatenate(
        [
            gain_sum.reshape(ctx_size, gain_width),
            bias_sum.reshape(ctx_size, bias_width),
            grad_ffn_gain.reshape(ctx_size, gain_width),
        ],
        axis=1,
    )

    def sums_for(k):
        return lax.dynamic_index_in_dim(sums, place ^ k, 0)

    vector_sum = sums_for(0)
    for k in range(1, ctx_size):
        vector_sum = vector_sum + hop(sums_for(k), ctx_size, k)
    mask = 1
    while mask < seq_size:
        vector_sum = vector_sum + lax.ppermute(
            vector_sum, "seq", [(i, i ^ mask) for i in range(seq_size)]
        )
        mask *= 2
    vector_sum = vector_sum[0]

    return (
        layer_output,
        tokens_gradient,
        vector_sum[:gain_width],
        project_out,
        vector_sum[gain_width : gain_width + bias_width],
        output_out,
        vector_sum[gain_width + bias_width :],
        weight_grads[0].astype(f32),
        weight_grads[1].astype(f32),
        down_out.astype(f32),
    )


def solution(mesh):
    matrix = P("seq", "ctx")
    vector = P("ctx")
    activation = P("seq", "ctx", None)

    def step(*arrays):
        return on_device(mesh.shape["seq"], mesh.shape["ctx"], *arrays)

    return jax.shard_map(
        step,
        mesh=mesh,
        in_specs=(
            activation,
            vector,
            matrix,
            vector,
            matrix,
            vector,
            matrix,
            matrix,
            matrix,
            activation,
        ),
        out_specs=(
            activation,
            activation,
            vector,
            matrix,
            vector,
            matrix,
            vector,
            matrix,
            matrix,
            matrix,
        ),
        check_vma=False,
    )
```

```python
import math
import jax
import jax.numpy as jnp
from jax import lax
from jax.experimental import pallas as pl
from jax.experimental.pallas import tpu as pltpu
from jax.sharding import PartitionSpec as P

HEADS = 14
KV_HEADS = 2
HEAD_DIM = 64
GROUP = HEADS // KV_HEADS
PAIRS = HEADS // 2
PAIR = 2 * HEAD_DIM
Q_WIDTH = HEADS * HEAD_DIM
K_WIDTH = KV_HEADS * HEAD_DIM

norm_eps = 1e-06
rope_base = 1000000.0
masked_value = -1e30
score_scale = HEAD_DIM ** (-0.5)
log2_e = math.log2(math.e)
bf16 = jnp.bfloat16
f32 = jnp.float32


def inverse_rms(tensor):
    return lax.rsqrt(jnp.mean(tensor * tensor, axis=-1, keepdims=True) + norm_eps)


def dot(a, b, dims):
    return lax.dot_general(a, b, (dims, ((), ())), preferred_element_type=f32)


NN = ((1,), (0,))
NT = ((1,), (1,))
TN = ((0,), (0,))


def rotation_tables(positions):
    half_width = HEAD_DIM // 2
    steps_up = jnp.arange(half_width).astype(f32)
    frequency = jnp.power(jnp.asarray(rope_base, f32), -2.0 * steps_up / HEAD_DIM)
    angles = positions.astype(f32)[:, None] * frequency[None, :]
    cosine = jnp.cos(angles)
    sine = jnp.sin(angles)
    return (
        jnp.concatenate([cosine, cosine, cosine, cosine], axis=-1),
        jnp.concatenate([-sine, sine, -sine, sine], axis=-1),
    )


def turn_pair(x, cosine, sine):
    lane = lax.broadcasted_iota(jnp.int32, x.shape, 1)
    quarter = HEAD_DIM // 2
    other = jnp.where(
        (lane // quarter) % 2 == 0,
        pltpu.roll(x, PAIR - quarter, 1),
        pltpu.roll(x, quarter, 1),
    )
    return x * cosine + other * sine


def swap_pair(x):
    return pltpu.roll(x.astype(f32), HEAD_DIM, 1)


def params():
    return pltpu.CompilerParams(vmem_limit_bytes=60 << 20)


def project_kernel(x_ref, gain_ref, w_ref, bias_ref, cos_ref, sin_ref, normed_ref, q_ref, kv_ref):
    x = x_ref[...].astype(f32)
    normed = (x * inverse_rms(x) * gain_ref[...]).astype(bf16)
    normed_ref[...] = normed
    projected = dot(normed, w_ref[...], NN) + bias_ref[...]
    cosine = cos_ref[...]
    sine = sin_ref[...]
    for pair in range(PAIRS + 1):
        lanes = slice(pair * PAIR, (pair + 1) * PAIR)
        turned = turn_pair(projected[:, lanes], cosine, sine).astype(bf16)
        if pair < PAIRS:
            q_ref[:, lanes] = turned
        else:
            kv_ref[:, :K_WIDTH] = turned
    kv_ref[:, K_WIDTH:] = projected[:, Q_WIDTH + K_WIDTH :].astype(bf16)


def row_spec(tile, width):
    return pl.BlockSpec((tile, width), lambda i: (i, 0))


def full_spec(*shape):
    return pl.BlockSpec(shape, lambda i: (0,) * len(shape))


def project_forward(tokens, gain, weight, bias, cosine, sine):
    rows, width = tokens.shape
    tile = rows // 2
    columns = Q_WIDTH + 2 * K_WIDTH
    return pl.pallas_call(
        project_kernel,
        grid=(2,),
        in_specs=[
            row_spec(tile, width),
            full_spec(1, width),
            full_spec(width, columns),
            full_spec(1, columns),
            row_spec(tile, PAIR),
            row_spec(tile, PAIR),
        ],
        out_specs=[row_spec(tile, width), row_spec(tile, Q_WIDTH), row_spec(tile, 2 * K_WIDTH)],
        out_shape=[
            jax.ShapeDtypeStruct((rows, width), bf16),
            jax.ShapeDtypeStruct((rows, Q_WIDTH), bf16),
            jax.ShapeDtypeStruct((rows, 2 * K_WIDTH), bf16),
        ],
        cost_estimate=pl.CostEstimate(
            flops=4 * rows * width * columns, bytes_accessed=5 << 20, transcendentals=0
        ),
        compiler_params=params(),
        name="project_forward",
    )(tokens, gain, weight, bias, cosine, sine)


def project_back_kernel(
    gq_ref, w_ref, x_ref, gain_ref, hidden_ref, cos_ref, sin_ref, *rest
):
    parts = rest[:-4]
    gkv_ref, tokens_ref, gain_sum_ref, bias_sum_ref = rest[-4:]
    total = parts[0][...].astype(f32)
    for part in parts[1:]:
        total = total + part[...].astype(f32)
    turned = turn_pair(total[:, :K_WIDTH], cos_ref[...], -sin_ref[...]).astype(bf16)
    gkv_ref[:, :K_WIDTH] = turned
    gkv_ref[:, K_WIDTH:] = total[:, K_WIDTH:].astype(bf16)
    grads = jnp.concatenate([gq_ref[...], gkv_ref[...]], axis=1)
    grad_normed = dot(grads, w_ref[...], NT)
    x = x_ref[...].astype(f32)
    inverse = inverse_rms(x)
    weighted = grad_normed * gain_ref[...]
    tokens_ref[...] = (
        hidden_ref[...]
        + inverse * weighted
        - x * (inverse * inverse * inverse * jnp.mean(weighted * x, axis=-1, keepdims=True))
    )

    @pl.when(pl.program_id(0) == 0)
    def _():
        gain_sum_ref[...] = jnp.zeros_like(gain_sum_ref)
        bias_sum_ref[...] = jnp.zeros_like(bias_sum_ref)

    gain_sum_ref[...] += jnp.sum(grad_normed * x * inverse, axis=0, keepdims=True)
    bias_sum_ref[...] += jnp.sum(grads.astype(f32), axis=0, keepdims=True)


def project_backward(grad_queries, weight, tokens, gain, grad_hidden, cosine, sine, parts):
    rows, width = tokens.shape
    tile = rows // 2
    columns = Q_WIDTH + 2 * K_WIDTH
    return pl.pallas_call(
        project_back_kernel,
        grid=(2,),
        in_specs=[
            row_spec(tile, Q_WIDTH),
            full_spec(width, columns),
            row_spec(tile, width),
            full_spec(1, width),
            row_spec(tile, width),
            row_spec(tile, PAIR),
            row_spec(tile, PAIR),
        ]
        + [row_spec(tile, 2 * K_WIDTH)] * len(parts),
        out_specs=[
            row_spec(tile, 2 * K_WIDTH),
            row_spec(tile, width),
            full_spec(1, width),
            full_spec(1, columns),
        ],
        out_shape=[
            jax.ShapeDtypeStruct((rows, 2 * K_WIDTH), bf16),
            jax.ShapeDtypeStruct((rows, width), f32),
            jax.ShapeDtypeStruct((1, width), f32),
            jax.ShapeDtypeStruct((1, columns), f32),
        ],
        cost_estimate=pl.CostEstimate(
            flops=4 * rows * width * columns, bytes_accessed=8 << 20, transcendentals=0
        ),
        compiler_params=params(),
        name="project_backward",
    )(grad_queries, weight, tokens, gain, grad_hidden, cosine, sine, *parts)


def pieces_kernel(core_ref, lhs_ref, *rest):
    rhs_refs = rest[:-2]
    mine_ref, other_ref = rest[-2:]
    ranks, floors, depth, own = mine_ref.shape
    rhs = jnp.concatenate([ref[...] for ref in rhs_refs], axis=1)
    whole = dot(lhs_ref[...], rhs, TN)
    first = core_ref[0] == 0
    for rank in range(ranks):
        part = whole[:, rank * own : (rank + 1) * own].reshape(floors, 2, depth, own)
        mine_ref[rank] = jnp.where(first, part[:, 0], part[:, 1]).astype(bf16)
        other_ref[rank] = jnp.where(first, part[:, 1], part[:, 0]).astype(bf16)


def weight_pieces(core, ctx_size, seq_size, lhs, *rhs):
    rows, width = lhs.shape
    columns = sum(x.shape[1] for x in rhs)
    shape = (ctx_size, seq_size // 2, width // seq_size, columns // ctx_size)

    def full(*shape):
        return pl.BlockSpec(shape, lambda i, core: (0,) * len(shape))

    return pl.pallas_call(
        pieces_kernel,
        grid_spec=pltpu.PrefetchScalarGridSpec(
            num_scalar_prefetch=1,
            grid=(1,),
            in_specs=[full(*x.shape) for x in (lhs, *rhs)],
            out_specs=[full(*shape)] * 2,
        ),
        out_shape=[jax.ShapeDtypeStruct(shape, bf16)] * 2,
        cost_estimate=pl.CostEstimate(
            flops=4 * rows * width * columns, bytes_accessed=5 << 20, transcendentals=0
        ),
        compiler_params=params(),
        name="weight_pieces",
    )(core.astype(jnp.int32)[None], lhs, *rhs)


def pair_sides(both):
    x, x_swapped = both[:, :PAIR], both[:, PAIR:]
    low = lax.broadcasted_iota(jnp.int32, x.shape, 1) < HEAD_DIM
    zero = jnp.zeros_like(x)
    left = (jnp.where(low, x, zero), jnp.where(low, x_swapped, zero))
    right = (jnp.where(low, zero, x_swapped), jnp.where(low, zero, x))
    sides = {}
    for pair in range(PAIRS):
        key = (2 * pair // GROUP, (2 * pair + 1) // GROUP)
        if key not in sides:
            sides[key] = jnp.concatenate([left[key[0]], right[key[1]]], axis=0)
    return sides


def causal(block):
    key_at = lax.broadcasted_iota(jnp.int32, (block, block), 0)
    query_at = lax.broadcasted_iota(jnp.int32, (block, block), 1)
    return key_at <= query_at


def forward_kernel(order_ref, q_ref, *rest):
    parts = rest[:-7]
    o_ref, lse_ref, keys_ref, turned_ref, top_ref, total_ref, acc_ref = rest[-7:]
    block = q_ref.shape[1]
    turn = pl.program_id(0) % 2
    last = order_ref[turn]

    @pl.when(turn == 0)
    def _():
        for number, part in enumerate(parts):
            for half in range(2):
                at = order_ref[2 * number + half]
                keys = part[0, half, :, :K_WIDTH]
                keys_ref[at, :, :PAIR] = keys
                keys_ref[at, :, PAIR:] = swap_pair(keys).astype(bf16)
                turned_ref[at] = jnp.transpose(part[0, half, :, K_WIDTH:].astype(f32)).astype(
                    bf16
                )

    top_ref[...] = jnp.full_like(top_ref, masked_value)
    total_ref[...] = jnp.zeros_like(total_ref)
    acc_ref[...] = jnp.zeros_like(acc_ref)
    scale = score_scale * log2_e

    def step(index, diagonal):
        sides = pair_sides(keys_ref[index])
        values = turned_ref[index]
        if diagonal:
            allowed = causal(block)
        for pair in range(PAIRS):
            both = dot(
                sides[(2 * pair // GROUP, (2 * pair + 1) // GROUP)],
                q_ref[0, :, pair * PAIR : (pair + 1) * PAIR],
                NT,
            )
            for odd in range(2):
                head = 2 * pair + odd
                kv = head // GROUP
                scores = both[odd * block : (odd + 1) * block] * scale
                if diagonal:
                    scores = jnp.where(allowed, scores, masked_value)
                old = top_ref[head : head + 1, :]
                new = jnp.maximum(old, jnp.max(scores, axis=0, keepdims=True))
                shrink = jnp.exp2(old - new)
                weights = jnp.exp2(scores - new)
                top_ref[head : head + 1, :] = new
                total_ref[head : head + 1, :] = total_ref[
                    head : head + 1, :
                ] * shrink + jnp.sum(weights, axis=0, keepdims=True)
                rows = slice(head * HEAD_DIM, (head + 1) * HEAD_DIM)
                acc_ref[rows, :] = acc_ref[rows, :] * shrink + dot(
                    values[kv * HEAD_DIM : (kv + 1) * HEAD_DIM], weights.astype(bf16), NN
                )

    def body(index, carry):
        step(index, False)
        return carry

    lax.fori_loop(0, last, body, 0)
    step(last, True)
    for pair in range(PAIRS):
        halves = []
        for odd in range(2):
            head = 2 * pair + odd
            halves.append(
                acc_ref[head * HEAD_DIM : (head + 1) * HEAD_DIM, :]
                / total_ref[head : head + 1, :]
            )
        o_ref[0, :, pair * PAIR : (pair + 1) * PAIR] = jnp.transpose(
            jnp.concatenate(halves, axis=0)
        ).astype(bf16)
    lse_ref[0] = top_ref[...] + jnp.log2(total_ref[...])


def backward_kernel(order_ref, q_ref, o_ref, g_ref, lse_ref, cos_ref, sin_ref, *rest):
    parts = rest[:-8]
    dq_ref, dkv_ref, keys_ref, values_ref, turned_ref, dk_ref, dv_ref, acc_ref = rest[-8:]
    block = q_ref.shape[1]
    turn = pl.program_id(0) % 2
    last = order_ref[turn]
    scale = score_scale * log2_e

    @pl.when(turn == 0)
    def _():
        dk_ref[...] = jnp.zeros_like(dk_ref)
        dv_ref[...] = jnp.zeros_like(dv_ref)
        for number, part in enumerate(parts):
            for half in range(2):
                at = order_ref[2 * number + half]
                keys = part[0, half, :, :K_WIDTH]
                values = part[0, half, :, K_WIDTH:]
                keys_ref[at, :, :PAIR] = keys
                keys_ref[at, :, PAIR:] = swap_pair(keys).astype(bf16)
                values_ref[at, :, :PAIR] = values
                values_ref[at, :, PAIR:] = swap_pair(values).astype(bf16)
                turned_ref[at] = jnp.transpose(keys.astype(f32)).astype(bf16)

    acc_ref[...] = jnp.zeros_like(acc_ref)
    product = g_ref[0].astype(f32) * o_ref[0].astype(f32)
    coarse = product.astype(bf16)
    fine = (product - coarse.astype(f32)).astype(bf16)
    head_of = lax.broadcasted_iota(jnp.int32, (16, Q_WIDTH), 1) // HEAD_DIM
    picks = (head_of == lax.broadcasted_iota(jnp.int32, (16, Q_WIDTH), 0)).astype(bf16)
    delta = dot(picks, coarse, NT) + dot(picks, fine, NT)

    def step(index, diagonal):
        key_sides = pair_sides(keys_ref[index])
        value_sides = pair_sides(values_ref[index])
        keys_turned = turned_ref[index]
        if diagonal:
            allowed = causal(block)
        key_sum = [[None, None], [None, None]]
        value_sum = [[None, None], [None, None]]

        def add(sums, odd, kv, part):
            sums[odd][kv] = part if sums[odd][kv] is None else sums[odd][kv] + part

        for pair in range(PAIRS):
            which = (2 * pair // GROUP, (2 * pair + 1) // GROUP)
            lanes = slice(pair * PAIR, (pair + 1) * PAIR)
            queries = q_ref[0, :, lanes]
            grads = g_ref[0, :, lanes]
            both = dot(key_sides[which], queries, NT)
            both_grads = dot(value_sides[which], grads, NT)
            low_weights = []
            low_scores = []
            for odd in range(2):
                head = 2 * pair + odd
                part = slice(odd * block, (odd + 1) * block)
                weights = jnp.exp2(both[part] * scale - lse_ref[0, head : head + 1, :])
                if diagonal:
                    weights = jnp.where(allowed, weights, 0.0)
                change = weights * (both_grads[part] - delta[head : head + 1, :])
                low_weights.append(weights.astype(bf16))
                low_scores.append(change.astype(bf16))
                rows = slice(head * HEAD_DIM, (head + 1) * HEAD_DIM)
                acc_ref[rows, :] += dot(
                    keys_turned[which[odd] * HEAD_DIM : (which[odd] + 1) * HEAD_DIM],
                    low_scores[odd],
                    NN,
                )
            value_part = dot(jnp.concatenate(low_weights, axis=0), grads, NN)
            key_part = dot(jnp.concatenate(low_scores, axis=0), queries, NN)
            for odd in range(2):
                part = slice(odd * block, (odd + 1) * block)
                add(value_sum, odd, which[odd], value_part[part])
                add(key_sum, odd, which[odd], key_part[part])
        low = lax.broadcasted_iota(jnp.int32, (block, PAIR), 1) < HEAD_DIM
        for sums, out_ref in ((key_sum, dk_ref), (value_sum, dv_ref)):
            out_ref[index, :, :PAIR] += jnp.where(low, sums[0][0], sums[1][1])
            out_ref[index, :, PAIR:] += jnp.where(low, sums[0][1], sums[1][0])

    def body(index, carry):
        step(index, False)
        return carry

    lax.fori_loop(0, last, body, 0)
    step(last, True)
    for pair in range(PAIRS):
        straight = jnp.transpose(acc_ref[pair * PAIR : (pair + 1) * PAIR, :]) * score_scale
        dq_ref[0, :, pair * PAIR : (pair + 1) * PAIR] = turn_pair(
            straight, cos_ref[0], -sin_ref[0]
        ).astype(bf16)

    @pl.when(turn == 1)
    def _():
        for slot in range(2 * len(parts)):
            at = order_ref[slot]
            keys = dk_ref[at, :, :PAIR] + swap_pair(dk_ref[at, :, PAIR:])
            dkv_ref[0, slot, :, :K_WIDTH] = (keys * score_scale).astype(bf16)
            values = dv_ref[at, :, :PAIR] + swap_pair(dv_ref[at, :, PAIR:])
            dkv_ref[0, slot, :, K_WIDTH:] = values.astype(bf16)


def attention_specs(block, parts):
    def rows(width):
        return pl.BlockSpec((1, block, width), lambda i, order: (i, 0, 0))

    def halves(number):
        return pl.BlockSpec((1, number, block, 2 * K_WIDTH), lambda i, order: (i // 2, 0, 0, 0))

    stats = pl.BlockSpec((1, 16, block), lambda i, order: (i, 0, 0))
    return rows, halves, stats


def attend_forward(order, queries, parts):
    count, block, _ = queries.shape
    slots = 2 * len(parts)
    rows, halves, stats = attention_specs(block, parts)
    pairs_done = count * block * (slots // 2 + 1) * block * HEADS
    return pl.pallas_call(
        forward_kernel,
        grid_spec=pltpu.PrefetchScalarGridSpec(
            num_scalar_prefetch=1,
            grid=(count,),
            in_specs=[rows(Q_WIDTH)] + [halves(2)] * len(parts),
            out_specs=[rows(Q_WIDTH), stats],
            scratch_shapes=[
                pltpu.VMEM((slots, block, 2 * PAIR), bf16),
                pltpu.VMEM((slots, PAIR, block), bf16),
                pltpu.VMEM((16, block), f32),
                pltpu.VMEM((16, block), f32),
                pltpu.VMEM((Q_WIDTH, block), f32),
            ],
        ),
        out_shape=[
            jax.ShapeDtypeStruct((count, block, Q_WIDTH), bf16),
            jax.ShapeDtypeStruct((count, 16, block), f32),
        ],
        cost_estimate=pl.CostEstimate(
            flops=pairs_done * 4 * 256, bytes_accessed=4 << 20, transcendentals=pairs_done
        ),
        compiler_params=params(),
        name="attend_forward",
    )(order, queries, *parts)


def attend_backward(order, queries, parts, mixed, grads, stats_in, cosine, sine):
    count, block, _ = queries.shape
    slots = 2 * len(parts)
    rows, halves, stats = attention_specs(block, parts)
    pairs_done = count * block * (slots // 2 + 1) * block * HEADS
    return pl.pallas_call(
        backward_kernel,
        grid_spec=pltpu.PrefetchScalarGridSpec(
            num_scalar_prefetch=1,
            grid=(count,),
            in_specs=[
                rows(Q_WIDTH),
                rows(Q_WIDTH),
                rows(Q_WIDTH),
                stats,
                rows(PAIR),
                rows(PAIR),
            ]
            + [halves(2)] * len(parts),
            out_specs=[rows(Q_WIDTH), halves(slots)],
            scratch_shapes=[
                pltpu.VMEM((slots, block, 2 * PAIR), bf16),
                pltpu.VMEM((slots, block, 2 * PAIR), bf16),
                pltpu.VMEM((slots, PAIR, block), bf16),
                pltpu.VMEM((slots, block, 2 * PAIR), f32),
                pltpu.VMEM((slots, block, 2 * PAIR), f32),
                pltpu.VMEM((Q_WIDTH, block), f32),
            ],
        ),
        out_shape=[
            jax.ShapeDtypeStruct((count, block, Q_WIDTH), bf16),
            jax.ShapeDtypeStruct((count // 2, slots, block, 2 * K_WIDTH), bf16),
        ],
        cost_estimate=pl.CostEstimate(
            flops=pairs_done * 10 * 256, bytes_accessed=8 << 20, transcendentals=pairs_done
        ),
        compiler_params=params(),
        name="attend_backward",
    )(order, queries, mixed, grads, stats_in, cosine, sine, *parts)


def ffn_kernel(x_ref, c_ref, w_ref, d_ref, *rest):
    out_ref, grad_ref, x_all, c_all, active_all, gate_all, up_all = rest[-7:]
    seq_size, _, depth, columns = w_ref.shape
    width = seq_size * depth
    x = x_ref[...]
    c = c_ref[...]
    x_all[0] = x
    c_all[0] = c
    gate_w = w_ref[:, 0].reshape(width, columns)
    up_w = w_ref[:, 1].reshape(width, columns)
    down_w = d_ref[...].reshape(width, columns)
    gate = dot(x, gate_w, NN)
    up = dot(x, up_w, NN)
    grad_active = dot(c, down_w, NN)
    sigmoid = jax.nn.sigmoid(gate)
    silu = gate * sigmoid
    active = (silu * up).astype(bf16)
    grad_gate = (grad_active * up * sigmoid * (1.0 + gate * (1.0 - sigmoid))).astype(bf16)
    grad_up = (grad_active * silu).astype(bf16)
    active_all[0] = active
    gate_all[0] = grad_gate
    up_all[0] = grad_up
    grad_ref[...] = (dot(grad_gate, gate_w, NT) + dot(grad_up, up_w, NT)).astype(bf16)
    out_ref[...] = dot(active, down_w, NT).astype(bf16)


def ffn(number, count, x, c, weights, down, buffers):
    rows, width = x.shape
    columns = weights.shape[3]
    tile = rows // 2

    def slot(columns):
        return pl.BlockSpec((1, tile, columns), lambda i: (number, i, 0))

    wide = jax.ShapeDtypeStruct((count, rows, width), bf16)
    inner = jax.ShapeDtypeStruct((count, rows, columns), bf16)
    return pl.pallas_call(
        ffn_kernel,
        grid=(2,),
        in_specs=[
            row_spec(tile, width),
            row_spec(tile, width),
            full_spec(*weights.shape),
            full_spec(*down.shape),
        ]
        + [pl.BlockSpec(memory_space=pl.ANY)] * len(buffers),
        out_specs=[row_spec(tile, width), row_spec(tile, width)]
        + [slot(width)] * 2
        + [slot(columns)] * 3,
        out_shape=[jax.ShapeDtypeStruct((rows, width), bf16)] * 2 + [wide] * 2 + [inner] * 3,
        input_output_aliases={4 + i: 2 + i for i in range(len(buffers))},
        cost_estimate=pl.CostEstimate(
            flops=14 * rows * width * columns, bytes_accessed=16 << 20, transcendentals=0
        ),
        compiler_params=params(),
        name="ffn",
    )(x, c, weights, down, *buffers)


def ffn_weights_kernel(x_ref, c_ref, active_ref, gate_ref, up_ref, out_ref, acc_ref):
    step = pl.program_id(0)
    seq_size, _, depth, columns = out_ref.shape

    @pl.when(step == 0)
    def _():
        acc_ref[...] = jnp.zeros_like(acc_ref)

    x = x_ref[0]
    acc_ref[0] += dot(x, gate_ref[0], TN)
    acc_ref[1] += dot(x, up_ref[0], TN)
    acc_ref[2] += dot(c_ref[0], active_ref[0], TN)

    @pl.when(step == pl.num_programs(0) - 1)
    def _():
        for which in range(3):
            out_ref[:, which] = acc_ref[which].reshape(seq_size, depth, columns).astype(bf16)


def ffn_weights(seq_size, x, c, active, grad_gate, grad_up):
    count, rows, width = x.shape
    columns = active.shape[2]

    def slot(columns):
        return pl.BlockSpec((1, rows, columns), lambda i: (i, 0, 0))

    shape = (seq_size, 3, width // seq_size, columns)
    return pl.pallas_call(
        ffn_weights_kernel,
        grid=(count,),
        in_specs=[slot(width)] * 2 + [slot(columns)] * 3,
        out_specs=pl.BlockSpec(shape, lambda i: (0, 0, 0, 0)),
        out_shape=jax.ShapeDtypeStruct(shape, bf16),
        scratch_shapes=[pltpu.VMEM((3, width, columns), f32)],
        cost_estimate=pl.CostEstimate(
            flops=6 * count * rows * width * columns, bytes_accessed=30 << 20, transcendentals=0
        ),
        compiler_params=params(),
        name="ffn_weights",
    )(x, c, active, grad_gate, grad_up)


def hop(x, ctx_size, mask):
    return lax.ppermute(x, "ctx", [(i, i ^ mask) for i in range(ctx_size)])


def spread_near(x, ctx_size):
    if ctx_size != 4:
        return [hop(x, ctx_size, k) for k in range(1, ctx_size)]
    half = x.shape[0] // 2
    return [hop(x[:half], 4, 1), hop(x[half:], 4, 2)]


def spread_far(x, near, ctx_size):
    if ctx_size != 4:
        return []
    half = x.shape[0] // 2
    return [
        hop(jnp.concatenate([x[:half], near[0]], axis=0), 4, 2),
        hop(jnp.concatenate([x[half:], near[1]], axis=0), 4, 1),
    ]


def spread_parts(x, near, far, ctx_size):
    return [x, *near] if ctx_size != 4 else [x, jnp.concatenate(near, axis=0), *far]


def first_hops(parts, ctx_size):
    if ctx_size != 4:
        return [hop(parts[k], ctx_size, k) for k in range(1, ctx_size)]
    return [hop(parts[2], 4, 2), hop(parts[3], 4, 1)]


def gathered_sum(parts, got, ctx_size):
    if ctx_size != 4:
        total = parts[0].astype(f32)
        for part in got:
            total = total + part.astype(f32)
        return total
    own, near = parts[:2]
    front_got, back_got = got
    half = own.shape[0] // 2
    front_next = (near[:half].astype(f32) + front_got[half:].astype(f32)).astype(bf16)
    back_next = (near[half:].astype(f32) + back_got[half:].astype(f32)).astype(bf16)
    front_last = hop(front_next, 4, 1)
    back_last = hop(back_next, 4, 2)
    return jnp.concatenate(
        [
            own[:half].astype(f32) + front_got[:half].astype(f32) + front_last.astype(f32),
            own[half:].astype(f32) + back_got[:half].astype(f32) + back_last.astype(f32),
        ],
        axis=0,
    )


def pick(index, cases):
    return cases[0] if len(cases) == 1 else lax.select_n(index, *cases)


def on_device(
    seq_size,
    ctx_size,
    tokens,
    attention_gain,
    project_weight,
    project_bias,
    output_weight,
    feedforward_gain,
    gate_weight,
    up_weight,
    down_weight,
    cotangent,
):
    sequences, block_rows, width = tokens.shape
    place = lax.axis_index("ctx")
    half = block_rows // 2
    rows = sequences * block_rows
    fold = seq_size // ctx_size
    seq_place = lax.axis_index("seq")
    fold_place = seq_place % fold
    core = seq_place % 2
    floor = seq_place // 2
    floors = seq_size // 2
    mirror = [(i, ctx_size - 1 - i) for i in range(ctx_size)]

    def crossed(x, j):
        return lax.ppermute(
            x,
            ("seq", "ctx"),
            [
                ((c * fold + r) * ctx_size + q, (q * fold + (r + j) % fold) * ctx_size + c)
                for c in range(ctx_size)
                for r in range(fold)
                for q in range(ctx_size)
            ],
        )

    def crossed_parts(parts):
        came = [
            crossed(pick(fold_place, [parts[(f + j) % fold] for f in range(fold)]), j)
            for j in range(fold)
        ]
        return [
            pick(fold_place, [came[(f - t) % fold] for f in range(fold)]) for t in range(fold)
        ]

    def zigzag(x):
        return jnp.concatenate([x[:, :half], lax.ppermute(x[:, half:], "ctx", mirror)], axis=1)

    owners = [place ^ k for k in range(ctx_size)]
    order = jnp.stack(
        [spot for owner in owners for spot in (2 * owner, 2 * (ctx_size - 1 - owner) + 1)]
    ).astype(jnp.int32)
    positions = (order[:2, None] * half + jnp.arange(half, dtype=jnp.int32)[None, :]).reshape(-1)
    cosine, sine = rotation_tables(jnp.tile(positions, sequences))

    def from_floors(x):
        came = [x] + [
            lax.ppermute(x, "seq", [(i, (i + 2 * step) % seq_size) for i in range(seq_size)])
            for step in range(1, floors)
        ]
        return jnp.concatenate(
            [
                pick(floor, [came[(mine - theirs) % floors] for mine in range(floors)])
                for theirs in range(floors)
            ],
            axis=0,
        )

    def from_ranks(x):
        return [x] + [hop(x, ctx_size, k) for k in range(1, ctx_size)]

    def by_rank(came):
        return [pick(place, [came[rank ^ p] for p in range(ctx_size)]) for rank in range(ctx_size)]

    def from_other_core(x):
        return lax.ppermute(x, "seq", [(i, i ^ 1) for i in range(seq_size)])

    def by_core(x, other):
        first, second = pick(core, [x, other]), pick(core, [other, x])
        shape = (floors, x.shape[0] // floors, x.shape[1])
        return jnp.stack([first.reshape(shape), second.reshape(shape)], axis=1).reshape(
            2 * x.shape[0], x.shape[1]
        )

    gate_up = lax.all_gather(jnp.stack([gate_weight, up_weight]), "seq", axis=0)
    gain_width = attention_gain.shape[0]
    own_width = project_weight.shape[1]
    vectors = jnp.concatenate([attention_gain, project_bias, feedforward_gain])
    spare = -vectors.shape[0] % own_width
    project_rows = from_floors(project_weight)
    held = project_rows.shape[0]
    tokens_mine = zigzag(tokens).reshape(rows, width)
    project_rows, tokens_mine = lax.optimization_barrier((project_rows, tokens_mine))
    project_came = from_ranks(
        jnp.concatenate(
            [project_rows, jnp.pad(vectors, (0, spare)).reshape(-1, own_width)], axis=0
        )
    )
    output_late = lax.optimization_barrier((output_weight, project_rows))[0]
    output_rows = from_floors(output_late)
    ordered = by_rank(project_came)
    vectors_all = [piece[held:].reshape(-1).astype(f32) for piece in ordered]

    def vector_whole(start, size):
        return jnp.concatenate([v[start : start + size] for v in vectors_all])[None, :]

    attention_full = vector_whole(0, gain_width)
    bias_full = vector_whole(gain_width, own_width)
    feedforward_full = vector_whole(gain_width + own_width, gain_width)
    project_columns = jnp.concatenate([piece[:held] for piece in ordered], axis=1)
    project_full = by_core(project_columns, from_other_core(project_columns))

    down_late, grad_late = lax.optimization_barrier((down_weight, cotangent, project_columns))[:2]
    grad_low = zigzag(grad_late).reshape(rows, width)
    grad_near = spread_near(grad_low, ctx_size)
    down_rows, down_columns = down_weight.shape
    depth = down_columns // fold
    down_turned = jnp.concatenate(
        crossed_parts(list(down_late.T.reshape(fold, depth, down_rows))), axis=1
    )
    normed, queries, pairs_mine = project_forward(
        tokens_mine, attention_full, project_full, bias_full, cosine, sine
    )
    down_turned, gate_up = lax.optimization_barrier((down_turned, gate_up, queries))[:2]
    down_mine = lax.all_gather(down_turned, "seq", axis=0)
    queries = queries.reshape(sequences * 2, half, Q_WIDTH)
    pairs_mine = pairs_mine.reshape(sequences, 2, half, 2 * K_WIDTH)
    pair_parts = [pairs_mine] + [hop(pairs_mine, ctx_size, k) for k in range(1, ctx_size)]
    grad_near, output_rows = lax.optimization_barrier((grad_near, output_rows, pair_parts))[:2]
    grad_far = spread_far(grad_low, grad_near, ctx_size)
    output_came = from_ranks(output_rows)
    queries = lax.optimization_barrier((queries, down_turned))[0]
    mixed, row_stats = attend_forward(order, queries, pair_parts)
    mixed, grad_far, output_came = lax.optimization_barrier((mixed, grad_far, output_came))
    grad_parts = spread_parts(grad_low, grad_near, grad_far, ctx_size)
    output_columns = jnp.concatenate(by_rank(output_came), axis=1)
    output_full = by_core(output_columns, from_other_core(output_columns))
    mixed_rows = mixed.reshape(rows, Q_WIDTH)
    hidden = tokens_mine.astype(f32) + dot(mixed_rows, output_full, NN)
    inverse_ffn = inverse_rms(hidden)
    normed_ffn = (hidden * inverse_ffn * feedforward_full).astype(bf16)

    normed_near = spread_near(normed_ffn, ctx_size)
    normed_far = spread_far(normed_ffn, normed_near, ctx_size)
    normed_parts = spread_parts(normed_ffn, normed_near, normed_far, ctx_size)
    output_parts = []
    grad_normed_parts = []
    buffers = []
    for number, (part, grad_part) in enumerate(zip(normed_parts, grad_parts)):
        output_part, grad_normed_part, *buffers = ffn(
            number, ctx_size, part, grad_part, gate_up, down_mine, buffers
        )
        output_parts.append(output_part)
        grad_normed_parts.append(grad_normed_part)
    ffn_grads, normed_got = lax.optimization_barrier(
        (ffn_weights(seq_size, *buffers), first_hops(grad_normed_parts, ctx_size))
    )
    grad_normed_ffn = gathered_sum(grad_normed_parts, normed_got, ctx_size)
    weight_grads = lax.psum_scatter(ffn_grads, "seq", scatter_dimension=0)

    grad_ffn_gain = jnp.sum(grad_normed_ffn * hidden * inverse_ffn, axis=0)
    weighted_ffn = grad_normed_ffn * feedforward_full
    grad_hidden = (
        grad_low.astype(f32)
        + inverse_ffn * weighted_ffn
        - hidden
        * inverse_ffn
        * inverse_ffn
        * inverse_ffn
        * jnp.mean(weighted_ffn * hidden, axis=-1, keepdims=True)
    )
    hidden_low = grad_hidden.astype(bf16)
    grad_mixed = dot(hidden_low, output_full, NT).astype(bf16)

    output_parts = lax.optimization_barrier((output_parts, grad_mixed))[0]
    output_got = first_hops(output_parts, ctx_size)

    grad_queries, pair_grads = attend_backward(
        order,
        queries,
        pair_parts,
        mixed,
        grad_mixed.reshape(sequences * 2, half, Q_WIDTH),
        row_stats,
        cosine.reshape(sequences * 2, half, PAIR),
        sine.reshape(sequences * 2, half, PAIR),
    )
    pair_grads, output_got = lax.optimization_barrier((pair_grads, output_got))
    pair_sums = [pair_grads[:, :2].reshape(rows, 2 * K_WIDTH)]
    for k in range(1, ctx_size):
        pair_sums.append(
            hop(pair_grads[:, 2 * k : 2 * k + 2], ctx_size, k).reshape(rows, 2 * K_WIDTH)
        )
    hidden_late = lax.optimization_barrier((hidden_low, pair_grads))[0]
    output_pieces = weight_pieces(core, ctx_size, seq_size, mixed_rows, hidden_late)
    output_got = lax.optimization_barrier((output_got, pair_sums))[0]
    output_sum = gathered_sum(output_parts, output_got, ctx_size)
    grad_queries = grad_queries.reshape(rows, Q_WIDTH)
    grad_pairs, tokens_grad, gain_sum, bias_sum = project_backward(
        grad_queries,
        project_full,
        tokens_mine,
        attention_full,
        grad_hidden,
        cosine,
        sine,
        pair_sums,
    )

    def core_sum(mine, other):
        return (mine.astype(f32) + from_other_core(other).astype(f32)).astype(bf16)

    def ctx_sum(parts):
        def part(k):
            return lax.dynamic_index_in_dim(parts, place ^ k, 0, keepdims=False)

        total = part(0).astype(f32)
        for k in range(1, ctx_size):
            total = total + hop(part(k), ctx_size, k).astype(f32)
        return total

    def floor_sum(column):
        column = column.astype(bf16).reshape(floors, -1, column.shape[1])
        total = lax.dynamic_index_in_dim(column, floor, 0, keepdims=False).astype(f32)
        for step in range(1, floors):
            sent = lax.dynamic_index_in_dim(column, (floor + step) % floors, 0, keepdims=False)
            total = total + lax.ppermute(
                sent, "seq", [(i, (i + 2 * step) % seq_size) for i in range(seq_size)]
            ).astype(f32)
        return total

    def by_owner(parts):
        return parts.reshape(ctx_size, -1, parts.shape[-1])

    output_chip = by_owner(core_sum(*output_pieces))
    output_chip = lax.optimization_barrier((output_chip, pair_sums))[0]
    output_total = ctx_sum(output_chip)

    project_pieces = weight_pieces(core, ctx_size, seq_size, normed, grad_queries, grad_pairs)
    sums = jnp.concatenate(
        [
            gain_sum.reshape(ctx_size, gain_width),
            bias_sum.reshape(ctx_size, own_width),
            grad_ffn_gain.reshape(ctx_size, gain_width),
        ],
        axis=1,
    )
    sums = jnp.pad(sums, ((0, 0), (0, spare))).reshape(ctx_size, -1, own_width).astype(bf16)
    project_chip = by_owner(core_sum(*project_pieces))
    project_chip, output_total, output_sum = lax.optimization_barrier(
        (project_chip, output_total, output_sum)
    )
    output_out = floor_sum(output_total)
    down_late = lax.optimization_barrier((weight_grads[2], project_pieces))[0]
    down_late = down_late.reshape(depth, fold, down_rows)
    down_came = crossed_parts([down_late[:, t] for t in range(fold)])
    project_total = ctx_sum(jnp.concatenate([project_chip, sums], axis=1))
    project_out = floor_sum(project_total[:held])
    vector_sum = project_total[held:].reshape(-1)
    mask = 1
    while mask < seq_size:
        vector_sum = vector_sum + lax.ppermute(
            vector_sum, "seq", [(i, i ^ mask) for i in range(seq_size)]
        )
        mask *= 2

    tokens_grad = tokens_grad.reshape(tokens.shape)
    tokens_gradient = jnp.concatenate(
        [
            tokens_grad[:, :half],
            lax.ppermute(tokens_grad[:, half:].astype(bf16), "ctx", mirror).astype(f32),
        ],
        axis=1,
    )
    output_zigzag = hidden + output_sum
    layer_output = zigzag(output_zigzag.astype(bf16).reshape(tokens.shape))

    down_out = jnp.concatenate(down_came, axis=0).T

    return (
        layer_output,
        tokens_gradient,
        vector_sum[:gain_width],
        project_out,
        vector_sum[gain_width : gain_width + own_width],
        output_out,
        vector_sum[gain_width + own_width : vectors.shape[0]],
        weight_grads[0].astype(f32),
        weight_grads[1].astype(f32),
        down_out.astype(f32),
    )


def solution(mesh):
    matrix = P("seq", "ctx")
    vector = P("ctx")
    activation = P("seq", "ctx", None)

    def step(*arrays):
        return on_device(mesh.shape["seq"], mesh.shape["ctx"], *arrays)

    return jax.shard_map(
        step,
        mesh=mesh,
        in_specs=(
            activation,
            vector,
            matrix,
            vector,
            matrix,
            vector,
            matrix,
            matrix,
            matrix,
            activation,
        ),
        out_specs=(
            activation,
            activation,
            vector,
            matrix,
            vector,
            matrix,
            vector,
            matrix,
            matrix,
            matrix,
        ),
        check_vma=False,
    )
```

```python
import functools
import math
import jax
import jax.numpy as jnp
from jax import lax
from jax.experimental import pallas as pl
from jax.experimental.pallas import tpu as pltpu
from jax.sharding import PartitionSpec as P

HEADS = 14
KV_HEADS = 2
HEAD_DIM = 64
GROUP = HEADS // KV_HEADS
PAIRS = HEADS // 2
PAIR = 2 * HEAD_DIM
Q_WIDTH = HEADS * HEAD_DIM
K_WIDTH = KV_HEADS * HEAD_DIM

norm_eps = 1e-06
rope_base = 1000000.0
masked_value = -1e30
score_scale = HEAD_DIM ** (-0.5)
log2_e = math.log2(math.e)
bf16 = jnp.bfloat16
f32 = jnp.float32


def inverse_rms(tensor):
    return lax.rsqrt(jnp.mean(tensor * tensor, axis=-1, keepdims=True) + norm_eps)


def dot(a, b, dims):
    return lax.dot_general(a, b, (dims, ((), ())), preferred_element_type=f32)


NN = ((1,), (0,))
NT = ((1,), (1,))
TN = ((0,), (0,))


def rotation_tables(positions):
    half_width = HEAD_DIM // 2
    steps_up = jnp.arange(half_width).astype(f32)
    frequency = jnp.power(jnp.asarray(rope_base, f32), -2.0 * steps_up / HEAD_DIM)
    angles = positions.astype(f32)[:, None] * frequency[None, :]
    cosine = jnp.cos(angles)
    sine = jnp.sin(angles)
    return (
        jnp.concatenate([cosine, cosine, cosine, cosine], axis=-1),
        jnp.concatenate([-sine, sine, -sine, sine], axis=-1),
    )


def turn_pair(x, cosine, sine):
    lane = lax.broadcasted_iota(jnp.int32, x.shape, 1)
    quarter = HEAD_DIM // 2
    other = jnp.where(
        (lane // quarter) % 2 == 0,
        pltpu.roll(x, PAIR - quarter, 1),
        pltpu.roll(x, quarter, 1),
    )
    return x * cosine + other * sine


def swap_pair(x):
    return pltpu.roll(x.astype(f32), HEAD_DIM, 1)


def params():
    return pltpu.CompilerParams(vmem_limit_bytes=60 << 20)


def project_kernel(x_ref, gain_ref, w_ref, bias_ref, cos_ref, sin_ref, normed_ref, q_ref, kv_ref):
    x = x_ref[...].astype(f32)
    normed = (x * inverse_rms(x) * gain_ref[...]).astype(bf16)
    normed_ref[...] = normed
    projected = dot(normed, w_ref[...], NN) + bias_ref[...]
    cosine = cos_ref[...]
    sine = sin_ref[...]
    for pair in range(PAIRS + 1):
        lanes = slice(pair * PAIR, (pair + 1) * PAIR)
        turned = turn_pair(projected[:, lanes], cosine, sine).astype(bf16)
        if pair < PAIRS:
            q_ref[:, lanes] = turned
        else:
            kv_ref[:, :K_WIDTH] = turned
    kv_ref[:, K_WIDTH:] = projected[:, Q_WIDTH + K_WIDTH :].astype(bf16)


def row_spec(tile, width):
    return pl.BlockSpec((tile, width), lambda i: (i, 0))


def full_spec(*shape):
    return pl.BlockSpec(shape, lambda i: (0,) * len(shape))


def project_forward(tokens, gain, weight, bias, cosine, sine):
    rows, width = tokens.shape
    tile = rows // 2
    columns = Q_WIDTH + 2 * K_WIDTH
    return pl.pallas_call(
        project_kernel,
        grid=(2,),
        in_specs=[
            row_spec(tile, width),
            full_spec(1, width),
            full_spec(width, columns),
            full_spec(1, columns),
            row_spec(tile, PAIR),
            row_spec(tile, PAIR),
        ],
        out_specs=[row_spec(tile, width), row_spec(tile, Q_WIDTH), row_spec(tile, 2 * K_WIDTH)],
        out_shape=[
            jax.ShapeDtypeStruct((rows, width), bf16),
            jax.ShapeDtypeStruct((rows, Q_WIDTH), bf16),
            jax.ShapeDtypeStruct((rows, 2 * K_WIDTH), bf16),
        ],
        cost_estimate=pl.CostEstimate(
            flops=4 * rows * width * columns, bytes_accessed=5 << 20, transcendentals=0
        ),
        compiler_params=params(),
        name="project_forward",
    )(tokens, gain, weight, bias, cosine, sine)


def project_back_kernel(
    gq_ref, w_ref, x_ref, gain_ref, hidden_ref, cos_ref, sin_ref, *rest
):
    parts = rest[:-4]
    gkv_ref, tokens_ref, gain_sum_ref, bias_sum_ref = rest[-4:]
    total = parts[0][...].astype(f32)
    for part in parts[1:]:
        total = total + part[...].astype(f32)
    turned = turn_pair(total[:, :K_WIDTH], cos_ref[...], -sin_ref[...]).astype(bf16)
    gkv_ref[:, :K_WIDTH] = turned
    gkv_ref[:, K_WIDTH:] = total[:, K_WIDTH:].astype(bf16)
    grads = jnp.concatenate([gq_ref[...], gkv_ref[...]], axis=1)
    grad_normed = dot(grads, w_ref[...], NT)
    x = x_ref[...].astype(f32)
    inverse = inverse_rms(x)
    weighted = grad_normed * gain_ref[...]
    tokens_ref[...] = (
        hidden_ref[...]
        + inverse * weighted
        - x * (inverse * inverse * inverse * jnp.mean(weighted * x, axis=-1, keepdims=True))
    )

    @pl.when(pl.program_id(0) == 0)
    def _():
        gain_sum_ref[...] = jnp.zeros_like(gain_sum_ref)
        bias_sum_ref[...] = jnp.zeros_like(bias_sum_ref)

    gain_sum_ref[...] += jnp.sum(grad_normed * x * inverse, axis=0, keepdims=True)
    bias_sum_ref[...] += jnp.sum(grads.astype(f32), axis=0, keepdims=True)


def project_backward(grad_queries, weight, tokens, gain, grad_hidden, cosine, sine, parts):
    rows, width = tokens.shape
    tile = rows // 2
    columns = Q_WIDTH + 2 * K_WIDTH
    return pl.pallas_call(
        project_back_kernel,
        grid=(2,),
        in_specs=[
            row_spec(tile, Q_WIDTH),
            full_spec(width, columns),
            row_spec(tile, width),
            full_spec(1, width),
            row_spec(tile, width),
            row_spec(tile, PAIR),
            row_spec(tile, PAIR),
        ]
        + [row_spec(tile, 2 * K_WIDTH)] * len(parts),
        out_specs=[
            row_spec(tile, 2 * K_WIDTH),
            row_spec(tile, width),
            full_spec(1, width),
            full_spec(1, columns),
        ],
        out_shape=[
            jax.ShapeDtypeStruct((rows, 2 * K_WIDTH), bf16),
            jax.ShapeDtypeStruct((rows, width), f32),
            jax.ShapeDtypeStruct((1, width), f32),
            jax.ShapeDtypeStruct((1, columns), f32),
        ],
        cost_estimate=pl.CostEstimate(
            flops=4 * rows * width * columns, bytes_accessed=8 << 20, transcendentals=0
        ),
        compiler_params=params(),
        name="project_backward",
    )(grad_queries, weight, tokens, gain, grad_hidden, cosine, sine, *parts)


def owned_weights_kernel(ctx_size, normed_ref, gq_ref, gkv_ref, mixed_ref, hidden_ref, out_ref):
    grads = jnp.concatenate([gq_ref[...], gkv_ref[...]], axis=1)
    project = dot(normed_ref[...], grads, TN)
    output = dot(mixed_ref[...], hidden_ref[...], TN)
    first = project.shape[1] // ctx_size
    second = output.shape[1] // ctx_size
    own = first + second
    for rank in range(ctx_size):
        out_ref[:, rank * own : (rank + 1) * own] = jnp.concatenate(
            [
                project[:, rank * first : (rank + 1) * first],
                output[:, rank * second : (rank + 1) * second],
            ],
            axis=1,
        ).astype(bf16)


def owned_weights(ctx_size, normed, grad_queries, grad_pairs, mixed, hidden_low):
    rows, width = normed.shape
    columns = Q_WIDTH + 2 * K_WIDTH + hidden_low.shape[1]
    arrays = (normed, grad_queries, grad_pairs, mixed, hidden_low)
    return pl.pallas_call(
        functools.partial(owned_weights_kernel, ctx_size),
        grid=(1,),
        in_specs=[full_spec(*x.shape) for x in arrays],
        out_specs=full_spec(width, columns),
        out_shape=jax.ShapeDtypeStruct((width, columns), bf16),
        cost_estimate=pl.CostEstimate(
            flops=4 * rows * width * columns, bytes_accessed=8 << 20, transcendentals=0
        ),
        compiler_params=params(),
        name="owned_weights",
    )(*arrays)


def pair_sides(both):
    x, x_swapped = both[:, :PAIR], both[:, PAIR:]
    low = lax.broadcasted_iota(jnp.int32, x.shape, 1) < HEAD_DIM
    zero = jnp.zeros_like(x)
    left = (jnp.where(low, x, zero), jnp.where(low, x_swapped, zero))
    right = (jnp.where(low, zero, x_swapped), jnp.where(low, zero, x))
    sides = {}
    for pair in range(PAIRS):
        key = (2 * pair // GROUP, (2 * pair + 1) // GROUP)
        if key not in sides:
            sides[key] = jnp.concatenate([left[key[0]], right[key[1]]], axis=0)
    return sides


def causal(block):
    key_at = lax.broadcasted_iota(jnp.int32, (block, block), 0)
    query_at = lax.broadcasted_iota(jnp.int32, (block, block), 1)
    return key_at <= query_at


def forward_kernel(order_ref, q_ref, *rest):
    parts = rest[:-7]
    o_ref, lse_ref, keys_ref, turned_ref, top_ref, total_ref, acc_ref = rest[-7:]
    block = q_ref.shape[1]
    turn = pl.program_id(0) % 2
    last = order_ref[turn]

    @pl.when(turn == 0)
    def _():
        for number, part in enumerate(parts):
            for half in range(2):
                at = order_ref[2 * number + half]
                keys = part[0, half, :, :K_WIDTH]
                keys_ref[at, :, :PAIR] = keys
                keys_ref[at, :, PAIR:] = swap_pair(keys).astype(bf16)
                turned_ref[at] = jnp.transpose(part[0, half, :, K_WIDTH:].astype(f32)).astype(
                    bf16
                )

    top_ref[...] = jnp.full_like(top_ref, masked_value)
    total_ref[...] = jnp.zeros_like(total_ref)
    acc_ref[...] = jnp.zeros_like(acc_ref)
    scale = score_scale * log2_e

    def step(index, diagonal):
        sides = pair_sides(keys_ref[index])
        values = turned_ref[index]
        if diagonal:
            allowed = causal(block)
        for pair in range(PAIRS):
            both = dot(
                sides[(2 * pair // GROUP, (2 * pair + 1) // GROUP)],
                q_ref[0, :, pair * PAIR : (pair + 1) * PAIR],
                NT,
            )
            for odd in range(2):
                head = 2 * pair + odd
                kv = head // GROUP
                scores = both[odd * block : (odd + 1) * block] * scale
                if diagonal:
                    scores = jnp.where(allowed, scores, masked_value)
                old = top_ref[head : head + 1, :]
                new = jnp.maximum(old, jnp.max(scores, axis=0, keepdims=True))
                shrink = jnp.exp2(old - new)
                weights = jnp.exp2(scores - new)
                top_ref[head : head + 1, :] = new
                total_ref[head : head + 1, :] = total_ref[
                    head : head + 1, :
                ] * shrink + jnp.sum(weights, axis=0, keepdims=True)
                rows = slice(head * HEAD_DIM, (head + 1) * HEAD_DIM)
                acc_ref[rows, :] = acc_ref[rows, :] * shrink + dot(
                    values[kv * HEAD_DIM : (kv + 1) * HEAD_DIM], weights.astype(bf16), NN
                )

    def body(index, carry):
        step(index, False)
        return carry

    lax.fori_loop(0, last, body, 0)
    step(last, True)
    for pair in range(PAIRS):
        halves = []
        for odd in range(2):
            head = 2 * pair + odd
            halves.append(
                acc_ref[head * HEAD_DIM : (head + 1) * HEAD_DIM, :]
                / total_ref[head : head + 1, :]
            )
        o_ref[0, :, pair * PAIR : (pair + 1) * PAIR] = jnp.transpose(
            jnp.concatenate(halves, axis=0)
        ).astype(bf16)
    lse_ref[0] = top_ref[...] + jnp.log2(total_ref[...])


def backward_kernel(order_ref, q_ref, o_ref, g_ref, lse_ref, cos_ref, sin_ref, *rest):
    parts = rest[:-8]
    dq_ref, dkv_ref, keys_ref, values_ref, turned_ref, dk_ref, dv_ref, acc_ref = rest[-8:]
    block = q_ref.shape[1]
    turn = pl.program_id(0) % 2
    last = order_ref[turn]
    scale = score_scale * log2_e

    @pl.when(turn == 0)
    def _():
        dk_ref[...] = jnp.zeros_like(dk_ref)
        dv_ref[...] = jnp.zeros_like(dv_ref)
        for number, part in enumerate(parts):
            for half in range(2):
                at = order_ref[2 * number + half]
                keys = part[0, half, :, :K_WIDTH]
                values = part[0, half, :, K_WIDTH:]
                keys_ref[at, :, :PAIR] = keys
                keys_ref[at, :, PAIR:] = swap_pair(keys).astype(bf16)
                values_ref[at, :, :PAIR] = values
                values_ref[at, :, PAIR:] = swap_pair(values).astype(bf16)
                turned_ref[at] = jnp.transpose(keys.astype(f32)).astype(bf16)

    acc_ref[...] = jnp.zeros_like(acc_ref)
    product = g_ref[0].astype(f32) * o_ref[0].astype(f32)
    coarse = product.astype(bf16)
    fine = (product - coarse.astype(f32)).astype(bf16)
    head_of = lax.broadcasted_iota(jnp.int32, (16, Q_WIDTH), 1) // HEAD_DIM
    picks = (head_of == lax.broadcasted_iota(jnp.int32, (16, Q_WIDTH), 0)).astype(bf16)
    delta = dot(picks, coarse, NT) + dot(picks, fine, NT)

    def step(index, diagonal):
        key_sides = pair_sides(keys_ref[index])
        value_sides = pair_sides(values_ref[index])
        keys_turned = turned_ref[index]
        if diagonal:
            allowed = causal(block)
        key_sum = [[None, None], [None, None]]
        value_sum = [[None, None], [None, None]]

        def add(sums, odd, kv, part):
            sums[odd][kv] = part if sums[odd][kv] is None else sums[odd][kv] + part

        for pair in range(PAIRS):
            which = (2 * pair // GROUP, (2 * pair + 1) // GROUP)
            lanes = slice(pair * PAIR, (pair + 1) * PAIR)
            queries = q_ref[0, :, lanes]
            grads = g_ref[0, :, lanes]
            both = dot(key_sides[which], queries, NT)
            both_grads = dot(value_sides[which], grads, NT)
            low_weights = []
            low_scores = []
            for odd in range(2):
                head = 2 * pair + odd
                part = slice(odd * block, (odd + 1) * block)
                weights = jnp.exp2(both[part] * scale - lse_ref[0, head : head + 1, :])
                if diagonal:
                    weights = jnp.where(allowed, weights, 0.0)
                change = weights * (both_grads[part] - delta[head : head + 1, :])
                low_weights.append(weights.astype(bf16))
                low_scores.append(change.astype(bf16))
                rows = slice(head * HEAD_DIM, (head + 1) * HEAD_DIM)
                acc_ref[rows, :] += dot(
                    keys_turned[which[odd] * HEAD_DIM : (which[odd] + 1) * HEAD_DIM],
                    low_scores[odd],
                    NN,
                )
            value_part = dot(jnp.concatenate(low_weights, axis=0), grads, NN)
            key_part = dot(jnp.concatenate(low_scores, axis=0), queries, NN)
            for odd in range(2):
                part = slice(odd * block, (odd + 1) * block)
                add(value_sum, odd, which[odd], value_part[part])
                add(key_sum, odd, which[odd], key_part[part])
        low = lax.broadcasted_iota(jnp.int32, (block, PAIR), 1) < HEAD_DIM
        for sums, out_ref in ((key_sum, dk_ref), (value_sum, dv_ref)):
            out_ref[index, :, :PAIR] += jnp.where(low, sums[0][0], sums[1][1])
            out_ref[index, :, PAIR:] += jnp.where(low, sums[0][1], sums[1][0])

    def body(index, carry):
        step(index, False)
        return carry

    lax.fori_loop(0, last, body, 0)
    step(last, True)
    for pair in range(PAIRS):
        straight = jnp.transpose(acc_ref[pair * PAIR : (pair + 1) * PAIR, :]) * score_scale
        dq_ref[0, :, pair * PAIR : (pair + 1) * PAIR] = turn_pair(
            straight, cos_ref[0], -sin_ref[0]
        ).astype(bf16)

    @pl.when(turn == 1)
    def _():
        for slot in range(2 * len(parts)):
            at = order_ref[slot]
            keys = dk_ref[at, :, :PAIR] + swap_pair(dk_ref[at, :, PAIR:])
            dkv_ref[0, slot, :, :K_WIDTH] = (keys * score_scale).astype(bf16)
            values = dv_ref[at, :, :PAIR] + swap_pair(dv_ref[at, :, PAIR:])
            dkv_ref[0, slot, :, K_WIDTH:] = values.astype(bf16)


def attention_specs(block, parts):
    def rows(width):
        return pl.BlockSpec((1, block, width), lambda i, order: (i, 0, 0))

    def halves(number):
        return pl.BlockSpec((1, number, block, 2 * K_WIDTH), lambda i, order: (i // 2, 0, 0, 0))

    stats = pl.BlockSpec((1, 16, block), lambda i, order: (i, 0, 0))
    return rows, halves, stats


def attend_forward(order, queries, parts):
    count, block, _ = queries.shape
    slots = 2 * len(parts)
    rows, halves, stats = attention_specs(block, parts)
    pairs_done = count * block * (slots // 2 + 1) * block * HEADS
    return pl.pallas_call(
        forward_kernel,
        grid_spec=pltpu.PrefetchScalarGridSpec(
            num_scalar_prefetch=1,
            grid=(count,),
            in_specs=[rows(Q_WIDTH)] + [halves(2)] * len(parts),
            out_specs=[rows(Q_WIDTH), stats],
            scratch_shapes=[
                pltpu.VMEM((slots, block, 2 * PAIR), bf16),
                pltpu.VMEM((slots, PAIR, block), bf16),
                pltpu.VMEM((16, block), f32),
                pltpu.VMEM((16, block), f32),
                pltpu.VMEM((Q_WIDTH, block), f32),
            ],
        ),
        out_shape=[
            jax.ShapeDtypeStruct((count, block, Q_WIDTH), bf16),
            jax.ShapeDtypeStruct((count, 16, block), f32),
        ],
        cost_estimate=pl.CostEstimate(
            flops=pairs_done * 4 * 256, bytes_accessed=4 << 20, transcendentals=pairs_done
        ),
        compiler_params=params(),
        name="attend_forward",
    )(order, queries, *parts)


def attend_backward(order, queries, parts, mixed, grads, stats_in, cosine, sine):
    count, block, _ = queries.shape
    slots = 2 * len(parts)
    rows, halves, stats = attention_specs(block, parts)
    pairs_done = count * block * (slots // 2 + 1) * block * HEADS
    return pl.pallas_call(
        backward_kernel,
        grid_spec=pltpu.PrefetchScalarGridSpec(
            num_scalar_prefetch=1,
            grid=(count,),
            in_specs=[
                rows(Q_WIDTH),
                rows(Q_WIDTH),
                rows(Q_WIDTH),
                stats,
                rows(PAIR),
                rows(PAIR),
            ]
            + [halves(2)] * len(parts),
            out_specs=[rows(Q_WIDTH), halves(slots)],
            scratch_shapes=[
                pltpu.VMEM((slots, block, 2 * PAIR), bf16),
                pltpu.VMEM((slots, block, 2 * PAIR), bf16),
                pltpu.VMEM((slots, PAIR, block), bf16),
                pltpu.VMEM((slots, block, 2 * PAIR), f32),
                pltpu.VMEM((slots, block, 2 * PAIR), f32),
                pltpu.VMEM((Q_WIDTH, block), f32),
            ],
        ),
        out_shape=[
            jax.ShapeDtypeStruct((count, block, Q_WIDTH), bf16),
            jax.ShapeDtypeStruct((count // 2, slots, block, 2 * K_WIDTH), bf16),
        ],
        cost_estimate=pl.CostEstimate(
            flops=pairs_done * 10 * 256, bytes_accessed=8 << 20, transcendentals=pairs_done
        ),
        compiler_params=params(),
        name="attend_backward",
    )(order, queries, mixed, grads, stats_in, cosine, sine, *parts)


def ffn_kernel(x_low, x_high, c_low, c_high, w_ref, d_ref, *rest):
    out_ref, grad_ref, x_all, c_all, active_all, gate_all, up_all = rest[-7:]
    seq_size, _, depth, columns = w_ref.shape
    width = seq_size * depth
    low = pl.program_id(0) == 0
    x = jnp.where(low, x_low[...], x_high[...])
    c = jnp.where(low, c_low[...], c_high[...])
    x_all[0] = x
    c_all[0] = c
    gate_w = w_ref[:, 0].reshape(width, columns)
    up_w = w_ref[:, 1].reshape(width, columns)
    down_w = d_ref[...].reshape(width, columns)
    gate = dot(x, gate_w, NN)
    up = dot(x, up_w, NN)
    grad_active = dot(c, down_w, NN)
    sigmoid = jax.nn.sigmoid(gate)
    silu = gate * sigmoid
    active = (silu * up).astype(bf16)
    grad_gate = (grad_active * up * sigmoid * (1.0 + gate * (1.0 - sigmoid))).astype(bf16)
    grad_up = (grad_active * silu).astype(bf16)
    active_all[0] = active
    gate_all[0] = grad_gate
    up_all[0] = grad_up
    grad_ref[...] = (dot(grad_gate, gate_w, NT) + dot(grad_up, up_w, NT)).astype(bf16)
    out_ref[...] = dot(active, down_w, NT).astype(bf16)


def ffn(number, count, rows, halves, weights, down, buffers):
    width = halves[0][0].shape[1]
    columns = weights.shape[3]
    tile = rows // 2

    def half_spec(at):
        return pl.BlockSpec((tile, width), lambda i: (at, 0))

    def slot(columns):
        return pl.BlockSpec((1, tile, columns), lambda i: (number, i, 0))

    wide = jax.ShapeDtypeStruct((count, rows, width), bf16)
    inner = jax.ShapeDtypeStruct((count, rows, columns), bf16)
    return pl.pallas_call(
        ffn_kernel,
        grid=(2,),
        in_specs=[half_spec(at) for _, at in halves]
        + [full_spec(*weights.shape), full_spec(*down.shape)]
        + [pl.BlockSpec(memory_space=pl.ANY)] * len(buffers),
        out_specs=[row_spec(tile, width), row_spec(tile, width)]
        + [slot(width)] * 2
        + [slot(columns)] * 3,
        out_shape=[jax.ShapeDtypeStruct((rows, width), bf16)] * 2 + [wide] * 2 + [inner] * 3,
        input_output_aliases={6 + i: 2 + i for i in range(len(buffers))},
        cost_estimate=pl.CostEstimate(
            flops=14 * rows * width * columns, bytes_accessed=16 << 20, transcendentals=0
        ),
        compiler_params=params(),
        name="ffn",
    )(*[x for x, _ in halves], weights, down, *buffers)


def ffn_weights_kernel(x_ref, c_ref, active_ref, gate_ref, up_ref, out_ref, acc_ref):
    step = pl.program_id(0)
    seq_size, _, depth, columns = out_ref.shape

    @pl.when(step == 0)
    def _():
        acc_ref[...] = jnp.zeros_like(acc_ref)

    x = x_ref[0]
    acc_ref[0] += dot(x, gate_ref[0], TN)
    acc_ref[1] += dot(x, up_ref[0], TN)
    acc_ref[2] += dot(c_ref[0], active_ref[0], TN)

    @pl.when(step == pl.num_programs(0) - 1)
    def _():
        for which in range(3):
            out_ref[:, which] = acc_ref[which].reshape(seq_size, depth, columns).astype(bf16)


def ffn_weights(seq_size, x, c, active, grad_gate, grad_up):
    count, rows, width = x.shape
    columns = active.shape[2]

    def slot(columns):
        return pl.BlockSpec((1, rows, columns), lambda i: (i, 0, 0))

    shape = (seq_size, 3, width // seq_size, columns)
    return pl.pallas_call(
        ffn_weights_kernel,
        grid=(count,),
        in_specs=[slot(width)] * 2 + [slot(columns)] * 3,
        out_specs=pl.BlockSpec(shape, lambda i: (0, 0, 0, 0)),
        out_shape=jax.ShapeDtypeStruct(shape, bf16),
        scratch_shapes=[pltpu.VMEM((3, width, columns), f32)],
        cost_estimate=pl.CostEstimate(
            flops=6 * count * rows * width * columns, bytes_accessed=30 << 20, transcendentals=0
        ),
        compiler_params=params(),
        name="ffn_weights",
    )(x, c, active, grad_gate, grad_up)


def hop(x, ctx_size, mask):
    return lax.ppermute(x, "ctx", [(i, i ^ mask) for i in range(ctx_size)])


def others(x, ctx_size):
    return [hop(x, ctx_size, k) for k in range(1, ctx_size)]


def others_sum(parts, got):
    total = parts[0].astype(f32)
    for part in got:
        total = total + part.astype(f32)
    return total


def pick(index, cases):
    return cases[0] if len(cases) == 1 else lax.select_n(index, *cases)


def on_device(
    seq_size,
    ctx_size,
    tokens,
    attention_gain,
    project_weight,
    project_bias,
    output_weight,
    feedforward_gain,
    gate_weight,
    up_weight,
    down_weight,
    cotangent,
):
    sequences, block_rows, width = tokens.shape
    place = lax.axis_index("ctx")
    half = block_rows // 2
    rows = sequences * block_rows
    fold = seq_size // ctx_size
    seq_place = lax.axis_index("seq")
    fold_place = seq_place % fold
    core = seq_place % 2
    floor = seq_place // 2
    floors = seq_size // 2
    far = ctx_size - 1
    half_rows = rows // 2

    def to_rows(x):
        shape = (sequences, 2, half, x.shape[-1])
        return jnp.swapaxes(x.reshape(shape), 0, 1).reshape(rows, x.shape[-1])

    def to_blocks(x):
        shape = (2, sequences, half, x.shape[-1])
        return jnp.swapaxes(x.reshape(shape), 0, 1)

    def attention_blocks(x):
        return to_blocks(x).reshape(2 * sequences, half, x.shape[-1])

    def crossed(x, j):
        return lax.ppermute(
            x,
            ("seq", "ctx"),
            [
                ((c * fold + r) * ctx_size + q, (q * fold + (r + j) % fold) * ctx_size + c)
                for c in range(ctx_size)
                for r in range(fold)
                for q in range(ctx_size)
            ],
        )

    def crossed_parts(parts):
        came = [
            crossed(pick(fold_place, [parts[(f + j) % fold] for f in range(fold)]), j)
            for j in range(fold)
        ]
        return [
            pick(fold_place, [came[(f - t) % fold] for f in range(fold)]) for t in range(fold)
        ]

    def swap_second(x):
        return jnp.concatenate([x[:half_rows], hop(x[half_rows:], ctx_size, far)], axis=0)

    owners = [place ^ k for k in range(ctx_size)]
    order = jnp.stack(
        [spot for owner in owners for spot in (2 * owner, 2 * (ctx_size - 1 - owner) + 1)]
    ).astype(jnp.int32)
    positions = order[:2, None, None] * half + jnp.arange(half, dtype=jnp.int32)[None, None, :]
    positions = jnp.broadcast_to(positions, (2, sequences, half)).reshape(-1)
    cosine, sine = rotation_tables(positions)

    def from_floors(x):
        came = [x] + [
            lax.ppermute(x, "seq", [(i, (i + 2 * step) % seq_size) for i in range(seq_size)])
            for step in range(1, floors)
        ]
        return jnp.concatenate(
            [
                pick(floor, [came[(mine - theirs) % floors] for mine in range(floors)])
                for theirs in range(floors)
            ],
            axis=0,
        )

    def from_ranks(x):
        return [x] + [hop(x, ctx_size, k) for k in range(1, ctx_size)]

    def by_rank(came):
        return [pick(place, [came[rank ^ p] for p in range(ctx_size)]) for rank in range(ctx_size)]

    def from_other_core(x):
        return lax.ppermute(x, "seq", [(i, i ^ 1) for i in range(seq_size)])

    def by_core(x, other):
        first, second = pick(core, [x, other]), pick(core, [other, x])
        shape = (floors, x.shape[0] // floors, x.shape[1])
        return jnp.stack([first.reshape(shape), second.reshape(shape)], axis=1).reshape(
            2 * x.shape[0], x.shape[1]
        )

    gate_up = lax.all_gather(jnp.stack([gate_weight, up_weight]), "seq", axis=0)
    gain_width = attention_gain.shape[0]
    own_width = project_weight.shape[1]
    vectors = jnp.concatenate([attention_gain, project_bias, feedforward_gain])
    spare = -vectors.shape[0] % own_width
    project_rows = from_floors(project_weight)
    held = project_rows.shape[0]
    tokens_mine = swap_second(to_rows(tokens))
    project_rows, tokens_mine = lax.optimization_barrier((project_rows, tokens_mine))
    project_came = from_ranks(
        jnp.concatenate(
            [project_rows, jnp.pad(vectors, (0, spare)).reshape(-1, own_width)], axis=0
        )
    )
    output_late = lax.optimization_barrier((output_weight, project_rows))[0]
    output_rows = from_floors(output_late)
    ordered = by_rank(project_came)
    vectors_all = [piece[held:].reshape(-1).astype(f32) for piece in ordered]

    def vector_whole(start, size):
        return jnp.concatenate([v[start : start + size] for v in vectors_all])[None, :]

    attention_full = vector_whole(0, gain_width)
    bias_full = vector_whole(gain_width, own_width)
    feedforward_full = vector_whole(gain_width + own_width, gain_width)
    project_columns = jnp.concatenate([piece[:held] for piece in ordered], axis=1)
    project_full = by_core(project_columns, from_other_core(project_columns))

    down_late, grad_late = lax.optimization_barrier((down_weight, cotangent, project_full))[:2]
    grad_rows = to_rows(grad_late)
    if ctx_size == 4:
        grad_near = [hop(grad_rows[:half_rows], 4, 1), hop(grad_rows[half_rows:], 4, 2)]
    else:
        grad_near = others(grad_rows, ctx_size)
    down_rows, down_columns = down_weight.shape
    depth = down_columns // fold
    down_turned = jnp.concatenate(
        crossed_parts(list(down_late.T.reshape(fold, depth, down_rows))), axis=1
    )
    normed, queries, pairs_mine = project_forward(
        tokens_mine, attention_full, project_full, bias_full, cosine, sine
    )
    down_turned, gate_up = lax.optimization_barrier((down_turned, gate_up, queries))[:2]
    down_mine = lax.all_gather(down_turned, "seq", axis=0)
    queries = attention_blocks(queries)
    pairs_mine = to_blocks(pairs_mine)
    pair_parts = [pairs_mine] + [hop(pairs_mine, ctx_size, k) for k in range(1, ctx_size)]
    grad_near, output_rows = lax.optimization_barrier((grad_near, output_rows, pair_parts))[:2]
    if ctx_size == 4:
        grad_far = [
            hop(jnp.concatenate([grad_rows[:half_rows], grad_near[0]], axis=0), 4, 2),
            hop(jnp.concatenate([grad_rows[half_rows:], grad_near[1]], axis=0), 4, 1),
        ]
    else:
        grad_far = []
    output_came = from_ranks(output_rows)
    queries = lax.optimization_barrier((queries, down_turned))[0]
    mixed, row_stats = attend_forward(order, queries, pair_parts)
    mixed, grad_far, output_came = lax.optimization_barrier((mixed, grad_far, output_came))
    if ctx_size == 4:
        firsts = [(grad_rows, 0), (grad_near[0], 0), (grad_far[0], 0), (grad_far[0], 1)]
        seconds = [(grad_rows, 1), (grad_far[1], 0), (grad_near[1], 0), (grad_far[1], 1)]
        own_second = grad_far[1][half_rows:]
    else:
        firsts = [(x, 0) for x in (grad_rows, *grad_near)]
        seconds = [(x, 1) for x in (grad_rows, *grad_near)]
        own_second = grad_near[far - 1][half_rows:]
    grad_low = jnp.concatenate([grad_rows[:half_rows], own_second], axis=0)
    output_columns = jnp.concatenate(by_rank(output_came), axis=1)
    output_full = by_core(output_columns, from_other_core(output_columns))
    mixed_rows = to_rows(mixed)
    hidden = tokens_mine.astype(f32) + dot(mixed_rows, output_full, NN)
    inverse_ffn = inverse_rms(hidden)
    normed_ffn = (hidden * inverse_ffn * feedforward_full).astype(bf16)

    normed_parts = [normed_ffn, *others(normed_ffn, ctx_size)]
    output_parts = []
    grad_normed_parts = []
    buffers = []
    for k, part in enumerate(normed_parts):
        output_part, grad_normed_part, *buffers = ffn(
            k,
            ctx_size,
            rows,
            [(part, 0), (part, 1), firsts[k], seconds[k ^ far]],
            gate_up,
            down_mine,
            buffers,
        )
        output_parts.append(output_part)
        grad_normed_parts.append(grad_normed_part)
    normed_got = [hop(grad_normed_parts[k], ctx_size, k) for k in range(1, ctx_size)]
    ffn_grads, normed_got = lax.optimization_barrier(
        (ffn_weights(seq_size, *buffers), normed_got)
    )
    grad_normed_ffn = others_sum(grad_normed_parts, normed_got)
    weight_grads = lax.psum_scatter(ffn_grads, "seq", scatter_dimension=0)

    grad_ffn_gain = jnp.sum(grad_normed_ffn * hidden * inverse_ffn, axis=0)
    weighted_ffn = grad_normed_ffn * feedforward_full
    grad_hidden = (
        grad_low.astype(f32)
        + inverse_ffn * weighted_ffn
        - hidden
        * inverse_ffn
        * inverse_ffn
        * inverse_ffn
        * jnp.mean(weighted_ffn * hidden, axis=-1, keepdims=True)
    )
    hidden_low = grad_hidden.astype(bf16)
    grad_mixed = dot(hidden_low, output_full, NT).astype(bf16)

    output_parts = lax.optimization_barrier((output_parts, grad_mixed))[0]
    output_got = [hop(output_parts[k], ctx_size, k) for k in range(1, ctx_size)]

    grad_queries, pair_grads = attend_backward(
        order,
        queries,
        pair_parts,
        mixed,
        attention_blocks(grad_mixed),
        row_stats,
        attention_blocks(cosine),
        attention_blocks(sine),
    )
    pair_grads, output_got = lax.optimization_barrier((pair_grads, output_got))
    pair_sums = [to_rows(pair_grads[:, :2])]
    for k in range(1, ctx_size):
        pair_sums.append(to_rows(hop(pair_grads[:, 2 * k : 2 * k + 2], ctx_size, k)))
    output_zigzag = hidden + others_sum(output_parts, output_got)
    grad_queries = to_rows(grad_queries)
    grad_pairs, tokens_grad, gain_sum, bias_sum = project_backward(
        grad_queries,
        project_full,
        tokens_mine,
        attention_full,
        grad_hidden,
        cosine,
        sine,
        pair_sums,
    )

    owned = lax.psum_scatter(
        owned_weights(ctx_size, normed, grad_queries, grad_pairs, mixed_rows, hidden_low),
        "seq",
        scatter_dimension=0,
        tiled=True,
    )

    layer_output = swap_second(output_zigzag.astype(bf16))
    tokens_gradient = jnp.concatenate(
        [
            tokens_grad[:half_rows],
            hop(tokens_grad[half_rows:].astype(bf16), ctx_size, far).astype(f32),
        ],
        axis=0,
    )
    sums = jnp.concatenate(
        [
            gain_sum.reshape(ctx_size, gain_width),
            bias_sum.reshape(ctx_size, own_width),
            grad_ffn_gain.reshape(ctx_size, gain_width),
        ],
        axis=1,
    )

    def sums_for(k):
        return lax.dynamic_index_in_dim(sums, place ^ k, 0)

    vector_sum = sums_for(0)
    for k in range(1, ctx_size):
        vector_sum = vector_sum + hop(sums_for(k), ctx_size, k)
    mask = 1
    while mask < seq_size:
        vector_sum = vector_sum + lax.ppermute(
            vector_sum, "seq", [(i, i ^ mask) for i in range(seq_size)]
        )
        mask *= 2
    vector_sum = vector_sum[0]
    down_late = weight_grads[2].reshape(depth, fold, down_rows)
    down_came = crossed_parts([down_late[:, t] for t in range(fold)])
    down_out = jnp.concatenate(down_came, axis=0).T
    owned, layer_output, tokens_gradient, vector_sum, down_out = lax.optimization_barrier(
        (owned, layer_output, tokens_gradient, vector_sum, down_out)
    )
    own_columns = owned.shape[1] // ctx_size

    def owned_for(k):
        return lax.dynamic_slice_in_dim(owned, (place ^ k) * own_columns, own_columns, 1)

    owned_total = owned_for(0).astype(f32)
    for k in range(1, ctx_size):
        owned_total = owned_total + hop(owned_for(k), ctx_size, k).astype(f32)

    return (
        to_blocks(layer_output).reshape(tokens.shape),
        to_blocks(tokens_gradient).reshape(tokens.shape),
        vector_sum[:gain_width],
        owned_total[:, :own_width],
        vector_sum[gain_width : gain_width + own_width],
        owned_total[:, own_width:],
        vector_sum[gain_width + own_width : vectors.shape[0]],
        weight_grads[0].astype(f32),
        weight_grads[1].astype(f32),
        down_out.astype(f32),
    )


def solution(mesh):
    matrix = P("seq", "ctx")
    vector = P("ctx")
    activation = P("seq", "ctx", None)

    def step(*arrays):
        return on_device(mesh.shape["seq"], mesh.shape["ctx"], *arrays)

    return jax.shard_map(
        step,
        mesh=mesh,
        in_specs=(
            activation,
            vector,
            matrix,
            vector,
            matrix,
            vector,
            matrix,
            matrix,
            matrix,
            activation,
        ),
        out_specs=(
            activation,
            activation,
            vector,
            matrix,
            vector,
            matrix,
            vector,
            matrix,
            matrix,
            matrix,
        ),
        check_vma=False,
    )
```

```python
import functools
import math
import jax
import jax.numpy as jnp
from jax import lax
from jax.experimental import pallas as pl
from jax.experimental.pallas import tpu as pltpu
from jax.sharding import PartitionSpec as P

HEADS = 14
KV_HEADS = 2
HEAD_DIM = 64
GROUP = HEADS // KV_HEADS
PAIRS = HEADS // 2
PAIR = 2 * HEAD_DIM
Q_WIDTH = HEADS * HEAD_DIM
K_WIDTH = KV_HEADS * HEAD_DIM

norm_eps = 1e-06
rope_base = 1000000.0
masked_value = -1e30
score_scale = HEAD_DIM ** (-0.5)
log2_e = math.log2(math.e)
bf16 = jnp.bfloat16
f32 = jnp.float32


def inverse_rms(tensor):
    return lax.rsqrt(jnp.mean(tensor * tensor, axis=-1, keepdims=True) + norm_eps)


def dot(a, b, dims):
    return lax.dot_general(a, b, (dims, ((), ())), preferred_element_type=f32)


NN = ((1,), (0,))
NT = ((1,), (1,))
TN = ((0,), (0,))


def rotation_tables(positions):
    half_width = HEAD_DIM // 2
    steps_up = jnp.arange(half_width).astype(f32)
    frequency = jnp.power(jnp.asarray(rope_base, f32), -2.0 * steps_up / HEAD_DIM)
    angles = positions.astype(f32)[:, None] * frequency[None, :]
    cosine = jnp.cos(angles)
    sine = jnp.sin(angles)
    return (
        jnp.concatenate([cosine, cosine, cosine, cosine], axis=-1),
        jnp.concatenate([-sine, sine, -sine, sine], axis=-1),
    )


def turn_pair(x, cosine, sine):
    lane = lax.broadcasted_iota(jnp.int32, x.shape, 1)
    quarter = HEAD_DIM // 2
    other = jnp.where(
        (lane // quarter) % 2 == 0,
        pltpu.roll(x, PAIR - quarter, 1),
        pltpu.roll(x, quarter, 1),
    )
    return x * cosine + other * sine


def swap_pair(x):
    return pltpu.roll(x.astype(f32), HEAD_DIM, 1)


def params():
    return pltpu.CompilerParams(vmem_limit_bytes=60 << 20)


def project_kernel(x_ref, gain_ref, w_ref, bias_ref, cos_ref, sin_ref, normed_ref, q_ref, kv_ref):
    x = x_ref[...].astype(f32)
    normed = (x * inverse_rms(x) * gain_ref[...]).astype(bf16)
    normed_ref[...] = normed
    projected = dot(normed, w_ref[...], NN) + bias_ref[...]
    cosine = cos_ref[...]
    sine = sin_ref[...]
    for pair in range(PAIRS + 1):
        lanes = slice(pair * PAIR, (pair + 1) * PAIR)
        turned = turn_pair(projected[:, lanes], cosine, sine).astype(bf16)
        if pair < PAIRS:
            q_ref[:, lanes] = turned
        else:
            kv_ref[:, :K_WIDTH] = turned
    kv_ref[:, K_WIDTH:] = projected[:, Q_WIDTH + K_WIDTH :].astype(bf16)


def row_spec(tile, width):
    return pl.BlockSpec((tile, width), lambda i: (i, 0))


def full_spec(*shape):
    return pl.BlockSpec(shape, lambda i: (0,) * len(shape))


def project_forward(tokens, gain, weight, bias, cosine, sine):
    rows, width = tokens.shape
    tile = rows // 2
    columns = Q_WIDTH + 2 * K_WIDTH
    return pl.pallas_call(
        project_kernel,
        grid=(2,),
        in_specs=[
            row_spec(tile, width),
            full_spec(1, width),
            full_spec(width, columns),
            full_spec(1, columns),
            row_spec(tile, PAIR),
            row_spec(tile, PAIR),
        ],
        out_specs=[row_spec(tile, width), row_spec(tile, Q_WIDTH), row_spec(tile, 2 * K_WIDTH)],
        out_shape=[
            jax.ShapeDtypeStruct((rows, width), bf16),
            jax.ShapeDtypeStruct((rows, Q_WIDTH), bf16),
            jax.ShapeDtypeStruct((rows, 2 * K_WIDTH), bf16),
        ],
        cost_estimate=pl.CostEstimate(
            flops=4 * rows * width * columns, bytes_accessed=5 << 20, transcendentals=0
        ),
        compiler_params=params(),
        name="project_forward",
    )(tokens, gain, weight, bias, cosine, sine)


def project_back_kernel(
    gq_ref, w_ref, x_ref, gain_ref, hidden_ref, cos_ref, sin_ref, *rest
):
    parts = rest[:-4]
    gkv_ref, tokens_ref, gain_sum_ref, bias_sum_ref = rest[-4:]
    total = parts[0][...].astype(f32)
    for part in parts[1:]:
        total = total + part[...].astype(f32)
    turned = turn_pair(total[:, :K_WIDTH], cos_ref[...], -sin_ref[...]).astype(bf16)
    gkv_ref[:, :K_WIDTH] = turned
    gkv_ref[:, K_WIDTH:] = total[:, K_WIDTH:].astype(bf16)
    grads = jnp.concatenate([gq_ref[...], gkv_ref[...]], axis=1)
    grad_normed = dot(grads, w_ref[...], NT)
    x = x_ref[...].astype(f32)
    inverse = inverse_rms(x)
    weighted = grad_normed * gain_ref[...]
    tokens_ref[...] = (
        hidden_ref[...]
        + inverse * weighted
        - x * (inverse * inverse * inverse * jnp.mean(weighted * x, axis=-1, keepdims=True))
    )

    @pl.when(pl.program_id(0) == 0)
    def _():
        gain_sum_ref[...] = jnp.zeros_like(gain_sum_ref)
        bias_sum_ref[...] = jnp.zeros_like(bias_sum_ref)

    gain_sum_ref[...] += jnp.sum(grad_normed * x * inverse, axis=0, keepdims=True)
    bias_sum_ref[...] += jnp.sum(grads.astype(f32), axis=0, keepdims=True)


def project_backward(grad_queries, weight, tokens, gain, grad_hidden, cosine, sine, parts):
    rows, width = tokens.shape
    tile = rows // 2
    columns = Q_WIDTH + 2 * K_WIDTH
    return pl.pallas_call(
        project_back_kernel,
        grid=(2,),
        in_specs=[
            row_spec(tile, Q_WIDTH),
            full_spec(width, columns),
            row_spec(tile, width),
            full_spec(1, width),
            row_spec(tile, width),
            row_spec(tile, PAIR),
            row_spec(tile, PAIR),
        ]
        + [row_spec(tile, 2 * K_WIDTH)] * len(parts),
        out_specs=[
            row_spec(tile, 2 * K_WIDTH),
            row_spec(tile, width),
            full_spec(1, width),
            full_spec(1, columns),
        ],
        out_shape=[
            jax.ShapeDtypeStruct((rows, 2 * K_WIDTH), bf16),
            jax.ShapeDtypeStruct((rows, width), f32),
            jax.ShapeDtypeStruct((1, width), f32),
            jax.ShapeDtypeStruct((1, columns), f32),
        ],
        cost_estimate=pl.CostEstimate(
            flops=4 * rows * width * columns, bytes_accessed=8 << 20, transcendentals=0
        ),
        compiler_params=params(),
        name="project_backward",
    )(grad_queries, weight, tokens, gain, grad_hidden, cosine, sine, *parts)


def owned_weights_kernel(ctx_size, normed_ref, gq_ref, gkv_ref, mixed_ref, hidden_ref, out_ref):
    grads = jnp.concatenate([gq_ref[...], gkv_ref[...]], axis=1)
    project = dot(normed_ref[...], grads, TN)
    output = dot(mixed_ref[...], hidden_ref[...], TN)
    first = project.shape[1] // ctx_size
    second = output.shape[1] // ctx_size
    own = first + second
    for rank in range(ctx_size):
        out_ref[:, rank * own : (rank + 1) * own] = jnp.concatenate(
            [
                project[:, rank * first : (rank + 1) * first],
                output[:, rank * second : (rank + 1) * second],
            ],
            axis=1,
        ).astype(bf16)


def owned_weights(ctx_size, normed, grad_queries, grad_pairs, mixed, hidden_low):
    rows, width = normed.shape
    columns = Q_WIDTH + 2 * K_WIDTH + hidden_low.shape[1]
    arrays = (normed, grad_queries, grad_pairs, mixed, hidden_low)
    return pl.pallas_call(
        functools.partial(owned_weights_kernel, ctx_size),
        grid=(1,),
        in_specs=[full_spec(*x.shape) for x in arrays],
        out_specs=full_spec(width, columns),
        out_shape=jax.ShapeDtypeStruct((width, columns), bf16),
        cost_estimate=pl.CostEstimate(
            flops=4 * rows * width * columns, bytes_accessed=8 << 20, transcendentals=0
        ),
        compiler_params=params(),
        name="owned_weights",
    )(*arrays)


def pair_sides(both):
    x, x_swapped = both[:, :PAIR], both[:, PAIR:]
    low = lax.broadcasted_iota(jnp.int32, x.shape, 1) < HEAD_DIM
    zero = jnp.zeros_like(x)
    left = (jnp.where(low, x, zero), jnp.where(low, x_swapped, zero))
    right = (jnp.where(low, zero, x_swapped), jnp.where(low, zero, x))
    sides = {}
    for pair in range(PAIRS):
        key = (2 * pair // GROUP, (2 * pair + 1) // GROUP)
        if key not in sides:
            sides[key] = jnp.concatenate([left[key[0]], right[key[1]]], axis=0)
    return sides


def causal(block):
    key_at = lax.broadcasted_iota(jnp.int32, (block, block), 0)
    query_at = lax.broadcasted_iota(jnp.int32, (block, block), 1)
    return key_at <= query_at


def forward_kernel(order_ref, q_ref, *rest):
    parts = rest[:-7]
    o_ref, lse_ref, keys_ref, turned_ref, top_ref, total_ref, acc_ref = rest[-7:]
    block = q_ref.shape[1]
    turn = pl.program_id(0) % 2
    last = order_ref[turn]

    @pl.when(turn == 0)
    def _():
        for number, part in enumerate(parts):
            for half in range(2):
                at = order_ref[2 * number + half]
                keys = part[0, half, :, :K_WIDTH]
                keys_ref[at, :, :PAIR] = keys
                keys_ref[at, :, PAIR:] = swap_pair(keys).astype(bf16)
                turned_ref[at] = jnp.transpose(part[0, half, :, K_WIDTH:].astype(f32)).astype(
                    bf16
                )

    top_ref[...] = jnp.full_like(top_ref, masked_value)
    total_ref[...] = jnp.zeros_like(total_ref)
    acc_ref[...] = jnp.zeros_like(acc_ref)
    scale = score_scale * log2_e

    def step(index, diagonal):
        sides = pair_sides(keys_ref[index])
        values = turned_ref[index]
        if diagonal:
            allowed = causal(block)
        for pair in range(PAIRS):
            both = dot(
                sides[(2 * pair // GROUP, (2 * pair + 1) // GROUP)],
                q_ref[0, :, pair * PAIR : (pair + 1) * PAIR],
                NT,
            )
            for odd in range(2):
                head = 2 * pair + odd
                kv = head // GROUP
                scores = both[odd * block : (odd + 1) * block] * scale
                if diagonal:
                    scores = jnp.where(allowed, scores, masked_value)
                old = top_ref[head : head + 1, :]
                new = jnp.maximum(old, jnp.max(scores, axis=0, keepdims=True))
                shrink = jnp.exp2(old - new)
                weights = jnp.exp2(scores - new)
                top_ref[head : head + 1, :] = new
                total_ref[head : head + 1, :] = total_ref[
                    head : head + 1, :
                ] * shrink + jnp.sum(weights, axis=0, keepdims=True)
                rows = slice(head * HEAD_DIM, (head + 1) * HEAD_DIM)
                acc_ref[rows, :] = acc_ref[rows, :] * shrink + dot(
                    values[kv * HEAD_DIM : (kv + 1) * HEAD_DIM], weights.astype(bf16), NN
                )

    def body(index, carry):
        step(index, False)
        return carry

    lax.fori_loop(0, last, body, 0)
    step(last, True)
    for pair in range(PAIRS):
        halves = []
        for odd in range(2):
            head = 2 * pair + odd
            halves.append(
                acc_ref[head * HEAD_DIM : (head + 1) * HEAD_DIM, :]
                / total_ref[head : head + 1, :]
            )
        o_ref[0, :, pair * PAIR : (pair + 1) * PAIR] = jnp.transpose(
            jnp.concatenate(halves, axis=0)
        ).astype(bf16)
    lse_ref[0] = top_ref[...] + jnp.log2(total_ref[...])


def backward_kernel(order_ref, q_ref, o_ref, g_ref, lse_ref, cos_ref, sin_ref, *rest):
    parts = rest[:-8]
    dq_ref, dkv_ref, keys_ref, values_ref, turned_ref, dk_ref, dv_ref, acc_ref = rest[-8:]
    block = q_ref.shape[1]
    turn = pl.program_id(0) % 2
    last = order_ref[turn]
    scale = score_scale * log2_e

    @pl.when(turn == 0)
    def _():
        dk_ref[...] = jnp.zeros_like(dk_ref)
        dv_ref[...] = jnp.zeros_like(dv_ref)
        for number, part in enumerate(parts):
            for half in range(2):
                at = order_ref[2 * number + half]
                keys = part[0, half, :, :K_WIDTH]
                values = part[0, half, :, K_WIDTH:]
                keys_ref[at, :, :PAIR] = keys
                keys_ref[at, :, PAIR:] = swap_pair(keys).astype(bf16)
                values_ref[at, :, :PAIR] = values
                values_ref[at, :, PAIR:] = swap_pair(values).astype(bf16)
                turned_ref[at] = jnp.transpose(keys.astype(f32)).astype(bf16)

    acc_ref[...] = jnp.zeros_like(acc_ref)
    product = g_ref[0].astype(f32) * o_ref[0].astype(f32)
    coarse = product.astype(bf16)
    fine = (product - coarse.astype(f32)).astype(bf16)
    head_of = lax.broadcasted_iota(jnp.int32, (16, Q_WIDTH), 1) // HEAD_DIM
    picks = (head_of == lax.broadcasted_iota(jnp.int32, (16, Q_WIDTH), 0)).astype(bf16)
    delta = dot(picks, coarse, NT) + dot(picks, fine, NT)

    def step(index, diagonal):
        key_sides = pair_sides(keys_ref[index])
        value_sides = pair_sides(values_ref[index])
        keys_turned = turned_ref[index]
        if diagonal:
            allowed = causal(block)
        key_sum = [[None, None], [None, None]]
        value_sum = [[None, None], [None, None]]

        def add(sums, odd, kv, part):
            sums[odd][kv] = part if sums[odd][kv] is None else sums[odd][kv] + part

        for pair in range(PAIRS):
            which = (2 * pair // GROUP, (2 * pair + 1) // GROUP)
            lanes = slice(pair * PAIR, (pair + 1) * PAIR)
            queries = q_ref[0, :, lanes]
            grads = g_ref[0, :, lanes]
            both = dot(key_sides[which], queries, NT)
            both_grads = dot(value_sides[which], grads, NT)
            low_weights = []
            low_scores = []
            for odd in range(2):
                head = 2 * pair + odd
                part = slice(odd * block, (odd + 1) * block)
                weights = jnp.exp2(both[part] * scale - lse_ref[0, head : head + 1, :])
                if diagonal:
                    weights = jnp.where(allowed, weights, 0.0)
                change = weights * (both_grads[part] - delta[head : head + 1, :])
                low_weights.append(weights.astype(bf16))
                low_scores.append(change.astype(bf16))
                rows = slice(head * HEAD_DIM, (head + 1) * HEAD_DIM)
                acc_ref[rows, :] += dot(
                    keys_turned[which[odd] * HEAD_DIM : (which[odd] + 1) * HEAD_DIM],
                    low_scores[odd],
                    NN,
                )
            value_part = dot(jnp.concatenate(low_weights, axis=0), grads, NN)
            key_part = dot(jnp.concatenate(low_scores, axis=0), queries, NN)
            for odd in range(2):
                part = slice(odd * block, (odd + 1) * block)
                add(value_sum, odd, which[odd], value_part[part])
                add(key_sum, odd, which[odd], key_part[part])
        low = lax.broadcasted_iota(jnp.int32, (block, PAIR), 1) < HEAD_DIM
        for sums, out_ref in ((key_sum, dk_ref), (value_sum, dv_ref)):
            out_ref[index, :, :PAIR] += jnp.where(low, sums[0][0], sums[1][1])
            out_ref[index, :, PAIR:] += jnp.where(low, sums[0][1], sums[1][0])

    def body(index, carry):
        step(index, False)
        return carry

    lax.fori_loop(0, last, body, 0)
    step(last, True)
    for pair in range(PAIRS):
        straight = jnp.transpose(acc_ref[pair * PAIR : (pair + 1) * PAIR, :]) * score_scale
        dq_ref[0, :, pair * PAIR : (pair + 1) * PAIR] = turn_pair(
            straight, cos_ref[0], -sin_ref[0]
        ).astype(bf16)

    @pl.when(turn == 1)
    def _():
        for slot in range(2 * len(parts)):
            at = order_ref[slot]
            keys = dk_ref[at, :, :PAIR] + swap_pair(dk_ref[at, :, PAIR:])
            dkv_ref[0, slot, :, :K_WIDTH] = (keys * score_scale).astype(bf16)
            values = dv_ref[at, :, :PAIR] + swap_pair(dv_ref[at, :, PAIR:])
            dkv_ref[0, slot, :, K_WIDTH:] = values.astype(bf16)


def attention_specs(block, parts):
    def rows(width):
        return pl.BlockSpec((1, block, width), lambda i, order: (i, 0, 0))

    def halves(number):
        return pl.BlockSpec((1, number, block, 2 * K_WIDTH), lambda i, order: (i // 2, 0, 0, 0))

    stats = pl.BlockSpec((1, 16, block), lambda i, order: (i, 0, 0))
    return rows, halves, stats


def attend_forward(order, queries, parts):
    count, block, _ = queries.shape
    slots = 2 * len(parts)
    rows, halves, stats = attention_specs(block, parts)
    pairs_done = count * block * (slots // 2 + 1) * block * HEADS
    return pl.pallas_call(
        forward_kernel,
        grid_spec=pltpu.PrefetchScalarGridSpec(
            num_scalar_prefetch=1,
            grid=(count,),
            in_specs=[rows(Q_WIDTH)] + [halves(2)] * len(parts),
            out_specs=[rows(Q_WIDTH), stats],
            scratch_shapes=[
                pltpu.VMEM((slots, block, 2 * PAIR), bf16),
                pltpu.VMEM((slots, PAIR, block), bf16),
                pltpu.VMEM((16, block), f32),
                pltpu.VMEM((16, block), f32),
                pltpu.VMEM((Q_WIDTH, block), f32),
            ],
        ),
        out_shape=[
            jax.ShapeDtypeStruct((count, block, Q_WIDTH), bf16),
            jax.ShapeDtypeStruct((count, 16, block), f32),
        ],
        cost_estimate=pl.CostEstimate(
            flops=pairs_done * 4 * 256, bytes_accessed=4 << 20, transcendentals=pairs_done
        ),
        compiler_params=params(),
        name="attend_forward",
    )(order, queries, *parts)


def attend_backward(order, queries, parts, mixed, grads, stats_in, cosine, sine):
    count, block, _ = queries.shape
    slots = 2 * len(parts)
    rows, halves, stats = attention_specs(block, parts)
    pairs_done = count * block * (slots // 2 + 1) * block * HEADS
    return pl.pallas_call(
        backward_kernel,
        grid_spec=pltpu.PrefetchScalarGridSpec(
            num_scalar_prefetch=1,
            grid=(count,),
            in_specs=[
                rows(Q_WIDTH),
                rows(Q_WIDTH),
                rows(Q_WIDTH),
                stats,
                rows(PAIR),
                rows(PAIR),
            ]
            + [halves(2)] * len(parts),
            out_specs=[rows(Q_WIDTH), halves(slots)],
            scratch_shapes=[
                pltpu.VMEM((slots, block, 2 * PAIR), bf16),
                pltpu.VMEM((slots, block, 2 * PAIR), bf16),
                pltpu.VMEM((slots, PAIR, block), bf16),
                pltpu.VMEM((slots, block, 2 * PAIR), f32),
                pltpu.VMEM((slots, block, 2 * PAIR), f32),
                pltpu.VMEM((Q_WIDTH, block), f32),
            ],
        ),
        out_shape=[
            jax.ShapeDtypeStruct((count, block, Q_WIDTH), bf16),
            jax.ShapeDtypeStruct((count // 2, slots, block, 2 * K_WIDTH), bf16),
        ],
        cost_estimate=pl.CostEstimate(
            flops=pairs_done * 10 * 256, bytes_accessed=8 << 20, transcendentals=pairs_done
        ),
        compiler_params=params(),
        name="attend_backward",
    )(order, queries, mixed, grads, stats_in, cosine, sine, *parts)


def ffn_kernel(x_low, x_high, c_low, c_high, w_ref, d_ref, *rest):
    out_ref, grad_ref, x_all, c_all, active_all, gate_all, up_all = rest[-7:]
    seq_size, _, depth, columns = w_ref.shape
    width = seq_size * depth
    low = pl.program_id(0) == 0
    x = jnp.where(low, x_low[...], x_high[...])
    c = jnp.where(low, c_low[...], c_high[...])
    x_all[0] = x
    c_all[0] = c
    gate_w = w_ref[:, 0].reshape(width, columns)
    up_w = w_ref[:, 1].reshape(width, columns)
    down_w = d_ref[...].reshape(width, columns)
    gate = dot(x, gate_w, NN)
    up = dot(x, up_w, NN)
    grad_active = dot(c, down_w, NN)
    sigmoid = jax.nn.sigmoid(gate)
    silu = gate * sigmoid
    active = (silu * up).astype(bf16)
    grad_gate = (grad_active * up * sigmoid * (1.0 + gate * (1.0 - sigmoid))).astype(bf16)
    grad_up = (grad_active * silu).astype(bf16)
    active_all[0] = active
    gate_all[0] = grad_gate
    up_all[0] = grad_up
    grad_ref[...] = (dot(grad_gate, gate_w, NT) + dot(grad_up, up_w, NT)).astype(bf16)
    out_ref[...] = dot(active, down_w, NT).astype(bf16)


def ffn(number, count, rows, halves, weights, down, buffers):
    width = halves[0][0].shape[1]
    columns = weights.shape[3]
    tile = rows // 2

    def half_spec(at):
        return pl.BlockSpec((tile, width), lambda i: (at, 0))

    def slot(columns):
        return pl.BlockSpec((1, tile, columns), lambda i: (number, i, 0))

    wide = jax.ShapeDtypeStruct((count, rows, width), bf16)
    inner = jax.ShapeDtypeStruct((count, rows, columns), bf16)
    return pl.pallas_call(
        ffn_kernel,
        grid=(2,),
        in_specs=[half_spec(at) for _, at in halves]
        + [full_spec(*weights.shape), full_spec(*down.shape)]
        + [pl.BlockSpec(memory_space=pl.ANY)] * len(buffers),
        out_specs=[row_spec(tile, width), row_spec(tile, width)]
        + [slot(width)] * 2
        + [slot(columns)] * 3,
        out_shape=[jax.ShapeDtypeStruct((rows, width), bf16)] * 2 + [wide] * 2 + [inner] * 3,
        input_output_aliases={6 + i: 2 + i for i in range(len(buffers))},
        cost_estimate=pl.CostEstimate(
            flops=14 * rows * width * columns, bytes_accessed=16 << 20, transcendentals=0
        ),
        compiler_params=params(),
        name="ffn",
    )(*[x for x, _ in halves], weights, down, *buffers)


def ffn_weights_kernel(x_ref, c_ref, active_ref, gate_ref, up_ref, out_ref, acc_ref):
    step = pl.program_id(0)
    seq_size, _, depth, columns = out_ref.shape

    @pl.when(step == 0)
    def _():
        acc_ref[...] = jnp.zeros_like(acc_ref)

    x = x_ref[0]
    acc_ref[0] += dot(x, gate_ref[0], TN)
    acc_ref[1] += dot(x, up_ref[0], TN)
    acc_ref[2] += dot(c_ref[0], active_ref[0], TN)

    @pl.when(step == pl.num_programs(0) - 1)
    def _():
        for which in range(3):
            out_ref[:, which] = acc_ref[which].reshape(seq_size, depth, columns).astype(bf16)


def ffn_weights(seq_size, x, c, active, grad_gate, grad_up):
    count, rows, width = x.shape
    columns = active.shape[2]

    def slot(columns):
        return pl.BlockSpec((1, rows, columns), lambda i: (i, 0, 0))

    shape = (seq_size, 3, width // seq_size, columns)
    return pl.pallas_call(
        ffn_weights_kernel,
        grid=(count,),
        in_specs=[slot(width)] * 2 + [slot(columns)] * 3,
        out_specs=pl.BlockSpec(shape, lambda i: (0, 0, 0, 0)),
        out_shape=jax.ShapeDtypeStruct(shape, bf16),
        scratch_shapes=[pltpu.VMEM((3, width, columns), f32)],
        cost_estimate=pl.CostEstimate(
            flops=6 * count * rows * width * columns, bytes_accessed=30 << 20, transcendentals=0
        ),
        compiler_params=params(),
        name="ffn_weights",
    )(x, c, active, grad_gate, grad_up)


def hop(x, ctx_size, mask):
    return lax.ppermute(x, "ctx", [(i, i ^ mask) for i in range(ctx_size)])


def others(x, ctx_size):
    return [hop(x, ctx_size, k) for k in range(1, ctx_size)]


def others_sum(parts, got):
    total = parts[0].astype(f32)
    for part in got:
        total = total + part.astype(f32)
    return total


def pick(index, cases):
    return cases[0] if len(cases) == 1 else lax.select_n(index, *cases)


def on_device(
    seq_size,
    ctx_size,
    tokens,
    attention_gain,
    project_weight,
    project_bias,
    output_weight,
    feedforward_gain,
    gate_weight,
    up_weight,
    down_weight,
    cotangent,
):
    sequences, block_rows, width = tokens.shape
    place = lax.axis_index("ctx")
    half = block_rows // 2
    rows = sequences * block_rows
    fold = seq_size // ctx_size
    seq_place = lax.axis_index("seq")
    fold_place = seq_place % fold
    core = seq_place % 2
    floor = seq_place // 2
    floors = seq_size // 2
    far = ctx_size - 1
    half_rows = rows // 2

    def to_rows(x):
        shape = (sequences, 2, half, x.shape[-1])
        return jnp.swapaxes(x.reshape(shape), 0, 1).reshape(rows, x.shape[-1])

    def to_blocks(x):
        shape = (2, sequences, half, x.shape[-1])
        return jnp.swapaxes(x.reshape(shape), 0, 1)

    def attention_blocks(x):
        return to_blocks(x).reshape(2 * sequences, half, x.shape[-1])

    def crossed(x, j):
        return lax.ppermute(
            x,
            ("seq", "ctx"),
            [
                ((c * fold + r) * ctx_size + q, (q * fold + (r + j) % fold) * ctx_size + c)
                for c in range(ctx_size)
                for r in range(fold)
                for q in range(ctx_size)
            ],
        )

    def send_crossed(parts):
        return [
            crossed(pick(fold_place, [parts[(f + j) % fold] for f in range(fold)]), j)
            for j in range(fold)
        ]

    def crossed_parts(came):
        return [
            pick(fold_place, [came[(f - t) % fold] for f in range(fold)]) for t in range(fold)
        ]

    def swap_second(x):
        return jnp.concatenate([x[:half_rows], hop(x[half_rows:], ctx_size, far)], axis=0)

    owners = [place ^ k for k in range(ctx_size)]
    order = jnp.stack(
        [spot for owner in owners for spot in (2 * owner, 2 * (ctx_size - 1 - owner) + 1)]
    ).astype(jnp.int32)
    positions = order[:2, None, None] * half + jnp.arange(half, dtype=jnp.int32)[None, None, :]
    positions = jnp.broadcast_to(positions, (2, sequences, half)).reshape(-1)
    cosine, sine = lax.optimization_barrier(rotation_tables(positions))

    def from_floors(x):
        came = [x] + [
            lax.ppermute(x, "seq", [(i, (i + 2 * step) % seq_size) for i in range(seq_size)])
            for step in range(1, floors)
        ]
        return jnp.concatenate(
            [
                pick(floor, [came[(mine - theirs) % floors] for mine in range(floors)])
                for theirs in range(floors)
            ],
            axis=0,
        )

    def from_ranks(x):
        return [x] + [hop(x, ctx_size, k) for k in range(1, ctx_size)]

    def by_rank(came):
        return [pick(place, [came[rank ^ p] for p in range(ctx_size)]) for rank in range(ctx_size)]

    def from_other_core(x):
        return lax.ppermute(x, "seq", [(i, i ^ 1) for i in range(seq_size)])

    def by_core(x, other):
        first, second = pick(core, [x, other]), pick(core, [other, x])
        shape = (floors, x.shape[0] // floors, x.shape[1])
        return jnp.stack([first.reshape(shape), second.reshape(shape)], axis=1).reshape(
            2 * x.shape[0], x.shape[1]
        )

    gate_up = lax.all_gather(jnp.stack([gate_weight, up_weight]), "seq", axis=0)
    gain_width = attention_gain.shape[0]
    own_width = project_weight.shape[1]
    vectors = jnp.concatenate([attention_gain, project_bias, feedforward_gain])
    spare = -vectors.shape[0] % own_width
    project_rows = from_floors(project_weight)
    held = project_rows.shape[0]
    tokens_mine = swap_second(to_rows(tokens))
    project_rows, tokens_mine = lax.optimization_barrier((project_rows, tokens_mine))
    project_came = from_ranks(
        jnp.concatenate(
            [project_rows, jnp.pad(vectors, (0, spare)).reshape(-1, own_width)], axis=0
        )
    )
    down_rows, down_columns = down_weight.shape
    depth = down_columns // fold
    down_late = lax.optimization_barrier((down_weight, project_came[1]))[0]
    down_came = send_crossed(list(down_late.T.reshape(fold, depth, down_rows)))
    output_late = lax.optimization_barrier((output_weight, project_rows))[0]
    output_rows = from_floors(output_late)
    ordered = by_rank(project_came)
    vectors_all = [piece[held:].reshape(-1).astype(f32) for piece in ordered]

    def vector_whole(start, size):
        return jnp.concatenate([v[start : start + size] for v in vectors_all])[None, :]

    attention_full = vector_whole(0, gain_width)
    bias_full = vector_whole(gain_width, own_width)
    feedforward_full = vector_whole(gain_width + own_width, gain_width)
    project_columns = jnp.concatenate([piece[:held] for piece in ordered], axis=1)
    project_other, down_came = lax.optimization_barrier(
        (from_other_core(project_columns), down_came)
    )
    project_full = by_core(project_columns, project_other)

    grad_late = lax.optimization_barrier((cotangent, project_full))[0]
    grad_rows = to_rows(grad_late)
    if ctx_size == 4:
        grad_near = [hop(grad_rows[:half_rows], 4, 1), hop(grad_rows[half_rows:], 4, 2)]
    else:
        grad_near = others(grad_rows, ctx_size)
    normed, queries, pairs_mine = project_forward(
        tokens_mine, attention_full, project_full, bias_full, cosine, sine
    )
    queries = attention_blocks(queries)
    pairs_mine = to_blocks(pairs_mine)
    pair_parts = [pairs_mine] + [hop(pairs_mine, ctx_size, k) for k in range(1, ctx_size)]
    grad_near, output_rows = lax.optimization_barrier((grad_near, output_rows, pair_parts))[:2]
    if ctx_size == 4:
        grad_far = [
            hop(jnp.concatenate([grad_rows[:half_rows], grad_near[0]], axis=0), 4, 2),
            hop(jnp.concatenate([grad_rows[half_rows:], grad_near[1]], axis=0), 4, 1),
        ]
    else:
        grad_far = []
    output_came = from_ranks(output_rows)
    down_came, gate_up, pair_parts = lax.optimization_barrier((down_came, gate_up, pair_parts))
    down_turned = jnp.concatenate(crossed_parts(down_came), axis=1)
    down_mine = lax.all_gather(down_turned, "seq", axis=0)
    queries = lax.optimization_barrier((queries, down_turned))[0]
    mixed, row_stats = attend_forward(order, queries, pair_parts)
    mixed, grad_far, output_came = lax.optimization_barrier((mixed, grad_far, output_came))
    if ctx_size == 4:
        firsts = [(grad_rows, 0), (grad_near[0], 0), (grad_far[0], 0), (grad_far[0], 1)]
        seconds = [(grad_rows, 1), (grad_far[1], 0), (grad_near[1], 0), (grad_far[1], 1)]
        own_second = grad_far[1][half_rows:]
    else:
        firsts = [(x, 0) for x in (grad_rows, *grad_near)]
        seconds = [(x, 1) for x in (grad_rows, *grad_near)]
        own_second = grad_near[far - 1][half_rows:]
    grad_low = jnp.concatenate([grad_rows[:half_rows], own_second], axis=0)
    output_columns = jnp.concatenate(by_rank(output_came), axis=1)
    output_full = by_core(output_columns, from_other_core(output_columns))
    mixed_rows = to_rows(mixed)
    hidden = tokens_mine.astype(f32) + dot(mixed_rows, output_full, NN)
    inverse_ffn = inverse_rms(hidden)
    normed_ffn = (hidden * inverse_ffn * feedforward_full).astype(bf16)

    normed_parts = [normed_ffn, *others(normed_ffn, ctx_size)]
    output_parts = []
    grad_normed_parts = []
    buffers = []
    for k, part in enumerate(normed_parts):
        output_part, grad_normed_part, *buffers = ffn(
            k,
            ctx_size,
            rows,
            [(part, 0), (part, 1), firsts[k], seconds[k ^ far]],
            gate_up,
            down_mine,
            buffers,
        )
        output_parts.append(output_part)
        grad_normed_parts.append(grad_normed_part)
    normed_got = [hop(grad_normed_parts[k], ctx_size, k) for k in range(1, ctx_size)]
    ffn_grads, normed_got = lax.optimization_barrier(
        (ffn_weights(seq_size, *buffers), normed_got)
    )
    grad_normed_ffn = others_sum(grad_normed_parts, normed_got)
    weight_grads = lax.psum_scatter(ffn_grads, "seq", scatter_dimension=0)

    grad_ffn_gain = jnp.sum(grad_normed_ffn * hidden * inverse_ffn, axis=0)
    weighted_ffn = grad_normed_ffn * feedforward_full
    grad_hidden = (
        grad_low.astype(f32)
        + inverse_ffn * weighted_ffn
        - hidden
        * inverse_ffn
        * inverse_ffn
        * inverse_ffn
        * jnp.mean(weighted_ffn * hidden, axis=-1, keepdims=True)
    )
    hidden_low = grad_hidden.astype(bf16)
    grad_mixed = dot(hidden_low, output_full, NT).astype(bf16)

    output_parts = lax.optimization_barrier((output_parts, grad_mixed))[0]
    output_got = [hop(output_parts[k], ctx_size, k) for k in range(1, ctx_size)]

    grad_queries, pair_grads = attend_backward(
        order,
        queries,
        pair_parts,
        mixed,
        attention_blocks(grad_mixed),
        row_stats,
        attention_blocks(cosine),
        attention_blocks(sine),
    )
    pair_grads, output_got = lax.optimization_barrier((pair_grads, output_got))
    pair_sums = [to_rows(pair_grads[:, :2])]
    for k in range(1, ctx_size):
        pair_sums.append(to_rows(hop(pair_grads[:, 2 * k : 2 * k + 2], ctx_size, k)))
    output_zigzag = hidden + others_sum(output_parts, output_got)
    grad_queries = to_rows(grad_queries)
    grad_pairs, tokens_grad, gain_sum, bias_sum = project_backward(
        grad_queries,
        project_full,
        tokens_mine,
        attention_full,
        grad_hidden,
        cosine,
        sine,
        pair_sums,
    )

    owned = lax.psum_scatter(
        owned_weights(ctx_size, normed, grad_queries, grad_pairs, mixed_rows, hidden_low),
        "seq",
        scatter_dimension=0,
        tiled=True,
    )

    layer_output = swap_second(output_zigzag.astype(bf16))
    tokens_gradient = jnp.concatenate(
        [
            tokens_grad[:half_rows],
            hop(tokens_grad[half_rows:].astype(bf16), ctx_size, far).astype(f32),
        ],
        axis=0,
    )
    sums = jnp.concatenate(
        [
            gain_sum.reshape(ctx_size, gain_width),
            bias_sum.reshape(ctx_size, own_width),
            grad_ffn_gain.reshape(ctx_size, gain_width),
        ],
        axis=1,
    )

    down_late = weight_grads[2].reshape(depth, fold, down_rows)
    grads_came = send_crossed([down_late[:, t] for t in range(fold)])
    sums, grads_came = lax.optimization_barrier((sums, grads_came))
    down_out = jnp.concatenate(crossed_parts(grads_came), axis=0).T

    def sums_for(k):
        return lax.dynamic_index_in_dim(sums, place ^ k, 0)

    vector_sum = sums_for(0)
    for k in range(1, ctx_size):
        vector_sum = vector_sum + hop(sums_for(k), ctx_size, k)
    mask = 1
    while mask < seq_size:
        vector_sum = vector_sum + lax.ppermute(
            vector_sum, "seq", [(i, i ^ mask) for i in range(seq_size)]
        )
        mask *= 2
    vector_sum = vector_sum[0]
    owned, layer_output, tokens_gradient, vector_sum, down_out = lax.optimization_barrier(
        (owned, layer_output, tokens_gradient, vector_sum, down_out)
    )
    own_columns = owned.shape[1] // ctx_size

    def owned_for(k):
        return lax.dynamic_slice_in_dim(owned, (place ^ k) * own_columns, own_columns, 1)

    owned_total = owned_for(0).astype(f32)
    for k in range(1, ctx_size):
        owned_total = owned_total + hop(owned_for(k), ctx_size, k).astype(f32)

    return (
        to_blocks(layer_output).reshape(tokens.shape),
        to_blocks(tokens_gradient).reshape(tokens.shape),
        vector_sum[:gain_width],
        owned_total[:, :own_width],
        vector_sum[gain_width : gain_width + own_width],
        owned_total[:, own_width:],
        vector_sum[gain_width + own_width : vectors.shape[0]],
        weight_grads[0].astype(f32),
        weight_grads[1].astype(f32),
        down_out.astype(f32),
    )


def solution(mesh):
    matrix = P("seq", "ctx")
    vector = P("ctx")
    activation = P("seq", "ctx", None)

    def step(*arrays):
        return on_device(mesh.shape["seq"], mesh.shape["ctx"], *arrays)

    return jax.shard_map(
        step,
        mesh=mesh,
        in_specs=(
            activation,
            vector,
            matrix,
            vector,
            matrix,
            vector,
            matrix,
            matrix,
            matrix,
            activation,
        ),
        out_specs=(
            activation,
            activation,
            vector,
            matrix,
            vector,
            matrix,
            vector,
            matrix,
            matrix,
            matrix,
        ),
        check_vma=False,
    )
```

```python
import functools
import math
import jax
import jax.numpy as jnp
from jax import lax
from jax.experimental import pallas as pl
from jax.experimental.pallas import tpu as pltpu
from jax.sharding import PartitionSpec as P

HEADS = 14
KV_HEADS = 2
HEAD_DIM = 64
GROUP = HEADS // KV_HEADS
PAIRS = HEADS // 2
PAIR = 2 * HEAD_DIM
Q_WIDTH = HEADS * HEAD_DIM
K_WIDTH = KV_HEADS * HEAD_DIM

norm_eps = 1e-06
rope_base = 1000000.0
masked_value = -1e30
score_scale = HEAD_DIM ** (-0.5)
log2_e = math.log2(math.e)
bf16 = jnp.bfloat16
f32 = jnp.float32


def inverse_rms(tensor):
    return lax.rsqrt(jnp.mean(tensor * tensor, axis=-1, keepdims=True) + norm_eps)


def dot(a, b, dims):
    return lax.dot_general(a, b, (dims, ((), ())), preferred_element_type=f32)


NN = ((1,), (0,))
NT = ((1,), (1,))
TN = ((0,), (0,))


def rotation_tables(positions):
    half_width = HEAD_DIM // 2
    steps_up = jnp.arange(half_width).astype(f32)
    frequency = jnp.power(jnp.asarray(rope_base, f32), -2.0 * steps_up / HEAD_DIM)
    angles = positions.astype(f32)[:, None] * frequency[None, :]
    cosine = jnp.cos(angles)
    sine = jnp.sin(angles)
    return (
        jnp.concatenate([cosine, cosine, cosine, cosine], axis=-1),
        jnp.concatenate([-sine, sine, -sine, sine], axis=-1),
    )


def turn_pair(x, cosine, sine):
    lane = lax.broadcasted_iota(jnp.int32, x.shape, 1)
    quarter = HEAD_DIM // 2
    other = jnp.where(
        (lane // quarter) % 2 == 0,
        pltpu.roll(x, PAIR - quarter, 1),
        pltpu.roll(x, quarter, 1),
    )
    return x * cosine + other * sine


def swap_pair(x):
    return pltpu.roll(x.astype(f32), HEAD_DIM, 1)


def params():
    return pltpu.CompilerParams(vmem_limit_bytes=60 << 20)


def project_kernel(x_ref, gain_ref, w_ref, bias_ref, cos_ref, sin_ref, normed_ref, q_ref, kv_ref):
    x = x_ref[...].astype(f32)
    normed = (x * inverse_rms(x) * gain_ref[...]).astype(bf16)
    normed_ref[...] = normed
    projected = dot(normed, w_ref[...], NN) + bias_ref[...]
    cosine = cos_ref[...]
    sine = sin_ref[...]
    for pair in range(PAIRS + 1):
        lanes = slice(pair * PAIR, (pair + 1) * PAIR)
        turned = turn_pair(projected[:, lanes], cosine, sine).astype(bf16)
        if pair < PAIRS:
            q_ref[:, lanes] = turned
        else:
            kv_ref[:, :K_WIDTH] = turned
    kv_ref[:, K_WIDTH:] = projected[:, Q_WIDTH + K_WIDTH :].astype(bf16)


def row_spec(tile, width):
    return pl.BlockSpec((tile, width), lambda i: (i, 0))


def full_spec(*shape):
    return pl.BlockSpec(shape, lambda i: (0,) * len(shape))


def project_forward(tokens, gain, weight, bias, cosine, sine):
    rows, width = tokens.shape
    tile = rows // 2
    columns = Q_WIDTH + 2 * K_WIDTH
    return pl.pallas_call(
        project_kernel,
        grid=(2,),
        in_specs=[
            row_spec(tile, width),
            full_spec(1, width),
            full_spec(width, columns),
            full_spec(1, columns),
            row_spec(tile, PAIR),
            row_spec(tile, PAIR),
        ],
        out_specs=[row_spec(tile, width), row_spec(tile, Q_WIDTH), row_spec(tile, 2 * K_WIDTH)],
        out_shape=[
            jax.ShapeDtypeStruct((rows, width), bf16),
            jax.ShapeDtypeStruct((rows, Q_WIDTH), bf16),
            jax.ShapeDtypeStruct((rows, 2 * K_WIDTH), bf16),
        ],
        cost_estimate=pl.CostEstimate(
            flops=4 * rows * width * columns, bytes_accessed=5 << 20, transcendentals=0
        ),
        compiler_params=params(),
        name="project_forward",
    )(tokens, gain, weight, bias, cosine, sine)


def project_back_kernel(
    gq_ref, w_ref, x_ref, gain_ref, hidden_ref, cos_ref, sin_ref, *rest
):
    parts = rest[:-4]
    gkv_ref, tokens_ref, gain_sum_ref, bias_sum_ref = rest[-4:]
    total = parts[0][...].astype(f32)
    for part in parts[1:]:
        total = total + part[...].astype(f32)
    turned = turn_pair(total[:, :K_WIDTH], cos_ref[...], -sin_ref[...]).astype(bf16)
    gkv_ref[:, :K_WIDTH] = turned
    gkv_ref[:, K_WIDTH:] = total[:, K_WIDTH:].astype(bf16)
    grads = jnp.concatenate([gq_ref[...], gkv_ref[...]], axis=1)
    grad_normed = dot(grads, w_ref[...], NT)
    x = x_ref[...].astype(f32)
    inverse = inverse_rms(x)
    weighted = grad_normed * gain_ref[...]
    tokens_ref[...] = (
        hidden_ref[...]
        + inverse * weighted
        - x * (inverse * inverse * inverse * jnp.mean(weighted * x, axis=-1, keepdims=True))
    )

    @pl.when(pl.program_id(0) == 0)
    def _():
        gain_sum_ref[...] = jnp.zeros_like(gain_sum_ref)
        bias_sum_ref[...] = jnp.zeros_like(bias_sum_ref)

    gain_sum_ref[...] += jnp.sum(grad_normed * x * inverse, axis=0, keepdims=True)
    bias_sum_ref[...] += jnp.sum(grads.astype(f32), axis=0, keepdims=True)


def project_backward(grad_queries, weight, tokens, gain, grad_hidden, cosine, sine, parts):
    rows, width = tokens.shape
    tile = rows // 2
    columns = Q_WIDTH + 2 * K_WIDTH
    return pl.pallas_call(
        project_back_kernel,
        grid=(2,),
        in_specs=[
            row_spec(tile, Q_WIDTH),
            full_spec(width, columns),
            row_spec(tile, width),
            full_spec(1, width),
            row_spec(tile, width),
            row_spec(tile, PAIR),
            row_spec(tile, PAIR),
        ]
        + [row_spec(tile, 2 * K_WIDTH)] * len(parts),
        out_specs=[
            row_spec(tile, 2 * K_WIDTH),
            row_spec(tile, width),
            full_spec(1, width),
            full_spec(1, columns),
        ],
        out_shape=[
            jax.ShapeDtypeStruct((rows, 2 * K_WIDTH), bf16),
            jax.ShapeDtypeStruct((rows, width), f32),
            jax.ShapeDtypeStruct((1, width), f32),
            jax.ShapeDtypeStruct((1, columns), f32),
        ],
        cost_estimate=pl.CostEstimate(
            flops=4 * rows * width * columns, bytes_accessed=8 << 20, transcendentals=0
        ),
        compiler_params=params(),
        name="project_backward",
    )(grad_queries, weight, tokens, gain, grad_hidden, cosine, sine, *parts)


def owned_weights_kernel(ctx_size, normed_ref, gq_ref, gkv_ref, mixed_ref, hidden_ref, out_ref):
    grads = jnp.concatenate([gq_ref[...], gkv_ref[...]], axis=1)
    project = dot(normed_ref[...], grads, TN)
    output = dot(mixed_ref[...], hidden_ref[...], TN)
    first = project.shape[1] // ctx_size
    second = output.shape[1] // ctx_size
    own = first + second
    for rank in range(ctx_size):
        out_ref[:, rank * own : (rank + 1) * own] = jnp.concatenate(
            [
                project[:, rank * first : (rank + 1) * first],
                output[:, rank * second : (rank + 1) * second],
            ],
            axis=1,
        ).astype(bf16)


def owned_weights(ctx_size, normed, grad_queries, grad_pairs, mixed, hidden_low):
    rows, width = normed.shape
    columns = Q_WIDTH + 2 * K_WIDTH + hidden_low.shape[1]
    arrays = (normed, grad_queries, grad_pairs, mixed, hidden_low)
    return pl.pallas_call(
        functools.partial(owned_weights_kernel, ctx_size),
        grid=(1,),
        in_specs=[full_spec(*x.shape) for x in arrays],
        out_specs=full_spec(width, columns),
        out_shape=jax.ShapeDtypeStruct((width, columns), bf16),
        cost_estimate=pl.CostEstimate(
            flops=4 * rows * width * columns, bytes_accessed=8 << 20, transcendentals=0
        ),
        compiler_params=params(),
        name="owned_weights",
    )(*arrays)


def pair_sides(both):
    x, x_swapped = both[:, :PAIR], both[:, PAIR:]
    low = lax.broadcasted_iota(jnp.int32, x.shape, 1) < HEAD_DIM
    zero = jnp.zeros_like(x)
    left = (jnp.where(low, x, zero), jnp.where(low, x_swapped, zero))
    right = (jnp.where(low, zero, x_swapped), jnp.where(low, zero, x))
    sides = {}
    for pair in range(PAIRS):
        key = (2 * pair // GROUP, (2 * pair + 1) // GROUP)
        if key not in sides:
            sides[key] = jnp.concatenate([left[key[0]], right[key[1]]], axis=0)
    return sides


def causal(block):
    key_at = lax.broadcasted_iota(jnp.int32, (block, block), 0)
    query_at = lax.broadcasted_iota(jnp.int32, (block, block), 1)
    return key_at <= query_at


def forward_kernel(order_ref, q_ref, *rest):
    parts = rest[:-7]
    o_ref, lse_ref, keys_ref, turned_ref, top_ref, total_ref, acc_ref = rest[-7:]
    block = q_ref.shape[1]
    turn = pl.program_id(0) % 2
    last = order_ref[turn]

    @pl.when(turn == 0)
    def _():
        for number, part in enumerate(parts):
            for half in range(2):
                at = order_ref[2 * number + half]
                keys = part[0, half, :, :K_WIDTH]
                keys_ref[at, :, :PAIR] = keys
                keys_ref[at, :, PAIR:] = swap_pair(keys).astype(bf16)
                turned_ref[at] = jnp.transpose(part[0, half, :, K_WIDTH:].astype(f32)).astype(
                    bf16
                )

    top_ref[...] = jnp.full_like(top_ref, masked_value)
    total_ref[...] = jnp.zeros_like(total_ref)
    acc_ref[...] = jnp.zeros_like(acc_ref)
    scale = score_scale * log2_e

    def step(index, diagonal):
        sides = pair_sides(keys_ref[index])
        values = turned_ref[index]
        if diagonal:
            allowed = causal(block)
        for pair in range(PAIRS):
            both = dot(
                sides[(2 * pair // GROUP, (2 * pair + 1) // GROUP)],
                q_ref[0, :, pair * PAIR : (pair + 1) * PAIR],
                NT,
            )
            for odd in range(2):
                head = 2 * pair + odd
                kv = head // GROUP
                scores = both[odd * block : (odd + 1) * block] * scale
                if diagonal:
                    scores = jnp.where(allowed, scores, masked_value)
                old = top_ref[head : head + 1, :]
                new = jnp.maximum(old, jnp.max(scores, axis=0, keepdims=True))
                shrink = jnp.exp2(old - new)
                weights = jnp.exp2(scores - new)
                top_ref[head : head + 1, :] = new
                total_ref[head : head + 1, :] = total_ref[
                    head : head + 1, :
                ] * shrink + jnp.sum(weights, axis=0, keepdims=True)
                rows = slice(head * HEAD_DIM, (head + 1) * HEAD_DIM)
                acc_ref[rows, :] = acc_ref[rows, :] * shrink + dot(
                    values[kv * HEAD_DIM : (kv + 1) * HEAD_DIM], weights.astype(bf16), NN
                )

    def body(index, carry):
        step(index, False)
        return carry

    lax.fori_loop(0, last, body, 0)
    step(last, True)
    for pair in range(PAIRS):
        halves = []
        for odd in range(2):
            head = 2 * pair + odd
            halves.append(
                acc_ref[head * HEAD_DIM : (head + 1) * HEAD_DIM, :]
                / total_ref[head : head + 1, :]
            )
        o_ref[0, :, pair * PAIR : (pair + 1) * PAIR] = jnp.transpose(
            jnp.concatenate(halves, axis=0)
        ).astype(bf16)
    lse_ref[0] = top_ref[...] + jnp.log2(total_ref[...])


def backward_kernel(order_ref, q_ref, o_ref, g_ref, lse_ref, cos_ref, sin_ref, *rest):
    parts = rest[:-8]
    dq_ref, dkv_ref, keys_ref, values_ref, turned_ref, dk_ref, dv_ref, acc_ref = rest[-8:]
    block = q_ref.shape[1]
    turn = pl.program_id(0) % 2
    last = order_ref[turn]
    scale = score_scale * log2_e

    @pl.when(turn == 0)
    def _():
        dk_ref[...] = jnp.zeros_like(dk_ref)
        dv_ref[...] = jnp.zeros_like(dv_ref)
        for number, part in enumerate(parts):
            for half in range(2):
                at = order_ref[2 * number + half]
                keys = part[0, half, :, :K_WIDTH]
                values = part[0, half, :, K_WIDTH:]
                keys_ref[at, :, :PAIR] = keys
                keys_ref[at, :, PAIR:] = swap_pair(keys).astype(bf16)
                values_ref[at, :, :PAIR] = values
                values_ref[at, :, PAIR:] = swap_pair(values).astype(bf16)
                turned_ref[at] = jnp.transpose(keys.astype(f32)).astype(bf16)

    acc_ref[...] = jnp.zeros_like(acc_ref)
    product = g_ref[0].astype(f32) * o_ref[0].astype(f32)
    coarse = product.astype(bf16)
    fine = (product - coarse.astype(f32)).astype(bf16)
    head_of = lax.broadcasted_iota(jnp.int32, (16, Q_WIDTH), 1) // HEAD_DIM
    picks = (head_of == lax.broadcasted_iota(jnp.int32, (16, Q_WIDTH), 0)).astype(bf16)
    delta = dot(picks, coarse, NT) + dot(picks, fine, NT)

    def step(index, diagonal):
        key_sides = pair_sides(keys_ref[index])
        value_sides = pair_sides(values_ref[index])
        keys_turned = turned_ref[index]
        if diagonal:
            allowed = causal(block)
        key_sum = [[None, None], [None, None]]
        value_sum = [[None, None], [None, None]]

        def add(sums, odd, kv, part):
            sums[odd][kv] = part if sums[odd][kv] is None else sums[odd][kv] + part

        for pair in range(PAIRS):
            which = (2 * pair // GROUP, (2 * pair + 1) // GROUP)
            lanes = slice(pair * PAIR, (pair + 1) * PAIR)
            queries = q_ref[0, :, lanes]
            grads = g_ref[0, :, lanes]
            both = dot(key_sides[which], queries, NT)
            both_grads = dot(value_sides[which], grads, NT)
            low_weights = []
            low_scores = []
            for odd in range(2):
                head = 2 * pair + odd
                part = slice(odd * block, (odd + 1) * block)
                weights = jnp.exp2(both[part] * scale - lse_ref[0, head : head + 1, :])
                if diagonal:
                    weights = jnp.where(allowed, weights, 0.0)
                change = weights * (both_grads[part] - delta[head : head + 1, :])
                low_weights.append(weights.astype(bf16))
                low_scores.append(change.astype(bf16))
                rows = slice(head * HEAD_DIM, (head + 1) * HEAD_DIM)
                acc_ref[rows, :] += dot(
                    keys_turned[which[odd] * HEAD_DIM : (which[odd] + 1) * HEAD_DIM],
                    low_scores[odd],
                    NN,
                )
            value_part = dot(jnp.concatenate(low_weights, axis=0), grads, NN)
            key_part = dot(jnp.concatenate(low_scores, axis=0), queries, NN)
            for odd in range(2):
                part = slice(odd * block, (odd + 1) * block)
                add(value_sum, odd, which[odd], value_part[part])
                add(key_sum, odd, which[odd], key_part[part])
        low = lax.broadcasted_iota(jnp.int32, (block, PAIR), 1) < HEAD_DIM
        for sums, out_ref in ((key_sum, dk_ref), (value_sum, dv_ref)):
            out_ref[index, :, :PAIR] += jnp.where(low, sums[0][0], sums[1][1])
            out_ref[index, :, PAIR:] += jnp.where(low, sums[0][1], sums[1][0])

    def body(index, carry):
        step(index, False)
        return carry

    lax.fori_loop(0, last, body, 0)
    step(last, True)
    for pair in range(PAIRS):
        straight = jnp.transpose(acc_ref[pair * PAIR : (pair + 1) * PAIR, :]) * score_scale
        dq_ref[0, :, pair * PAIR : (pair + 1) * PAIR] = turn_pair(
            straight, cos_ref[0], -sin_ref[0]
        ).astype(bf16)

    @pl.when(turn == 1)
    def _():
        for slot in range(2 * len(parts)):
            at = order_ref[slot]
            keys = dk_ref[at, :, :PAIR] + swap_pair(dk_ref[at, :, PAIR:])
            dkv_ref[0, slot, :, :K_WIDTH] = (keys * score_scale).astype(bf16)
            values = dv_ref[at, :, :PAIR] + swap_pair(dv_ref[at, :, PAIR:])
            dkv_ref[0, slot, :, K_WIDTH:] = values.astype(bf16)


def attention_specs(block, parts):
    def rows(width):
        return pl.BlockSpec((1, block, width), lambda i, order: (i, 0, 0))

    def halves(number):
        return pl.BlockSpec((1, number, block, 2 * K_WIDTH), lambda i, order: (i // 2, 0, 0, 0))

    stats = pl.BlockSpec((1, 16, block), lambda i, order: (i, 0, 0))
    return rows, halves, stats


def attend_forward(order, queries, parts):
    count, block, _ = queries.shape
    slots = 2 * len(parts)
    rows, halves, stats = attention_specs(block, parts)
    pairs_done = count * block * (slots // 2 + 1) * block * HEADS
    return pl.pallas_call(
        forward_kernel,
        grid_spec=pltpu.PrefetchScalarGridSpec(
            num_scalar_prefetch=1,
            grid=(count,),
            in_specs=[rows(Q_WIDTH)] + [halves(2)] * len(parts),
            out_specs=[rows(Q_WIDTH), stats],
            scratch_shapes=[
                pltpu.VMEM((slots, block, 2 * PAIR), bf16),
                pltpu.VMEM((slots, PAIR, block), bf16),
                pltpu.VMEM((16, block), f32),
                pltpu.VMEM((16, block), f32),
                pltpu.VMEM((Q_WIDTH, block), f32),
            ],
        ),
        out_shape=[
            jax.ShapeDtypeStruct((count, block, Q_WIDTH), bf16),
            jax.ShapeDtypeStruct((count, 16, block), f32),
        ],
        cost_estimate=pl.CostEstimate(
            flops=pairs_done * 4 * 256, bytes_accessed=4 << 20, transcendentals=pairs_done
        ),
        compiler_params=params(),
        name="attend_forward",
    )(order, queries, *parts)


def attend_backward(order, queries, parts, mixed, grads, stats_in, cosine, sine):
    count, block, _ = queries.shape
    slots = 2 * len(parts)
    rows, halves, stats = attention_specs(block, parts)
    pairs_done = count * block * (slots // 2 + 1) * block * HEADS
    return pl.pallas_call(
        backward_kernel,
        grid_spec=pltpu.PrefetchScalarGridSpec(
            num_scalar_prefetch=1,
            grid=(count,),
            in_specs=[
                rows(Q_WIDTH),
                rows(Q_WIDTH),
                rows(Q_WIDTH),
                stats,
                rows(PAIR),
                rows(PAIR),
            ]
            + [halves(2)] * len(parts),
            out_specs=[rows(Q_WIDTH), halves(slots)],
            scratch_shapes=[
                pltpu.VMEM((slots, block, 2 * PAIR), bf16),
                pltpu.VMEM((slots, block, 2 * PAIR), bf16),
                pltpu.VMEM((slots, PAIR, block), bf16),
                pltpu.VMEM((slots, block, 2 * PAIR), f32),
                pltpu.VMEM((slots, block, 2 * PAIR), f32),
                pltpu.VMEM((Q_WIDTH, block), f32),
            ],
        ),
        out_shape=[
            jax.ShapeDtypeStruct((count, block, Q_WIDTH), bf16),
            jax.ShapeDtypeStruct((count // 2, slots, block, 2 * K_WIDTH), bf16),
        ],
        cost_estimate=pl.CostEstimate(
            flops=pairs_done * 10 * 256, bytes_accessed=8 << 20, transcendentals=pairs_done
        ),
        compiler_params=params(),
        name="attend_backward",
    )(order, queries, mixed, grads, stats_in, cosine, sine, *parts)


def ffn_kernel(x_low, x_high, c_low, c_high, w_ref, d_ref, *rest):
    out_ref, grad_ref, x_all, c_all, active_all, gate_all, up_all = rest[-7:]
    seq_size, _, depth, columns = w_ref.shape
    width = seq_size * depth
    low = pl.program_id(0) == 0
    x = jnp.where(low, x_low[...], x_high[...])
    c = jnp.where(low, c_low[...], c_high[...])
    x_all[0] = x
    c_all[0] = c
    gate_w = w_ref[:, 0].reshape(width, columns)
    up_w = w_ref[:, 1].reshape(width, columns)
    down_w = d_ref[...].reshape(width, columns)
    gate = dot(x, gate_w, NN)
    up = dot(x, up_w, NN)
    grad_active = dot(c, down_w, NN)
    sigmoid = jax.nn.sigmoid(gate)
    silu = gate * sigmoid
    active = (silu * up).astype(bf16)
    grad_gate = (grad_active * up * sigmoid * (1.0 + gate * (1.0 - sigmoid))).astype(bf16)
    grad_up = (grad_active * silu).astype(bf16)
    active_all[0] = active
    gate_all[0] = grad_gate
    up_all[0] = grad_up
    grad_ref[...] = (dot(grad_gate, gate_w, NT) + dot(grad_up, up_w, NT)).astype(bf16)
    out_ref[...] = dot(active, down_w, NT).astype(bf16)


def ffn(number, count, rows, halves, weights, down, buffers):
    width = halves[0][0].shape[1]
    columns = weights.shape[3]
    tile = rows // 2

    def half_spec(at):
        return pl.BlockSpec((tile, width), lambda i: (at, 0))

    def slot(columns):
        return pl.BlockSpec((1, tile, columns), lambda i: (number, i, 0))

    wide = jax.ShapeDtypeStruct((count, rows, width), bf16)
    inner = jax.ShapeDtypeStruct((count, rows, columns), bf16)
    return pl.pallas_call(
        ffn_kernel,
        grid=(2,),
        in_specs=[half_spec(at) for _, at in halves]
        + [full_spec(*weights.shape), full_spec(*down.shape)]
        + [pl.BlockSpec(memory_space=pl.ANY)] * len(buffers),
        out_specs=[row_spec(tile, width), row_spec(tile, width)]
        + [slot(width)] * 2
        + [slot(columns)] * 3,
        out_shape=[jax.ShapeDtypeStruct((rows, width), bf16)] * 2 + [wide] * 2 + [inner] * 3,
        input_output_aliases={6 + i: 2 + i for i in range(len(buffers))},
        cost_estimate=pl.CostEstimate(
            flops=14 * rows * width * columns, bytes_accessed=16 << 20, transcendentals=0
        ),
        compiler_params=params(),
        name="ffn",
    )(*[x for x, _ in halves], weights, down, *buffers)


def ffn_weights_kernel(x_ref, c_ref, active_ref, gate_ref, up_ref, out_ref, acc_ref):
    step = pl.program_id(0)
    seq_size, _, depth, columns = out_ref.shape

    @pl.when(step == 0)
    def _():
        acc_ref[...] = jnp.zeros_like(acc_ref)

    x = x_ref[0]
    acc_ref[0] += dot(x, gate_ref[0], TN)
    acc_ref[1] += dot(x, up_ref[0], TN)
    acc_ref[2] += dot(c_ref[0], active_ref[0], TN)

    @pl.when(step == pl.num_programs(0) - 1)
    def _():
        for which in range(3):
            out_ref[:, which] = acc_ref[which].reshape(seq_size, depth, columns).astype(bf16)


def ffn_weights(seq_size, x, c, active, grad_gate, grad_up):
    count, rows, width = x.shape
    columns = active.shape[2]

    def slot(columns):
        return pl.BlockSpec((1, rows, columns), lambda i: (i, 0, 0))

    shape = (seq_size, 3, width // seq_size, columns)
    return pl.pallas_call(
        ffn_weights_kernel,
        grid=(count,),
        in_specs=[slot(width)] * 2 + [slot(columns)] * 3,
        out_specs=pl.BlockSpec(shape, lambda i: (0, 0, 0, 0)),
        out_shape=jax.ShapeDtypeStruct(shape, bf16),
        scratch_shapes=[pltpu.VMEM((3, width, columns), f32)],
        cost_estimate=pl.CostEstimate(
            flops=6 * count * rows * width * columns, bytes_accessed=30 << 20, transcendentals=0
        ),
        compiler_params=params(),
        name="ffn_weights",
    )(x, c, active, grad_gate, grad_up)


def hop(x, ctx_size, mask):
    return lax.ppermute(x, "ctx", [(i, i ^ mask) for i in range(ctx_size)])


def others(x, ctx_size):
    return [hop(x, ctx_size, k) for k in range(1, ctx_size)]


def others_sum(parts, got):
    total = parts[0].astype(f32)
    for part in got:
        total = total + part.astype(f32)
    return total


def pick(index, cases):
    return cases[0] if len(cases) == 1 else lax.select_n(index, *cases)


def on_device(
    seq_size,
    ctx_size,
    tokens,
    attention_gain,
    project_weight,
    project_bias,
    output_weight,
    feedforward_gain,
    gate_weight,
    up_weight,
    down_weight,
    cotangent,
):
    sequences, block_rows, width = tokens.shape
    place = lax.axis_index("ctx")
    half = block_rows // 2
    rows = sequences * block_rows
    fold = seq_size // ctx_size
    seq_place = lax.axis_index("seq")
    fold_place = seq_place % fold
    core = seq_place % 2
    floor = seq_place // 2
    floors = seq_size // 2
    far = ctx_size - 1
    half_rows = rows // 2

    def to_rows(x):
        shape = (sequences, 2, half, x.shape[-1])
        return jnp.swapaxes(x.reshape(shape), 0, 1).reshape(rows, x.shape[-1])

    def to_blocks(x):
        shape = (2, sequences, half, x.shape[-1])
        return jnp.swapaxes(x.reshape(shape), 0, 1)

    def attention_blocks(x):
        return to_blocks(x).reshape(2 * sequences, half, x.shape[-1])

    def crossed(x, j):
        return lax.ppermute(
            x,
            ("seq", "ctx"),
            [
                ((c * fold + r) * ctx_size + q, (q * fold + (r + j) % fold) * ctx_size + c)
                for c in range(ctx_size)
                for r in range(fold)
                for q in range(ctx_size)
            ],
        )

    def send_crossed(parts):
        return [
            crossed(pick(fold_place, [parts[(f + j) % fold] for f in range(fold)]), j)
            for j in range(fold)
        ]

    def crossed_parts(came):
        return [
            pick(fold_place, [came[(f - t) % fold] for f in range(fold)]) for t in range(fold)
        ]

    def swap_second(x):
        return jnp.concatenate([x[:half_rows], hop(x[half_rows:], ctx_size, far)], axis=0)

    owners = [place ^ k for k in range(ctx_size)]
    order = jnp.stack(
        [spot for owner in owners for spot in (2 * owner, 2 * (ctx_size - 1 - owner) + 1)]
    ).astype(jnp.int32)
    positions = order[:2, None, None] * half + jnp.arange(half, dtype=jnp.int32)[None, None, :]
    positions = jnp.broadcast_to(positions, (2, sequences, half)).reshape(-1)
    cosine, sine = lax.optimization_barrier(rotation_tables(positions))

    def from_floors(x):
        came = [x] + [
            lax.ppermute(x, "seq", [(i, (i + 2 * step) % seq_size) for i in range(seq_size)])
            for step in range(1, floors)
        ]
        return jnp.concatenate(
            [
                pick(floor, [came[(mine - theirs) % floors] for mine in range(floors)])
                for theirs in range(floors)
            ],
            axis=0,
        )

    def from_ranks(x):
        return [x] + [hop(x, ctx_size, k) for k in range(1, ctx_size)]

    def by_rank(came):
        return [pick(place, [came[rank ^ p] for p in range(ctx_size)]) for rank in range(ctx_size)]

    def from_other_core(x):
        return lax.ppermute(x, "seq", [(i, i ^ 1) for i in range(seq_size)])

    def by_core(x, other):
        first, second = pick(core, [x, other]), pick(core, [other, x])
        shape = (floors, x.shape[0] // floors, x.shape[1])
        return jnp.stack([first.reshape(shape), second.reshape(shape)], axis=1).reshape(
            2 * x.shape[0], x.shape[1]
        )

    gate_up = lax.all_gather(jnp.stack([gate_weight, up_weight]), "seq", axis=0)
    gain_width = attention_gain.shape[0]
    own_width = project_weight.shape[1]
    vectors = jnp.concatenate([attention_gain, project_bias, feedforward_gain])
    spare = -vectors.shape[0] % own_width
    project_rows = from_floors(project_weight)
    held = project_rows.shape[0]
    tokens_mine = swap_second(to_rows(tokens))
    grad_rows = to_rows(cotangent)
    if ctx_size == 4:
        grad_near = [hop(grad_rows[:half_rows], 4, 1), hop(grad_rows[half_rows:], 4, 2)]
    else:
        grad_near = others(grad_rows, ctx_size)
    project_came = from_ranks(
        jnp.concatenate(
            [project_rows, jnp.pad(vectors, (0, spare)).reshape(-1, own_width)], axis=0
        )
    )
    project_came, tokens_mine, grad_near = lax.optimization_barrier(
        (project_came, tokens_mine, grad_near)
    )
    output_late = lax.optimization_barrier((output_weight, project_rows))[0]
    output_rows = from_floors(output_late)
    ordered = by_rank(project_came)
    vectors_all = [piece[held:].reshape(-1).astype(f32) for piece in ordered]

    def vector_whole(start, size):
        return jnp.concatenate([v[start : start + size] for v in vectors_all])[None, :]

    attention_full = vector_whole(0, gain_width)
    bias_full = vector_whole(gain_width, own_width)
    feedforward_full = vector_whole(gain_width + own_width, gain_width)
    project_columns = jnp.concatenate([piece[:held] for piece in ordered], axis=1)
    project_full = by_core(project_columns, from_other_core(project_columns))

    down_late = lax.optimization_barrier((down_weight, project_full))[0]
    down_rows, down_columns = down_weight.shape
    depth = down_columns // fold
    down_came = send_crossed(list(down_late.T.reshape(fold, depth, down_rows)))

    normed, queries, pairs_mine = project_forward(
        tokens_mine, attention_full, project_full, bias_full, cosine, sine
    )
    queries = attention_blocks(queries)
    pairs_mine = to_blocks(pairs_mine)
    pair_parts = [pairs_mine] + [hop(pairs_mine, ctx_size, k) for k in range(1, ctx_size)]
    grad_near, output_rows = lax.optimization_barrier((grad_near, output_rows, pair_parts))[:2]
    if ctx_size == 4:
        grad_far = [
            hop(jnp.concatenate([grad_rows[:half_rows], grad_near[0]], axis=0), 4, 2),
            hop(jnp.concatenate([grad_rows[half_rows:], grad_near[1]], axis=0), 4, 1),
        ]
    else:
        grad_far = []
    down_came, gate_up, pair_parts = lax.optimization_barrier((down_came, gate_up, pair_parts))
    down_turned = jnp.concatenate(crossed_parts(down_came), axis=1)
    down_mine = lax.all_gather(down_turned, "seq", axis=0)
    queries = lax.optimization_barrier((queries, down_turned))[0]
    output_came = from_ranks(output_rows)
    mixed, row_stats = attend_forward(order, queries, pair_parts)
    mixed, grad_far, output_came = lax.optimization_barrier((mixed, grad_far, output_came))
    if ctx_size == 4:
        firsts = [(grad_rows, 0), (grad_near[0], 0), (grad_far[0], 0), (grad_far[0], 1)]
        seconds = [(grad_rows, 1), (grad_far[1], 0), (grad_near[1], 0), (grad_far[1], 1)]
        own_second = grad_far[1][half_rows:]
    else:
        firsts = [(x, 0) for x in (grad_rows, *grad_near)]
        seconds = [(x, 1) for x in (grad_rows, *grad_near)]
        own_second = grad_near[far - 1][half_rows:]
    grad_low = jnp.concatenate([grad_rows[:half_rows], own_second], axis=0)
    output_columns = jnp.concatenate(by_rank(output_came), axis=1)
    output_full = by_core(output_columns, from_other_core(output_columns))
    mixed_rows = to_rows(mixed)
    hidden = tokens_mine.astype(f32) + dot(mixed_rows, output_full, NN)
    inverse_ffn = inverse_rms(hidden)
    normed_ffn = (hidden * inverse_ffn * feedforward_full).astype(bf16)

    normed_parts = [normed_ffn, *others(normed_ffn, ctx_size)]
    output_parts = []
    grad_normed_parts = []
    buffers = []
    for k, part in enumerate(normed_parts):
        output_part, grad_normed_part, *buffers = ffn(
            k,
            ctx_size,
            rows,
            [(part, 0), (part, 1), firsts[k], seconds[k ^ far]],
            gate_up,
            down_mine,
            buffers,
        )
        output_parts.append(output_part)
        grad_normed_parts.append(grad_normed_part)
    normed_got = [hop(grad_normed_parts[k], ctx_size, k) for k in range(1, ctx_size)]
    ffn_grads, normed_got = lax.optimization_barrier(
        (ffn_weights(seq_size, *buffers), normed_got)
    )
    grad_normed_ffn = others_sum(grad_normed_parts, normed_got)
    weight_grads = lax.psum_scatter(ffn_grads, "seq", scatter_dimension=0)

    grad_ffn_gain = jnp.sum(grad_normed_ffn * hidden * inverse_ffn, axis=0)
    weighted_ffn = grad_normed_ffn * feedforward_full
    grad_hidden = (
        grad_low.astype(f32)
        + inverse_ffn * weighted_ffn
        - hidden
        * inverse_ffn
        * inverse_ffn
        * inverse_ffn
        * jnp.mean(weighted_ffn * hidden, axis=-1, keepdims=True)
    )
    hidden_low = grad_hidden.astype(bf16)
    grad_mixed = dot(hidden_low, output_full, NT).astype(bf16)

    output_parts = lax.optimization_barrier((output_parts, grad_mixed))[0]
    output_got = [hop(output_parts[k], ctx_size, k) for k in range(1, ctx_size)]

    grad_queries, pair_grads = attend_backward(
        order,
        queries,
        pair_parts,
        mixed,
        attention_blocks(grad_mixed),
        row_stats,
        attention_blocks(cosine),
        attention_blocks(sine),
    )
    pair_grads, output_got = lax.optimization_barrier((pair_grads, output_got))
    pair_sums = [to_rows(pair_grads[:, :2])]
    for k in range(1, ctx_size):
        pair_sums.append(to_rows(hop(pair_grads[:, 2 * k : 2 * k + 2], ctx_size, k)))
    output_zigzag = hidden + others_sum(output_parts, output_got)
    grad_queries = to_rows(grad_queries)
    grad_pairs, tokens_grad, gain_sum, bias_sum = project_backward(
        grad_queries,
        project_full,
        tokens_mine,
        attention_full,
        grad_hidden,
        cosine,
        sine,
        pair_sums,
    )

    owned = lax.psum_scatter(
        owned_weights(ctx_size, normed, grad_queries, grad_pairs, mixed_rows, hidden_low),
        "seq",
        scatter_dimension=0,
        tiled=True,
    )

    layer_output = swap_second(output_zigzag.astype(bf16))
    tokens_gradient = jnp.concatenate(
        [
            tokens_grad[:half_rows],
            hop(tokens_grad[half_rows:].astype(bf16), ctx_size, far).astype(f32),
        ],
        axis=0,
    )
    sums = jnp.concatenate(
        [
            gain_sum.reshape(ctx_size, gain_width),
            bias_sum.reshape(ctx_size, own_width),
            grad_ffn_gain.reshape(ctx_size, gain_width),
        ],
        axis=1,
    )

    def sums_for(k):
        return lax.dynamic_index_in_dim(sums, place ^ k, 0)

    vector_sum = sums_for(0)
    for k in range(1, ctx_size):
        vector_sum = vector_sum + hop(sums_for(k), ctx_size, k)
    mask = 1
    while mask < seq_size:
        vector_sum = vector_sum + lax.ppermute(
            vector_sum, "seq", [(i, i ^ mask) for i in range(seq_size)]
        )
        mask *= 2
    vector_sum = vector_sum[0]
    down_late = weight_grads[2].reshape(depth, fold, down_rows)
    grads_came = send_crossed([down_late[:, t] for t in range(fold)])
    down_out = jnp.concatenate(crossed_parts(grads_came), axis=0).T
    owned, layer_output, tokens_gradient, vector_sum, down_out = lax.optimization_barrier(
        (owned, layer_output, tokens_gradient, vector_sum, down_out)
    )
    own_columns = owned.shape[1] // ctx_size

    def owned_for(k):
        return lax.dynamic_slice_in_dim(owned, (place ^ k) * own_columns, own_columns, 1)

    owned_total = owned_for(0).astype(f32)
    for k in range(1, ctx_size):
        owned_total = owned_total + hop(owned_for(k), ctx_size, k).astype(f32)

    return (
        to_blocks(layer_output).reshape(tokens.shape),
        to_blocks(tokens_gradient).reshape(tokens.shape),
        vector_sum[:gain_width],
        owned_total[:, :own_width],
        vector_sum[gain_width : gain_width + own_width],
        owned_total[:, own_width:],
        vector_sum[gain_width + own_width : vectors.shape[0]],
        weight_grads[0].astype(f32),
        weight_grads[1].astype(f32),
        down_out.astype(f32),
    )


def solution(mesh):
    matrix = P("seq", "ctx")
    vector = P("ctx")
    activation = P("seq", "ctx", None)

    def step(*arrays):
        return on_device(mesh.shape["seq"], mesh.shape["ctx"], *arrays)

    return jax.shard_map(
        step,
        mesh=mesh,
        in_specs=(
            activation,
            vector,
            matrix,
            vector,
            matrix,
            vector,
            matrix,
            matrix,
            matrix,
            activation,
        ),
        out_specs=(
            activation,
            activation,
            vector,
            matrix,
            vector,
            matrix,
            vector,
            matrix,
            matrix,
            matrix,
        ),
        check_vma=False,
    )
```

```python
import functools
import math
import jax
import jax.numpy as jnp
from jax import lax
from jax.experimental import pallas as pl
from jax.experimental.pallas import tpu as pltpu
from jax.sharding import PartitionSpec as P

HEADS = 14
KV_HEADS = 2
HEAD_DIM = 64
GROUP = HEADS // KV_HEADS
PAIRS = HEADS // 2
PAIR = 2 * HEAD_DIM
Q_WIDTH = HEADS * HEAD_DIM
K_WIDTH = KV_HEADS * HEAD_DIM

norm_eps = 1e-06
rope_base = 1000000.0
masked_value = -1e30
score_scale = HEAD_DIM ** (-0.5)
log2_e = math.log2(math.e)
bf16 = jnp.bfloat16
f32 = jnp.float32


def inverse_rms(tensor):
    return lax.rsqrt(jnp.mean(tensor * tensor, axis=-1, keepdims=True) + norm_eps)


def dot(a, b, dims):
    return lax.dot_general(a, b, (dims, ((), ())), preferred_element_type=f32)


NN = ((1,), (0,))
NT = ((1,), (1,))
TN = ((0,), (0,))


def rotation_tables(positions):
    half_width = HEAD_DIM // 2
    steps_up = jnp.arange(half_width).astype(f32)
    frequency = jnp.power(jnp.asarray(rope_base, f32), -2.0 * steps_up / HEAD_DIM)
    angles = positions.astype(f32)[:, None] * frequency[None, :]
    cosine = jnp.cos(angles)
    sine = jnp.sin(angles)
    return (
        jnp.concatenate([cosine, cosine, cosine, cosine], axis=-1),
        jnp.concatenate([-sine, sine, -sine, sine], axis=-1),
    )


def turn_pair(x, cosine, sine):
    lane = lax.broadcasted_iota(jnp.int32, x.shape, 1)
    quarter = HEAD_DIM // 2
    other = jnp.where(
        (lane // quarter) % 2 == 0,
        pltpu.roll(x, PAIR - quarter, 1),
        pltpu.roll(x, quarter, 1),
    )
    return x * cosine + other * sine


def swap_pair(x):
    return pltpu.roll(x.astype(f32), HEAD_DIM, 1)


def params():
    return pltpu.CompilerParams(vmem_limit_bytes=60 << 20)


def project_kernel(x_ref, gain_ref, w_ref, bias_ref, cos_ref, sin_ref, normed_ref, q_ref, kv_ref):
    x = x_ref[...].astype(f32)
    normed = (x * inverse_rms(x) * gain_ref[...]).astype(bf16)
    normed_ref[...] = normed
    projected = dot(normed, w_ref[...], NN) + bias_ref[...]
    cosine = cos_ref[...]
    sine = sin_ref[...]
    for pair in range(PAIRS + 1):
        lanes = slice(pair * PAIR, (pair + 1) * PAIR)
        turned = turn_pair(projected[:, lanes], cosine, sine).astype(bf16)
        if pair < PAIRS:
            q_ref[:, lanes] = turned
        else:
            kv_ref[:, :K_WIDTH] = turned
    kv_ref[:, K_WIDTH:] = projected[:, Q_WIDTH + K_WIDTH :].astype(bf16)


def row_spec(tile, width):
    return pl.BlockSpec((tile, width), lambda i: (i, 0))


def full_spec(*shape):
    return pl.BlockSpec(shape, lambda i: (0,) * len(shape))


def project_forward(tokens, gain, weight, bias, cosine, sine):
    rows, width = tokens.shape
    tile = rows // 2
    columns = Q_WIDTH + 2 * K_WIDTH
    return pl.pallas_call(
        project_kernel,
        grid=(2,),
        in_specs=[
            row_spec(tile, width),
            full_spec(1, width),
            full_spec(width, columns),
            full_spec(1, columns),
            row_spec(tile, PAIR),
            row_spec(tile, PAIR),
        ],
        out_specs=[row_spec(tile, width), row_spec(tile, Q_WIDTH), row_spec(tile, 2 * K_WIDTH)],
        out_shape=[
            jax.ShapeDtypeStruct((rows, width), bf16),
            jax.ShapeDtypeStruct((rows, Q_WIDTH), bf16),
            jax.ShapeDtypeStruct((rows, 2 * K_WIDTH), bf16),
        ],
        cost_estimate=pl.CostEstimate(
            flops=4 * rows * width * columns, bytes_accessed=5 << 20, transcendentals=0
        ),
        compiler_params=params(),
        name="project_forward",
    )(tokens, gain, weight, bias, cosine, sine)


def project_back_kernel(
    gq_ref, w_ref, x_ref, gain_ref, hidden_ref, cos_ref, sin_ref, *rest
):
    parts = rest[:-4]
    gkv_ref, tokens_ref, gain_sum_ref, bias_sum_ref = rest[-4:]
    total = parts[0][...].astype(f32)
    for part in parts[1:]:
        total = total + part[...].astype(f32)
    turned = turn_pair(total[:, :K_WIDTH], cos_ref[...], -sin_ref[...]).astype(bf16)
    gkv_ref[:, :K_WIDTH] = turned
    gkv_ref[:, K_WIDTH:] = total[:, K_WIDTH:].astype(bf16)
    grads = jnp.concatenate([gq_ref[...], gkv_ref[...]], axis=1)
    grad_normed = dot(grads, w_ref[...], NT)
    x = x_ref[...].astype(f32)
    inverse = inverse_rms(x)
    weighted = grad_normed * gain_ref[...]
    tokens_ref[...] = (
        hidden_ref[...]
        + inverse * weighted
        - x * (inverse * inverse * inverse * jnp.mean(weighted * x, axis=-1, keepdims=True))
    )

    @pl.when(pl.program_id(0) == 0)
    def _():
        gain_sum_ref[...] = jnp.zeros_like(gain_sum_ref)
        bias_sum_ref[...] = jnp.zeros_like(bias_sum_ref)

    gain_sum_ref[...] += jnp.sum(grad_normed * x * inverse, axis=0, keepdims=True)
    bias_sum_ref[...] += jnp.sum(grads.astype(f32), axis=0, keepdims=True)


def project_backward(grad_queries, weight, tokens, gain, grad_hidden, cosine, sine, parts):
    rows, width = tokens.shape
    tile = rows // 2
    columns = Q_WIDTH + 2 * K_WIDTH
    return pl.pallas_call(
        project_back_kernel,
        grid=(2,),
        in_specs=[
            row_spec(tile, Q_WIDTH),
            full_spec(width, columns),
            row_spec(tile, width),
            full_spec(1, width),
            row_spec(tile, width),
            row_spec(tile, PAIR),
            row_spec(tile, PAIR),
        ]
        + [row_spec(tile, 2 * K_WIDTH)] * len(parts),
        out_specs=[
            row_spec(tile, 2 * K_WIDTH),
            row_spec(tile, width),
            full_spec(1, width),
            full_spec(1, columns),
        ],
        out_shape=[
            jax.ShapeDtypeStruct((rows, 2 * K_WIDTH), bf16),
            jax.ShapeDtypeStruct((rows, width), f32),
            jax.ShapeDtypeStruct((1, width), f32),
            jax.ShapeDtypeStruct((1, columns), f32),
        ],
        cost_estimate=pl.CostEstimate(
            flops=4 * rows * width * columns, bytes_accessed=8 << 20, transcendentals=0
        ),
        compiler_params=params(),
        name="project_backward",
    )(grad_queries, weight, tokens, gain, grad_hidden, cosine, sine, *parts)


def owned_weights_kernel(ctx_size, normed_ref, gq_ref, gkv_ref, mixed_ref, hidden_ref, out_ref):
    grads = jnp.concatenate([gq_ref[...], gkv_ref[...]], axis=1)
    project = dot(normed_ref[...], grads, TN)
    output = dot(mixed_ref[...], hidden_ref[...], TN)
    first = project.shape[1] // ctx_size
    second = output.shape[1] // ctx_size
    own = first + second
    for rank in range(ctx_size):
        out_ref[:, rank * own : (rank + 1) * own] = jnp.concatenate(
            [
                project[:, rank * first : (rank + 1) * first],
                output[:, rank * second : (rank + 1) * second],
            ],
            axis=1,
        ).astype(bf16)


def owned_weights(ctx_size, normed, grad_queries, grad_pairs, mixed, hidden_low):
    rows, width = normed.shape
    columns = Q_WIDTH + 2 * K_WIDTH + hidden_low.shape[1]
    arrays = (normed, grad_queries, grad_pairs, mixed, hidden_low)
    return pl.pallas_call(
        functools.partial(owned_weights_kernel, ctx_size),
        grid=(1,),
        in_specs=[full_spec(*x.shape) for x in arrays],
        out_specs=full_spec(width, columns),
        out_shape=jax.ShapeDtypeStruct((width, columns), bf16),
        cost_estimate=pl.CostEstimate(
            flops=4 * rows * width * columns, bytes_accessed=8 << 20, transcendentals=0
        ),
        compiler_params=params(),
        name="owned_weights",
    )(*arrays)


def pair_sides(both):
    x, x_swapped = both[:, :PAIR], both[:, PAIR:]
    low = lax.broadcasted_iota(jnp.int32, x.shape, 1) < HEAD_DIM
    zero = jnp.zeros_like(x)
    left = (jnp.where(low, x, zero), jnp.where(low, x_swapped, zero))
    right = (jnp.where(low, zero, x_swapped), jnp.where(low, zero, x))
    sides = {}
    for pair in range(PAIRS):
        key = (2 * pair // GROUP, (2 * pair + 1) // GROUP)
        if key not in sides:
            sides[key] = jnp.concatenate([left[key[0]], right[key[1]]], axis=0)
    return sides


def causal(block):
    key_at = lax.broadcasted_iota(jnp.int32, (block, block), 0)
    query_at = lax.broadcasted_iota(jnp.int32, (block, block), 1)
    return key_at <= query_at


def forward_kernel(order_ref, q_ref, *rest):
    parts = rest[:-7]
    o_ref, lse_ref, keys_ref, turned_ref, top_ref, total_ref, acc_ref = rest[-7:]
    block = q_ref.shape[1]
    turn = pl.program_id(0) % 2
    last = order_ref[turn]

    @pl.when(turn == 0)
    def _():
        for number, part in enumerate(parts):
            for half in range(2):
                at = order_ref[2 * number + half]
                keys = part[0, half, :, :K_WIDTH]
                keys_ref[at, :, :PAIR] = keys
                keys_ref[at, :, PAIR:] = swap_pair(keys).astype(bf16)
                turned_ref[at] = jnp.transpose(part[0, half, :, K_WIDTH:].astype(f32)).astype(
                    bf16
                )

    top_ref[...] = jnp.full_like(top_ref, masked_value)
    total_ref[...] = jnp.zeros_like(total_ref)
    acc_ref[...] = jnp.zeros_like(acc_ref)
    scale = score_scale * log2_e

    def step(index, diagonal):
        sides = pair_sides(keys_ref[index])
        values = turned_ref[index]
        if diagonal:
            allowed = causal(block)
        for pair in range(PAIRS):
            both = dot(
                sides[(2 * pair // GROUP, (2 * pair + 1) // GROUP)],
                q_ref[0, :, pair * PAIR : (pair + 1) * PAIR],
                NT,
            )
            for odd in range(2):
                head = 2 * pair + odd
                kv = head // GROUP
                scores = both[odd * block : (odd + 1) * block] * scale
                if diagonal:
                    scores = jnp.where(allowed, scores, masked_value)
                old = top_ref[head : head + 1, :]
                new = jnp.maximum(old, jnp.max(scores, axis=0, keepdims=True))
                shrink = jnp.exp2(old - new)
                weights = jnp.exp2(scores - new)
                top_ref[head : head + 1, :] = new
                total_ref[head : head + 1, :] = total_ref[
                    head : head + 1, :
                ] * shrink + jnp.sum(weights, axis=0, keepdims=True)
                rows = slice(head * HEAD_DIM, (head + 1) * HEAD_DIM)
                acc_ref[rows, :] = acc_ref[rows, :] * shrink + dot(
                    values[kv * HEAD_DIM : (kv + 1) * HEAD_DIM], weights.astype(bf16), NN
                )

    def body(index, carry):
        step(index, False)
        return carry

    lax.fori_loop(0, last, body, 0)
    step(last, True)
    for pair in range(PAIRS):
        halves = []
        for odd in range(2):
            head = 2 * pair + odd
            halves.append(
                acc_ref[head * HEAD_DIM : (head + 1) * HEAD_DIM, :]
                / total_ref[head : head + 1, :]
            )
        o_ref[0, :, pair * PAIR : (pair + 1) * PAIR] = jnp.transpose(
            jnp.concatenate(halves, axis=0)
        ).astype(bf16)
    lse_ref[0] = top_ref[...] + jnp.log2(total_ref[...])


def backward_kernel(order_ref, q_ref, o_ref, g_ref, lse_ref, cos_ref, sin_ref, *rest):
    parts = rest[:-8]
    dq_ref, dkv_ref, keys_ref, values_ref, turned_ref, dk_ref, dv_ref, acc_ref = rest[-8:]
    block = q_ref.shape[1]
    turn = pl.program_id(0) % 2
    last = order_ref[turn]
    scale = score_scale * log2_e

    @pl.when(turn == 0)
    def _():
        dk_ref[...] = jnp.zeros_like(dk_ref)
        dv_ref[...] = jnp.zeros_like(dv_ref)
        for number, part in enumerate(parts):
            for half in range(2):
                at = order_ref[2 * number + half]
                keys = part[0, half, :, :K_WIDTH]
                values = part[0, half, :, K_WIDTH:]
                keys_ref[at, :, :PAIR] = keys
                keys_ref[at, :, PAIR:] = swap_pair(keys).astype(bf16)
                values_ref[at, :, :PAIR] = values
                values_ref[at, :, PAIR:] = swap_pair(values).astype(bf16)
                turned_ref[at] = jnp.transpose(keys.astype(f32)).astype(bf16)

    acc_ref[...] = jnp.zeros_like(acc_ref)
    product = g_ref[0].astype(f32) * o_ref[0].astype(f32)
    coarse = product.astype(bf16)
    fine = (product - coarse.astype(f32)).astype(bf16)
    head_of = lax.broadcasted_iota(jnp.int32, (16, Q_WIDTH), 1) // HEAD_DIM
    picks = (head_of == lax.broadcasted_iota(jnp.int32, (16, Q_WIDTH), 0)).astype(bf16)
    delta = dot(picks, coarse, NT) + dot(picks, fine, NT)

    def step(index, diagonal):
        key_sides = pair_sides(keys_ref[index])
        value_sides = pair_sides(values_ref[index])
        keys_turned = turned_ref[index]
        if diagonal:
            allowed = causal(block)
        key_sum = [[None, None], [None, None]]
        value_sum = [[None, None], [None, None]]

        def add(sums, odd, kv, part):
            sums[odd][kv] = part if sums[odd][kv] is None else sums[odd][kv] + part

        for pair in range(PAIRS):
            which = (2 * pair // GROUP, (2 * pair + 1) // GROUP)
            lanes = slice(pair * PAIR, (pair + 1) * PAIR)
            queries = q_ref[0, :, lanes]
            grads = g_ref[0, :, lanes]
            both = dot(key_sides[which], queries, NT)
            both_grads = dot(value_sides[which], grads, NT)
            low_weights = []
            low_scores = []
            for odd in range(2):
                head = 2 * pair + odd
                part = slice(odd * block, (odd + 1) * block)
                weights = jnp.exp2(both[part] * scale - lse_ref[0, head : head + 1, :])
                if diagonal:
                    weights = jnp.where(allowed, weights, 0.0)
                change = weights * (both_grads[part] - delta[head : head + 1, :])
                low_weights.append(weights.astype(bf16))
                low_scores.append(change.astype(bf16))
                rows = slice(head * HEAD_DIM, (head + 1) * HEAD_DIM)
                acc_ref[rows, :] += dot(
                    keys_turned[which[odd] * HEAD_DIM : (which[odd] + 1) * HEAD_DIM],
                    low_scores[odd],
                    NN,
                )
            value_part = dot(jnp.concatenate(low_weights, axis=0), grads, NN)
            key_part = dot(jnp.concatenate(low_scores, axis=0), queries, NN)
            for odd in range(2):
                part = slice(odd * block, (odd + 1) * block)
                add(value_sum, odd, which[odd], value_part[part])
                add(key_sum, odd, which[odd], key_part[part])
        low = lax.broadcasted_iota(jnp.int32, (block, PAIR), 1) < HEAD_DIM
        for sums, out_ref in ((key_sum, dk_ref), (value_sum, dv_ref)):
            out_ref[index, :, :PAIR] += jnp.where(low, sums[0][0], sums[1][1])
            out_ref[index, :, PAIR:] += jnp.where(low, sums[0][1], sums[1][0])

    def body(index, carry):
        step(index, False)
        return carry

    lax.fori_loop(0, last, body, 0)
    step(last, True)
    for pair in range(PAIRS):
        straight = jnp.transpose(acc_ref[pair * PAIR : (pair + 1) * PAIR, :]) * score_scale
        dq_ref[0, :, pair * PAIR : (pair + 1) * PAIR] = turn_pair(
            straight, cos_ref[0], -sin_ref[0]
        ).astype(bf16)

    @pl.when(turn == 1)
    def _():
        for slot in range(2 * len(parts)):
            at = order_ref[slot]
            keys = dk_ref[at, :, :PAIR] + swap_pair(dk_ref[at, :, PAIR:])
            dkv_ref[0, slot, :, :K_WIDTH] = (keys * score_scale).astype(bf16)
            values = dv_ref[at, :, :PAIR] + swap_pair(dv_ref[at, :, PAIR:])
            dkv_ref[0, slot, :, K_WIDTH:] = values.astype(bf16)


def attention_specs(block, parts):
    def rows(width):
        return pl.BlockSpec((1, block, width), lambda i, order: (i, 0, 0))

    def halves(number):
        return pl.BlockSpec((1, number, block, 2 * K_WIDTH), lambda i, order: (i // 2, 0, 0, 0))

    stats = pl.BlockSpec((1, 16, block), lambda i, order: (i, 0, 0))
    return rows, halves, stats


def attend_forward(order, queries, parts):
    count, block, _ = queries.shape
    slots = 2 * len(parts)
    rows, halves, stats = attention_specs(block, parts)
    pairs_done = count * block * (slots // 2 + 1) * block * HEADS
    return pl.pallas_call(
        forward_kernel,
        grid_spec=pltpu.PrefetchScalarGridSpec(
            num_scalar_prefetch=1,
            grid=(count,),
            in_specs=[rows(Q_WIDTH)] + [halves(2)] * len(parts),
            out_specs=[rows(Q_WIDTH), stats],
            scratch_shapes=[
                pltpu.VMEM((slots, block, 2 * PAIR), bf16),
                pltpu.VMEM((slots, PAIR, block), bf16),
                pltpu.VMEM((16, block), f32),
                pltpu.VMEM((16, block), f32),
                pltpu.VMEM((Q_WIDTH, block), f32),
            ],
        ),
        out_shape=[
            jax.ShapeDtypeStruct((count, block, Q_WIDTH), bf16),
            jax.ShapeDtypeStruct((count, 16, block), f32),
        ],
        cost_estimate=pl.CostEstimate(
            flops=pairs_done * 4 * 256, bytes_accessed=4 << 20, transcendentals=pairs_done
        ),
        compiler_params=params(),
        name="attend_forward",
    )(order, queries, *parts)


def attend_backward(order, queries, parts, mixed, grads, stats_in, cosine, sine):
    count, block, _ = queries.shape
    slots = 2 * len(parts)
    rows, halves, stats = attention_specs(block, parts)
    pairs_done = count * block * (slots // 2 + 1) * block * HEADS
    return pl.pallas_call(
        backward_kernel,
        grid_spec=pltpu.PrefetchScalarGridSpec(
            num_scalar_prefetch=1,
            grid=(count,),
            in_specs=[
                rows(Q_WIDTH),
                rows(Q_WIDTH),
                rows(Q_WIDTH),
                stats,
                rows(PAIR),
                rows(PAIR),
            ]
            + [halves(2)] * len(parts),
            out_specs=[rows(Q_WIDTH), halves(slots)],
            scratch_shapes=[
                pltpu.VMEM((slots, block, 2 * PAIR), bf16),
                pltpu.VMEM((slots, block, 2 * PAIR), bf16),
                pltpu.VMEM((slots, PAIR, block), bf16),
                pltpu.VMEM((slots, block, 2 * PAIR), f32),
                pltpu.VMEM((slots, block, 2 * PAIR), f32),
                pltpu.VMEM((Q_WIDTH, block), f32),
            ],
        ),
        out_shape=[
            jax.ShapeDtypeStruct((count, block, Q_WIDTH), bf16),
            jax.ShapeDtypeStruct((count // 2, slots, block, 2 * K_WIDTH), bf16),
        ],
        cost_estimate=pl.CostEstimate(
            flops=pairs_done * 10 * 256, bytes_accessed=8 << 20, transcendentals=pairs_done
        ),
        compiler_params=params(),
        name="attend_backward",
    )(order, queries, mixed, grads, stats_in, cosine, sine, *parts)


def ffn_kernel(x_low, x_high, c_low, c_high, w_ref, d_ref, *rest):
    out_ref, grad_ref, x_all, c_all, active_all, gate_all, up_all = rest[-7:]
    seq_size, _, depth, columns = w_ref.shape
    width = seq_size * depth
    low = pl.program_id(0) == 0
    x = jnp.where(low, x_low[...], x_high[...])
    c = jnp.where(low, c_low[...], c_high[...])
    x_all[0] = x
    c_all[0] = c
    gate_w = w_ref[:, 0].reshape(width, columns)
    up_w = w_ref[:, 1].reshape(width, columns)
    down_w = d_ref[...].reshape(width, columns)
    gate = dot(x, gate_w, NN)
    up = dot(x, up_w, NN)
    grad_active = dot(c, down_w, NN)
    sigmoid = jax.nn.sigmoid(gate)
    silu = gate * sigmoid
    active = (silu * up).astype(bf16)
    grad_gate = (grad_active * up * sigmoid * (1.0 + gate * (1.0 - sigmoid))).astype(bf16)
    grad_up = (grad_active * silu).astype(bf16)
    active_all[0] = active
    gate_all[0] = grad_gate
    up_all[0] = grad_up
    grad_ref[...] = (dot(grad_gate, gate_w, NT) + dot(grad_up, up_w, NT)).astype(bf16)
    out_ref[...] = dot(active, down_w, NT).astype(bf16)


def ffn(number, count, rows, halves, weights, down, buffers):
    width = halves[0][0].shape[1]
    columns = weights.shape[3]
    tile = rows // 2

    def half_spec(at):
        return pl.BlockSpec((tile, width), lambda i: (at, 0))

    def slot(columns):
        return pl.BlockSpec((1, tile, columns), lambda i: (number, i, 0))

    wide = jax.ShapeDtypeStruct((count, rows, width), bf16)
    inner = jax.ShapeDtypeStruct((count, rows, columns), bf16)
    return pl.pallas_call(
        ffn_kernel,
        grid=(2,),
        in_specs=[half_spec(at) for _, at in halves]
        + [full_spec(*weights.shape), full_spec(*down.shape)]
        + [pl.BlockSpec(memory_space=pl.ANY)] * len(buffers),
        out_specs=[row_spec(tile, width), row_spec(tile, width)]
        + [slot(width)] * 2
        + [slot(columns)] * 3,
        out_shape=[jax.ShapeDtypeStruct((rows, width), bf16)] * 2 + [wide] * 2 + [inner] * 3,
        input_output_aliases={6 + i: 2 + i for i in range(len(buffers))},
        cost_estimate=pl.CostEstimate(
            flops=14 * rows * width * columns, bytes_accessed=16 << 20, transcendentals=0
        ),
        compiler_params=params(),
        name="ffn",
    )(*[x for x, _ in halves], weights, down, *buffers)


def ffn_weights_kernel(x_ref, c_ref, active_ref, gate_ref, up_ref, out_ref, acc_ref):
    step = pl.program_id(0)
    seq_size, _, depth, columns = out_ref.shape

    @pl.when(step == 0)
    def _():
        acc_ref[...] = jnp.zeros_like(acc_ref)

    x = x_ref[0]
    acc_ref[0] += dot(x, gate_ref[0], TN)
    acc_ref[1] += dot(x, up_ref[0], TN)
    acc_ref[2] += dot(c_ref[0], active_ref[0], TN)

    @pl.when(step == pl.num_programs(0) - 1)
    def _():
        for which in range(3):
            out_ref[:, which] = acc_ref[which].reshape(seq_size, depth, columns).astype(bf16)


def ffn_weights(seq_size, x, c, active, grad_gate, grad_up):
    count, rows, width = x.shape
    columns = active.shape[2]

    def slot(columns):
        return pl.BlockSpec((1, rows, columns), lambda i: (i, 0, 0))

    shape = (seq_size, 3, width // seq_size, columns)
    return pl.pallas_call(
        ffn_weights_kernel,
        grid=(count,),
        in_specs=[slot(width)] * 2 + [slot(columns)] * 3,
        out_specs=pl.BlockSpec(shape, lambda i: (0, 0, 0, 0)),
        out_shape=jax.ShapeDtypeStruct(shape, bf16),
        scratch_shapes=[pltpu.VMEM((3, width, columns), f32)],
        cost_estimate=pl.CostEstimate(
            flops=6 * count * rows * width * columns, bytes_accessed=30 << 20, transcendentals=0
        ),
        compiler_params=params(),
        name="ffn_weights",
    )(x, c, active, grad_gate, grad_up)


def hop(x, ctx_size, mask):
    return lax.ppermute(x, "ctx", [(i, i ^ mask) for i in range(ctx_size)])


def others(x, ctx_size):
    return [hop(x, ctx_size, k) for k in range(1, ctx_size)]


def others_sum(parts, got):
    total = parts[0].astype(f32)
    for part in got:
        total = total + part.astype(f32)
    return total


def pick(index, cases):
    return cases[0] if len(cases) == 1 else lax.select_n(index, *cases)


def on_device(
    seq_size,
    ctx_size,
    tokens,
    attention_gain,
    project_weight,
    project_bias,
    output_weight,
    feedforward_gain,
    gate_weight,
    up_weight,
    down_weight,
    cotangent,
):
    sequences, block_rows, width = tokens.shape
    place = lax.axis_index("ctx")
    half = block_rows // 2
    rows = sequences * block_rows
    fold = seq_size // ctx_size
    seq_place = lax.axis_index("seq")
    fold_place = seq_place % fold
    core = seq_place % 2
    floor = seq_place // 2
    floors = seq_size // 2
    far = ctx_size - 1
    half_rows = rows // 2

    def to_rows(x):
        shape = (sequences, 2, half, x.shape[-1])
        return jnp.swapaxes(x.reshape(shape), 0, 1).reshape(rows, x.shape[-1])

    def to_blocks(x):
        shape = (2, sequences, half, x.shape[-1])
        return jnp.swapaxes(x.reshape(shape), 0, 1)

    def attention_blocks(x):
        return to_blocks(x).reshape(2 * sequences, half, x.shape[-1])

    def crossed(x, j):
        return lax.ppermute(
            x,
            ("seq", "ctx"),
            [
                ((c * fold + r) * ctx_size + q, (q * fold + (r + j) % fold) * ctx_size + c)
                for c in range(ctx_size)
                for r in range(fold)
                for q in range(ctx_size)
            ],
        )

    def crossed_parts(parts):
        return ordered_parts(send_parts(parts))

    def send_parts(parts):
        return [
            crossed(pick(fold_place, [parts[(f + j) % fold] for f in range(fold)]), j)
            for j in range(fold)
        ]

    def ordered_parts(came):
        return [
            pick(fold_place, [came[(f - t) % fold] for f in range(fold)]) for t in range(fold)
        ]

    def swap_second(x):
        return jnp.concatenate([x[:half_rows], hop(x[half_rows:], ctx_size, far)], axis=0)

    owners = [place ^ k for k in range(ctx_size)]
    order = jnp.stack(
        [spot for owner in owners for spot in (2 * owner, 2 * (ctx_size - 1 - owner) + 1)]
    ).astype(jnp.int32)
    positions = order[:2, None, None] * half + jnp.arange(half, dtype=jnp.int32)[None, None, :]
    positions = jnp.broadcast_to(positions, (2, sequences, half)).reshape(-1)
    cosine, sine = rotation_tables(positions)

    def from_floors(x):
        came = [x] + [
            lax.ppermute(x, "seq", [(i, (i + 2 * step) % seq_size) for i in range(seq_size)])
            for step in range(1, floors)
        ]
        return jnp.concatenate(
            [
                pick(floor, [came[(mine - theirs) % floors] for mine in range(floors)])
                for theirs in range(floors)
            ],
            axis=0,
        )

    def from_ranks(x):
        return [x] + [hop(x, ctx_size, k) for k in range(1, ctx_size)]

    def by_rank(came):
        return [pick(place, [came[rank ^ p] for p in range(ctx_size)]) for rank in range(ctx_size)]

    def from_other_core(x):
        return lax.ppermute(x, "seq", [(i, i ^ 1) for i in range(seq_size)])

    def by_core(x, other):
        first, second = pick(core, [x, other]), pick(core, [other, x])
        shape = (floors, x.shape[0] // floors, x.shape[1])
        return jnp.stack([first.reshape(shape), second.reshape(shape)], axis=1).reshape(
            2 * x.shape[0], x.shape[1]
        )

    gate_up = lax.all_gather(jnp.stack([gate_weight, up_weight]), "seq", axis=0)
    gain_width = attention_gain.shape[0]
    own_width = project_weight.shape[1]
    vectors = jnp.concatenate([attention_gain, project_bias, feedforward_gain])
    spare = -vectors.shape[0] % own_width
    project_rows = from_floors(project_weight)
    held = project_rows.shape[0]
    tokens_mine = swap_second(to_rows(tokens))
    project_rows, tokens_mine = lax.optimization_barrier((project_rows, tokens_mine))
    project_came = from_ranks(
        jnp.concatenate(
            [project_rows, jnp.pad(vectors, (0, spare)).reshape(-1, own_width)], axis=0
        )
    )
    output_late = lax.optimization_barrier((output_weight, project_rows))[0]
    output_rows = from_floors(output_late)
    ordered = by_rank(project_came)
    vectors_all = [piece[held:].reshape(-1).astype(f32) for piece in ordered]

    def vector_whole(start, size):
        return jnp.concatenate([v[start : start + size] for v in vectors_all])[None, :]

    attention_full = vector_whole(0, gain_width)
    bias_full = vector_whole(gain_width, own_width)
    feedforward_full = vector_whole(gain_width + own_width, gain_width)
    project_columns = jnp.concatenate([piece[:held] for piece in ordered], axis=1)
    project_full = by_core(project_columns, from_other_core(project_columns))

    down_late, grad_late = lax.optimization_barrier((down_weight, cotangent, project_full))[:2]
    grad_rows = to_rows(grad_late)
    if ctx_size == 4:
        grad_near = [hop(grad_rows[:half_rows], 4, 1), hop(grad_rows[half_rows:], 4, 2)]
    else:
        grad_near = others(grad_rows, ctx_size)
    down_rows, down_columns = down_weight.shape
    depth = down_columns // fold
    down_turned = jnp.concatenate(
        crossed_parts(list(down_late.T.reshape(fold, depth, down_rows))), axis=1
    )
    normed, queries, pairs_mine = project_forward(
        tokens_mine, attention_full, project_full, bias_full, cosine, sine
    )
    down_turned, gate_up = lax.optimization_barrier((down_turned, gate_up, queries))[:2]
    down_mine = lax.all_gather(down_turned, "seq", axis=0)
    queries = attention_blocks(queries)
    pairs_mine = to_blocks(pairs_mine)
    pair_parts = [pairs_mine] + [hop(pairs_mine, ctx_size, k) for k in range(1, ctx_size)]
    grad_near, output_rows = lax.optimization_barrier((grad_near, output_rows, pair_parts))[:2]
    if ctx_size == 4:
        grad_far = [
            hop(jnp.concatenate([grad_rows[:half_rows], grad_near[0]], axis=0), 4, 2),
            hop(jnp.concatenate([grad_rows[half_rows:], grad_near[1]], axis=0), 4, 1),
        ]
    else:
        grad_far = []
    output_came = from_ranks(output_rows)
    queries = lax.optimization_barrier((queries, down_turned))[0]
    mixed, row_stats = attend_forward(order, queries, pair_parts)
    mixed, grad_far, output_came = lax.optimization_barrier((mixed, grad_far, output_came))
    if ctx_size == 4:
        firsts = [(grad_rows, 0), (grad_near[0], 0), (grad_far[0], 0), (grad_far[0], 1)]
        seconds = [(grad_rows, 1), (grad_far[1], 0), (grad_near[1], 0), (grad_far[1], 1)]
        own_second = grad_far[1][half_rows:]
    else:
        firsts = [(x, 0) for x in (grad_rows, *grad_near)]
        seconds = [(x, 1) for x in (grad_rows, *grad_near)]
        own_second = grad_near[far - 1][half_rows:]
    grad_low = jnp.concatenate([grad_rows[:half_rows], own_second], axis=0)
    output_columns = jnp.concatenate(by_rank(output_came), axis=1)
    output_full = by_core(output_columns, from_other_core(output_columns))
    mixed_rows = to_rows(mixed)
    hidden = tokens_mine.astype(f32) + dot(mixed_rows, output_full, NN)
    inverse_ffn = inverse_rms(hidden)
    normed_ffn = (hidden * inverse_ffn * feedforward_full).astype(bf16)

    normed_parts = [normed_ffn, *others(normed_ffn, ctx_size)]
    output_parts = []
    grad_normed_parts = []
    buffers = []
    for k, part in enumerate(normed_parts):
        output_part, grad_normed_part, *buffers = ffn(
            k,
            ctx_size,
            rows,
            [(part, 0), (part, 1), firsts[k], seconds[k ^ far]],
            gate_up,
            down_mine,
            buffers,
        )
        output_parts.append(output_part)
        grad_normed_parts.append(grad_normed_part)
    normed_got = [hop(grad_normed_parts[k], ctx_size, k) for k in range(1, ctx_size)]
    ffn_grads, normed_got = lax.optimization_barrier(
        (ffn_weights(seq_size, *buffers), normed_got)
    )
    grad_normed_ffn = others_sum(grad_normed_parts, normed_got)
    weight_grads = lax.psum_scatter(ffn_grads, "seq", scatter_dimension=0)

    grad_ffn_gain = jnp.sum(grad_normed_ffn * hidden * inverse_ffn, axis=0)
    weighted_ffn = grad_normed_ffn * feedforward_full
    grad_hidden = (
        grad_low.astype(f32)
        + inverse_ffn * weighted_ffn
        - hidden
        * inverse_ffn
        * inverse_ffn
        * inverse_ffn
        * jnp.mean(weighted_ffn * hidden, axis=-1, keepdims=True)
    )
    hidden_low = grad_hidden.astype(bf16)
    grad_mixed = dot(hidden_low, output_full, NT).astype(bf16)

    output_parts = lax.optimization_barrier((output_parts, grad_mixed))[0]
    output_got = [hop(output_parts[k], ctx_size, k) for k in range(1, ctx_size)]

    grad_queries, pair_grads = attend_backward(
        order,
        queries,
        pair_parts,
        mixed,
        attention_blocks(grad_mixed),
        row_stats,
        attention_blocks(cosine),
        attention_blocks(sine),
    )
    pair_grads, output_got = lax.optimization_barrier((pair_grads, output_got))
    pair_sums = [to_rows(pair_grads[:, :2])]
    for k in range(1, ctx_size):
        pair_sums.append(to_rows(hop(pair_grads[:, 2 * k : 2 * k + 2], ctx_size, k)))
    output_zigzag = hidden + others_sum(output_parts, output_got)
    grad_queries = to_rows(grad_queries)
    grad_pairs, tokens_grad, gain_sum, bias_sum = project_backward(
        grad_queries,
        project_full,
        tokens_mine,
        attention_full,
        grad_hidden,
        cosine,
        sine,
        pair_sums,
    )

    owned, weight_grads = lax.optimization_barrier(
        (
            owned_weights(ctx_size, normed, grad_queries, grad_pairs, mixed_rows, hidden_low),
            weight_grads,
        )
    )
    owned = lax.psum_scatter(
        owned,
        "seq",
        scatter_dimension=0,
        tiled=True,
    )

    layer_output = swap_second(output_zigzag.astype(bf16))
    tokens_gradient = jnp.concatenate(
        [
            tokens_grad[:half_rows],
            hop(tokens_grad[half_rows:].astype(bf16), ctx_size, far).astype(f32),
        ],
        axis=0,
    )
    sums = jnp.concatenate(
        [
            gain_sum.reshape(ctx_size, gain_width),
            bias_sum.reshape(ctx_size, own_width),
            grad_ffn_gain.reshape(ctx_size, gain_width),
        ],
        axis=1,
    )

    def sums_for(k):
        return lax.dynamic_index_in_dim(sums, place ^ k, 0)

    vector_sum = sums_for(0)
    for k in range(1, ctx_size):
        vector_sum = vector_sum + hop(sums_for(k), ctx_size, k)
    mask = 1
    while mask < seq_size:
        vector_sum = vector_sum + lax.ppermute(
            vector_sum, "seq", [(i, i ^ mask) for i in range(seq_size)]
        )
        mask *= 2
    vector_sum = vector_sum[0]
    down_late = weight_grads[2].reshape(depth, fold, down_rows)
    down_came = send_parts([down_late[:, t] for t in range(fold)])
    owned, layer_output, tokens_gradient, vector_sum = lax.optimization_barrier(
        (owned, layer_output, tokens_gradient, vector_sum)
    )
    own_columns = owned.shape[1] // ctx_size

    def owned_for(k):
        return lax.dynamic_slice_in_dim(owned, (place ^ k) * own_columns, own_columns, 1)

    owned_got, down_came = lax.optimization_barrier(
        ([hop(owned_for(k), ctx_size, k) for k in range(1, ctx_size)], down_came)
    )
    owned_total = others_sum([owned_for(0)], owned_got)
    down_out = jnp.concatenate(ordered_parts(down_came), axis=0).T

    return (
        to_blocks(layer_output).reshape(tokens.shape),
        to_blocks(tokens_gradient).reshape(tokens.shape),
        vector_sum[:gain_width],
        owned_total[:, :own_width],
        vector_sum[gain_width : gain_width + own_width],
        owned_total[:, own_width:],
        vector_sum[gain_width + own_width : vectors.shape[0]],
        weight_grads[0].astype(f32),
        weight_grads[1].astype(f32),
        down_out.astype(f32),
    )


def solution(mesh):
    matrix = P("seq", "ctx")
    vector = P("ctx")
    activation = P("seq", "ctx", None)

    def step(*arrays):
        return on_device(mesh.shape["seq"], mesh.shape["ctx"], *arrays)

    return jax.shard_map(
        step,
        mesh=mesh,
        in_specs=(
            activation,
            vector,
            matrix,
            vector,
            matrix,
            vector,
            matrix,
            matrix,
            matrix,
            activation,
        ),
        out_specs=(
            activation,
            activation,
            vector,
            matrix,
            vector,
            matrix,
            vector,
            matrix,
            matrix,
            matrix,
        ),
        check_vma=False,
    )
```
